32 devices in a mesh: dp: 8 (over z, x), seq: 4 (over y, core).
Axes of the slice: x: 2, y: 2, z: 4, core: 2. Of those that a mesh axis runs over, the one named last changes fastest.
Arguments:
- dec_in: bfloat16 [16, 1024, 768], P('dp', 'seq'), may hold values from -6 to 6
- memory: bfloat16 [16, 512, 768], P('dp', 'seq'), may hold values from -6 to 6
- cotangent: bfloat16 [16, 1024, 768], P('dp', 'seq'), may hold values from -6 to 6
- dec_lengths: int32 [16], P('dp'), may hold values from 1 to 1024, as said below
- mem_mask: int32 [16, 512], P('dp', 'seq'), may hold values from 0 to 1, as said below
- bucket_map: int32 [1024], replicated, may hold values from 0 to 31, as said below
- self_weights: bfloat16 [4, 768, 768], P(None, ('dp', 'seq'))
- cross_weights: bfloat16 [4, 768, 768], P(None, ('dp', 'seq'))
- ffn_in: bfloat16 [2, 768, 2048], P(None, ('dp', 'seq')), may hold values from -0.21875 to 0.21875
- ffn_out: bfloat16 [2048, 768], P(('dp', 'seq')), may hold values from -0.1875 to 0.1875
- norm_gains: float32 [3, 768], replicated, may hold values from 0.5 to 1.5
- bias_table: float32 [32, 12], replicated, may hold values from -3 to 3
Outputs:
- layer_out: bfloat16 [16, 1024, 768], P('dp', 'seq')
- dec_grad: float32 [16, 1024, 768], P('dp', 'seq')
- mem_grad: float32 [16, 512, 768], P('dp', 'seq')
- self_grad: float32 [4, 768, 768], P(None, ('dp', 'seq'))
- cross_grad: float32 [4, 768, 768], P(None, ('dp', 'seq'))
- ffn_in_grad: float32 [2, 768, 2048], P(None, ('dp', 'seq'))
- ffn_out_grad: float32 [2048, 768], P(('dp', 'seq'))
- gains_grad: float32 [3, 768], replicated
- table_grad: float32 [32, 12], replicated
- self_rows: float32 [3, 768], P(None, ('dp', 'seq'))
- self_cols: float32 [3, 768], replicated
- cross_rows: float32 [3, 768], P(None, ('dp', 'seq'))
- cross_cols: float32 [3, 768], replicated
- ffn_in_rows: float32 [2, 768], P(None, ('dp', 'seq'))
- ffn_in_cols: float32 [2, 2048], replicated
- ffn_out_rows: float32 [2048], P(('dp', 'seq'))
- ffn_out_cols: float32 [768], replicated
- out_proj_stats: float32 [2, 2, 768], P(None, None, ('dp', 'seq'))
The draws below stay inside these ranges and needn't reach their ends.
Inputs may be any that keep to these rules, and one draw needn't show every extreme that they name: `dec_lengths`: the non-padding tokens of a slot are a prefix of its 1024 positions; some slot is full. `mem_mask`: the ones of a slot form a prefix of its 512 rows, at least one; some slot has all 512. `bucket_map`: never falls with the distance; 0 at distance 0; every bucket is used.
All inputs are finite; a program needn't handle non-finite values.
Results may differ from the reference program's by a relative error of at most 0.029.
The reference program's roundings to bfloat16 on the way count: a program that leaves them out, or rounds other values in their place, can miss the bound.
Values may be sent and summed in bfloat16 or wider, within the bound.
No kernel may reach another device: no remote copies, remote signals or barrier semaphores. Data moves between devices by JAX's collectives and lax.ppermute only.
A program may use at most 256 MiB of HBM per device.

```python
import jax
import jax.numpy as jnp
from jax import lax

D = 768
FF = 2048
H = 12
DK = 64
NB = 32
LEN = 1024
MEM = 512
SLOTS = 16


def ragged_lengths(key, limit):
    keys_split = jax.random.split(key, 3)
    first_draw = jax.random.randint(keys_split[0], (SLOTS,), 0, limit, dtype=jnp.int32)
    second_draw = jax.random.randint(keys_split[1], (SLOTS,), 0, limit, dtype=jnp.int32)
    full_slot = jax.random.randint(keys_split[2], (), 0, SLOTS, dtype=jnp.int32)
    lengths_out = limit - first_draw * second_draw // limit
    slot_index = jnp.arange(SLOTS, dtype=jnp.int32)
    return jnp.where(slot_index == full_slot, limit, lengths_out).astype(jnp.int32)


def draw_dec_lengths(key, part):
    return ragged_lengths(key, LEN)


def draw_mem_mask(key, part):
    lengths_out = ragged_lengths(jax.random.fold_in(key, 7), MEM)
    row_index = jnp.arange(MEM, dtype=jnp.int32)
    return (row_index[None, :] < lengths_out[:, None]).astype(jnp.int32)


def draw_bucket_map(key, part):
    shuffled = jax.random.permutation(key, LEN - 1).astype(jnp.int32) + 1
    chosen = shuffled[:NB - 1]
    distances = jnp.arange(LEN, dtype=jnp.int32)
    return jnp.sum((chosen[None, :] <= distances[:, None]).astype(jnp.int32), axis=1).astype(jnp.int32)


def stacked_weights(key):
    noise = jnp.clip(jax.random.normal(key, (4, D, D), jnp.float32), -6.0, 6.0)
    scales = jnp.array([(4.0 * D) ** (-0.5), (4.0 * D) ** (-0.5), D ** (-0.5), 4.0 * D ** (-0.5)], jnp.float32)
    return (noise * scales[:, None, None]).astype(jnp.bfloat16)


def draw_self_weights(key, part):
    return stacked_weights(jax.random.fold_in(key, 11))


def draw_cross_weights(key, part):
    return stacked_weights(jax.random.fold_in(key, 13))


def block_scale(key, shape, shards, smallest, largest):
    factor_of = 1.0
    for dim, parts in shards:
        heights = jax.random.uniform(jax.random.fold_in(jax.random.fold_in(key, 6), dim), (parts,), jnp.float32, smallest / len(shards), largest / len(shards))
        factor_of = factor_of * jnp.repeat(jnp.exp(heights), shape[dim] // parts).reshape((-1,) + (1,) * (len(shape) - 1 - dim))
    return factor_of


def normal_values(stream_key, shape, scale, most, cuts=(), held_as=jnp.bfloat16):
    result = scale * jax.random.normal(stream_key, shape, jnp.float32)
    if cuts:
        result = result * block_scale(stream_key, shape, cuts, -0.22, 0.18)
    return jnp.clip(result, -most, most).astype(held_as)


def setup_inputs(seed: int = 0) -> dict:
    arg_keys = jax.random.split(jax.random.key(seed), 13)
    dec_in = normal_values(arg_keys[0], (SLOTS, LEN, D), 1.0, 6.0, ((0, 8), (1, 4)))
    memory = normal_values(arg_keys[1], (SLOTS, MEM, D), 1.0, 6.0, ((0, 8), (1, 4)))
    cotangent = normal_values(arg_keys[2], (SLOTS, LEN, D), 1.0, 6.0, ((0, 8), (1, 4)))
    dec_lengths = draw_dec_lengths(jax.random.fold_in(arg_keys[12], 71), 0)
    mem_mask = draw_mem_mask(jax.random.fold_in(arg_keys[12], 71), 0)
    bucket_map = draw_bucket_map(jax.random.fold_in(arg_keys[12], 71), 0)
    self_weights = draw_self_weights(jax.random.fold_in(arg_keys[12], 71), 0)
    cross_weights = draw_cross_weights(jax.random.fold_in(arg_keys[12], 71), 0)
    ffn_in = normal_values(arg_keys[8], (2, D, FF), D ** -0.5, 0.21875, ((1, 32),))
    ffn_out = normal_values(arg_keys[9], (FF, D), (FF // 2) ** -0.5, 0.1875, ((0, 32),))
    norm_gains = jnp.clip(1.0 + 0.1 * jax.random.normal(arg_keys[10], (3, D), jnp.float32), 0.5, 1.5)
    bias_table = normal_values(arg_keys[11], (NB, H), 0.5, 3.0, (), jnp.float32)
    return {"dec_in": dec_in, "memory": memory, "cotangent": cotangent, "dec_lengths": dec_lengths, "mem_mask": mem_mask, "bucket_map": bucket_map, "self_weights": self_weights, "cross_weights": cross_weights, "ffn_in": ffn_in, "ffn_out": ffn_out, "norm_gains": norm_gains, "bias_table": bias_table}


@jax.custom_vjp
def low(v):
    return lax.optimization_barrier(v.astype(jnp.bfloat16)).astype(jnp.float32)

@jax.custom_vjp
def low_back(v):
    return v

def low_keep(v):
    return (low(v), None)

def low_pass(kept, grad):
    return (grad,)

def back_keep(v):
    return (v, None)

def back_low(kept, grad):
    return (low(grad),)
low.defvjp(low_keep, low_pass)
low_back.defvjp(back_keep, back_low)
epsilon = 1e-06
masked_out = -1000000000.0
highest = lax.Precision.HIGHEST

def rms_norm(inputs, scales):
    return inputs * lax.rsqrt(lax.optimization_barrier(jnp.mean(inputs * inputs, axis=-1, keepdims=True)) + epsilon) * scales

def round_both(inputs):
    return low_back(low(inputs))

def matmul(inputs, matrix):
    return jnp.dot(inputs, matrix, precision=highest, preferred_element_type=jnp.float32)

def attend(queries, key_rows, values, extra, allowed):
    query_count = queries.shape[0]
    key_count = key_rows.shape[0]
    scores = jnp.einsum('qhd,khd->hqk', queries.reshape(query_count, H, DK), key_rows.reshape(key_count, H, DK), precision=highest) + extra
    scores = jnp.where(allowed, low_back(scores), masked_out)
    shares = low(jax.nn.softmax(scores, axis=-1))
    mixed_out = jnp.einsum('hqk,khd->qhd', shares, values.reshape(key_count, H, DK), precision=highest)
    return round_both(mixed_out.reshape(query_count, H * DK))

def layer_slot(weights, slot_tokens, slot_memory, slot_length, slot_mask, bucket_map):
    self_matrix, cross_matrix, gate_matrix, down_matrix, gain_rows, table_in = weights
    positions = jnp.arange(LEN, dtype=jnp.int32)
    distance = jnp.maximum(positions[:, None] - positions[None, :], 0)
    pos_bias = jnp.transpose(table_in[bucket_map[distance]], (2, 0, 1))
    allowed = (positions[None, :] <= positions[:, None]) & (positions[None, :] < slot_length)
    normed = low(rms_norm(slot_tokens, gain_rows[0]))
    queries = round_both(matmul(normed, self_matrix[0]))
    key_rows = round_both(matmul(normed, self_matrix[1]))
    values = round_both(matmul(normed, self_matrix[2]))
    mixed_out = attend(queries, key_rows, values, pos_bias, allowed[None])
    first_sum = slot_tokens + low_back(matmul(mixed_out, self_matrix[3]))
    normed = low(rms_norm(first_sum, gain_rows[1]))
    queries = round_both(matmul(normed, cross_matrix[0]))
    key_rows = round_both(matmul(slot_memory, cross_matrix[1]))
    values = round_both(matmul(slot_memory, cross_matrix[2]))
    visible = (slot_mask > 0)[None, None, :]
    mixed_out = attend(queries, key_rows, values, 0.0, visible)
    second_sum = first_sum + low_back(matmul(mixed_out, cross_matrix[3]))
    normed = low(rms_norm(second_sum, gain_rows[2]))
    gate_pre = low_back(matmul(normed, gate_matrix[0]))
    up_pre = low_back(matmul(normed, gate_matrix[1]))
    hidden = low(jax.nn.gelu(gate_pre, approximate=True) * up_pre)
    return second_sum + low_back(matmul(hidden, down_matrix))

def reference(dec_in, memory, cotangent, dec_lengths, mem_mask, bucket_map, self_weights, cross_weights, ffn_in, ffn_out, norm_gains, bias_table):

    def forward(residual_in, memory_in, self_matrix, cross_matrix, gate_matrix, down_matrix, gain_rows, table_in):
        weights = (self_matrix, cross_matrix, gate_matrix, down_matrix, gain_rows, table_in)

        def slot_step(slot_items):
            return layer_slot(weights, slot_items[0], slot_items[1], slot_items[2], slot_items[3], bucket_map)
        return lax.map(jax.checkpoint(slot_step), (residual_in, memory_in, dec_lengths, mem_mask))
    layer_out, pullback = jax.vjp(forward, dec_in.astype(jnp.float32), memory.astype(jnp.float32), self_weights.astype(jnp.float32), cross_weights.astype(jnp.float32), ffn_in.astype(jnp.float32), ffn_out.astype(jnp.float32), norm_gains.astype(jnp.float32), bias_table.astype(jnp.float32))
    dec_grad, mem_grad, self_grad, cross_grad, ffn_in_grad, ffn_out_grad, gains_grad, table_grad = pullback(cotangent.astype(jnp.float32))
    self_square = self_grad * self_grad
    cross_square = cross_grad * cross_grad
    gate_square = ffn_in_grad * ffn_in_grad
    down_square = ffn_out_grad * ffn_out_grad
    self_rows_all = lax.optimization_barrier(jnp.mean(self_square, axis=2))
    self_cols_all = lax.optimization_barrier(jnp.mean(self_square, axis=1))
    cross_rows_all = lax.optimization_barrier(jnp.mean(cross_square, axis=2))
    cross_cols_all = lax.optimization_barrier(jnp.mean(cross_square, axis=1))
    out_proj_stats = jnp.stack([jnp.stack([self_rows_all[3], self_cols_all[3]]), jnp.stack([cross_rows_all[3], cross_cols_all[3]])])
    return (layer_out.astype(jnp.bfloat16), dec_grad, mem_grad, self_grad, cross_grad, ffn_in_grad, ffn_out_grad, gains_grad, table_grad, self_rows_all[:3], self_cols_all[:3], cross_rows_all[:3], cross_cols_all[:3], lax.optimization_barrier(jnp.mean(gate_square, axis=2)), lax.optimization_barrier(jnp.mean(gate_square, axis=1)), lax.optimization_barrier(jnp.mean(down_square, axis=1)), lax.optimization_barrier(jnp.mean(down_square, axis=0)), out_proj_stats)
```

```python
import functools

import jax
import jax.numpy as jnp
from jax import lax
from jax.experimental import pallas as pl
from jax.experimental.pallas import tpu as pltpu
from jax.sharding import PartitionSpec as P

H = 12
DK = 64
PAIR = 2 * DK
WIDE = 4 * DK
EPS = 1e-06
MASKED = -1000000000.0
BF = jnp.bfloat16
F32 = jnp.float32
BUDGET = 60 * 1024 * 1024


def dot_nn(a, b):
    return lax.dot_general(a, b, (((1,), (0,)), ((), ())), preferred_element_type=F32)


def dot_nt(a, b):
    return lax.dot_general(a, b, (((1,), (1,)), ((), ())), preferred_element_type=F32)


def dot_tn(a, b):
    return lax.dot_general(a, b, (((0,), (0,)), ((), ())), preferred_element_type=F32)


def inverse_rms(v):
    return lax.rsqrt(jnp.mean(v * v, axis=-1, keepdims=True) + EPS)


def normed(v, gain):
    return (v * inverse_rms(v) * gain).astype(BF)


def normed_back(v, gain, c):
    r = inverse_rms(v)
    scaled = c * gain
    inner = jnp.mean(v * scaled, axis=-1, keepdims=True)
    dv = r * scaled - v * (r * r * r * inner)
    dgain = jnp.sum(c * v * r, axis=0, keepdims=True)
    return dv, dgain


def shear(rows, sign):
    keys = rows.shape[1]
    r = lax.broadcasted_iota(jnp.int32, (8, 1), 0)
    for bit in (1, 2, 4):
        turned = pltpu.roll(rows, bit if sign > 0 else keys - bit, 1)
        rows = jnp.where((r & bit) != 0, turned, rows)
    return rows


def build_bias(line, off, out_ref):
    count, keys = out_ref.shape
    base = shear(pltpu.roll(jnp.broadcast_to(line, (8, keys)), off + 1, 1), 1)
    for g in range(count // 8):
        out_ref[8 * g : 8 * g + 8, :] = pltpu.roll(base, (8 * g) % keys, 1) if g else base


def sum_diagonals(sum_ref, off):
    count, keys = sum_ref.shape
    total = sum_ref[0:8, :]
    for g in range(1, count // 8):
        total = total + pltpu.roll(sum_ref[8 * g : 8 * g + 8, :], (keys - 8 * g) % keys, 1)
    total = jnp.sum(shear(total, -1), axis=0, keepdims=True)
    return pltpu.roll(jnp.broadcast_to(total, (8, keys)), keys - 1 - off, 1)[0:1]


def low_lanes():
    return lax.broadcasted_iota(jnp.int32, (1, PAIR), 1) < DK


def head_part(x, head):
    low = low_lanes()
    mine = low if head % 2 == 0 else jnp.logical_not(low)
    return jnp.where(mine, x, jnp.zeros_like(x))


def row_limit(start, rows, count, causal):
    if not causal:
        return count
    seen = start + 1 + lax.broadcasted_iota(jnp.int32, (rows, 1), 0)
    return jnp.minimum(seen, count)


def attend(q_ref, k_ref, v_ref, o_ref, lse_ref, bias_ref, s_ref, p_ref, off, counts):
    slots, rows, _ = q_ref.shape
    keys = k_ref.shape[1]
    causal = bias_ref is not None
    cols = lax.broadcasted_iota(jnp.int32, (1, keys), 1)
    low = low_lanes()
    work = [(s, h) for s in range(slots) for h in range(WIDE // DK)]

    def lanes(h):
        return slice((h // 2) * PAIR, (h // 2) * PAIR + PAIR)

    def scores(n):
        s, h = work[n]
        s_ref[n % 2] = dot_nt(head_part(q_ref[s, :, lanes(h)], h), k_ref[s, :, lanes(h)])

    scores(0)
    kept = None
    for n, (s, h) in enumerate(work):
        if n + 1 < len(work):
            scores(n + 1)
        sc = s_ref[n % 2]
        if causal:
            sc = sc + bias_ref[h]
        sc = jnp.where(cols < row_limit(off, rows, counts[s], causal), sc, MASKED)
        top = jnp.max(sc, axis=1, keepdims=True)
        e = jnp.exp(sc - top)
        total = jnp.sum(e, axis=1, keepdims=True)
        p_ref[n % 2] = (e * (1.0 / total)).astype(BF)
        out = dot_nn(p_ref[n % 2], v_ref[s, :, lanes(h)])
        log_total = jnp.broadcast_to(top + jnp.log(total), (rows, PAIR))
        if h % 2 == 0:
            kept = (out, log_total)
        else:
            o_ref[s, :, lanes(h)] = jnp.where(low, kept[0], out).astype(BF)
            lse_ref[s, h // 2] = jnp.where(low, kept[1], log_total)


def attend_back(
    q_ref, k_ref, v_ref, g_ref, lse_ref, dq_ref, dk_ref, dv_ref,
    bias_ref, sum_ref, s_ref, dp_ref, p_ref, ds_ref, off, counts,
):
    slots, rows, _ = q_ref.shape
    keys = k_ref.shape[1]
    causal = bias_ref is not None
    cols = lax.broadcasted_iota(jnp.int32, (1, keys), 1)
    low = low_lanes()
    work = [(s, h) for s in range(slots) for h in range(WIDE // DK)]

    def lanes(h):
        return slice((h // 2) * PAIR, (h // 2) * PAIR + PAIR)

    def products(n):
        s, h = work[n]
        s_ref[n % 2] = dot_nt(head_part(q_ref[s, :, lanes(h)], h), k_ref[s, :, lanes(h)])
        dp_ref[n % 2] = dot_nt(head_part(g_ref[s, :, lanes(h)], h), v_ref[s, :, lanes(h)])

    products(0)
    kept = None
    for n, (s, h) in enumerate(work):
        if n + 1 < len(work):
            products(n + 1)
        sc = s_ref[n % 2]
        if causal:
            sc = sc + bias_ref[h]
        sc = jnp.where(cols < row_limit(off, rows, counts[s], causal), sc, MASKED)
        at = (h % 2) * DK
        p = jnp.exp(sc - lse_ref[s, h // 2, :, at : at + 1])
        dp = dp_ref[n % 2]
        inner = jnp.sum(p * dp, axis=1, keepdims=True)
        ds = (p * (dp - inner)).astype(BF)
        p_ref[n % 2] = p.astype(BF)
        ds_ref[n % 2] = ds
        if causal:
            if s == 0:
                sum_ref[h] = ds.astype(F32)
            else:
                sum_ref[h] += ds.astype(F32)
        ds = ds_ref[n % 2]
        dq = dot_nn(ds, k_ref[s, :, lanes(h)])
        dk = dot_tn(head_part(q_ref[s, :, lanes(h)], h), ds)
        dv = dot_tn(head_part(g_ref[s, :, lanes(h)], h), p_ref[n % 2])
        if h % 2 == 0:
            kept = (dq, dk, dv)
        else:
            dq_ref[s * rows : (s + 1) * rows, lanes(h)] = jnp.where(low, kept[0], dq).astype(BF)
            dk_ref[s * keys : (s + 1) * keys, lanes(h)] = (kept[1] + dk).astype(BF).T
            dv_ref[s * keys : (s + 1) * keys, lanes(h)] = (kept[2] + dv).astype(BF).T


def whole(shape):
    return pl.BlockSpec(shape, lambda b, *_: (0,) * len(shape), pipeline_mode=pl.Buffered(1))


def result(shape):
    return pl.BlockSpec(shape, lambda b, *_: (0,) * len(shape))


def wide(shape):
    return pl.BlockSpec(shape[:-1] + (WIDE,), lambda b, *_: (0,) * (len(shape) - 1) + (b,))


def wide_of(index, shape):
    return pl.BlockSpec((None,) + shape[:-1] + (WIDE,), lambda b, *_: (index,) + (0,) * (len(shape) - 1) + (b,))


def whole_of(index, shape):
    return pl.BlockSpec(
        (None,) + shape, lambda b, *_: (index,) + (0,) * len(shape), pipeline_mode=pl.Buffered(1)
    )


def params():
    return pltpu.CompilerParams(dimension_semantics=("arbitrary",), vmem_limit_bytes=BUDGET)


def self_forward_body(
    lims, x_ref, gain_ref, wq_ref, wk_ref, wv_ref, line_ref,
    q_ref, k_ref, v_ref, o_ref, lse_ref, a_ref, bias_ref, s_ref, p_ref,
):
    slots, keys, width = x_ref.shape
    rows = q_ref.shape[1]
    off = lims[0]

    @pl.when(pl.program_id(0) == 0)
    def _():
        for s in range(slots):
            a_ref[s * keys : (s + 1) * keys, :] = normed(x_ref[s].astype(F32), gain_ref[0:1, :])

    for s in range(slots):
        mine = pl.ds(pl.multiple_of(s * keys + off, 128), rows)
        q_ref[s] = dot_nn(a_ref[mine, :], wq_ref[...]).astype(BF)
        k_ref[s] = dot_nn(a_ref[s * keys : (s + 1) * keys, :], wk_ref[...]).astype(BF)
        v_ref[s] = dot_nn(a_ref[s * keys : (s + 1) * keys, :], wv_ref[...]).astype(BF)
    for h in range(WIDE // DK):
        build_bias(line_ref[0, h : h + 1, :], off, bias_ref.at[h])
    counts = [lims[1 + s] for s in range(slots)]
    attend(q_ref, k_ref, v_ref, o_ref, lse_ref, bias_ref, s_ref, p_ref, off, counts)


def self_forward(lims, x_full, gains, w01, w23, line, rows):
    slots, keys, width = x_full.shape
    blocks = width // WIDE
    return pl.pallas_call(
        self_forward_body,
        grid_spec=pltpu.PrefetchScalarGridSpec(
            num_scalar_prefetch=1,
            grid=(blocks,),
            in_specs=[
                whole((slots, keys, width)),
                whole(gains.shape),
                wide_of(0, (width, width)),
                wide_of(1, (width, width)),
                wide_of(0, (width, width)),
                pl.BlockSpec((1, WIDE // DK, keys), lambda b, *_: (b, 0, 0)),
            ],
            out_specs=[
                wide((slots, rows, width)),
                wide((slots, keys, width)),
                wide((slots, keys, width)),
                wide((slots, rows, width)),
                pl.BlockSpec((slots, 2, rows, PAIR), lambda b, *_: (0, b, 0, 0)),
            ],
            scratch_shapes=[
                pltpu.VMEM((slots * keys, width), BF),
                pltpu.VMEM((WIDE // DK, rows, keys), F32),
                pltpu.VMEM((2, rows, keys), F32),
                pltpu.VMEM((2, rows, keys), BF),
            ],
        ),
        out_shape=[
            jax.ShapeDtypeStruct((slots, rows, width), BF),
            jax.ShapeDtypeStruct((slots, keys, width), BF),
            jax.ShapeDtypeStruct((slots, keys, width), BF),
            jax.ShapeDtypeStruct((slots, rows, width), BF),
            jax.ShapeDtypeStruct((slots, H // 2, rows, PAIR), F32),
        ],
        compiler_params=params(),
        cost_estimate=pl.CostEstimate(
            flops=2 * slots * keys * width * width * 3, bytes_accessed=16 << 20, transcendentals=slots * rows * keys * H
        ),
        name="self_forward",
    )(lims, x_full, gains, w01, w01, w23, line)


def cross_forward_body(
    lims, x_ref, o1_ref, wo_ref, gain_ref, mem_ref, wq_ref, wk_ref, wv_ref,
    h_ref, q_ref, k_ref, v_ref, o_ref, lse_ref, a_ref, s_ref, p_ref,
):
    slots, keys, width = mem_ref.shape
    rows = q_ref.shape[1]

    @pl.when(pl.program_id(0) == 0)
    def _():
        for s in range(slots):
            h = x_ref[s].astype(F32) + dot_nn(o1_ref[s], wo_ref[...])
            h_ref[s] = h
            a_ref[s * rows : (s + 1) * rows, :] = normed(h, gain_ref[1:2, :])

    for s in range(slots):
        q_ref[s] = dot_nn(a_ref[s * rows : (s + 1) * rows, :], wq_ref[...]).astype(BF)
        k_ref[s] = dot_nn(mem_ref[s], wk_ref[...]).astype(BF)
        v_ref[s] = dot_nn(mem_ref[s], wv_ref[...]).astype(BF)
    counts = [lims[1 + s] for s in range(slots)]
    attend(q_ref, k_ref, v_ref, o_ref, lse_ref, None, s_ref, p_ref, 0, counts)


def cross_forward(lims, x, o1, w23, gains, mem_full, c01, c23):
    slots, keys, width = mem_full.shape
    rows = x.shape[1]
    blocks = width // WIDE
    return pl.pallas_call(
        cross_forward_body,
        grid_spec=pltpu.PrefetchScalarGridSpec(
            num_scalar_prefetch=1,
            grid=(blocks,),
            in_specs=[
                whole((slots, rows, width)),
                whole((slots, rows, width)),
                whole_of(1, (width, width)),
                whole(gains.shape),
                whole((slots, keys, width)),
                wide_of(0, (width, width)),
                wide_of(1, (width, width)),
                wide_of(0, (width, width)),
            ],
            out_specs=[
                result((slots, rows, width)),
                wide((slots, rows, width)),
                wide((slots, keys, width)),
                wide((slots, keys, width)),
                wide((slots, rows, width)),
                pl.BlockSpec((slots, 2, rows, PAIR), lambda b, *_: (0, b, 0, 0)),
            ],
            scratch_shapes=[
                pltpu.VMEM((slots * rows, width), BF),
                pltpu.VMEM((2, rows, keys), F32),
                pltpu.VMEM((2, rows, keys), BF),
            ],
        ),
        out_shape=[
            jax.ShapeDtypeStruct((slots, rows, width), F32),
            jax.ShapeDtypeStruct((slots, rows, width), BF),
            jax.ShapeDtypeStruct((slots, keys, width), BF),
            jax.ShapeDtypeStruct((slots, keys, width), BF),
            jax.ShapeDtypeStruct((slots, rows, width), BF),
            jax.ShapeDtypeStruct((slots, H // 2, rows, PAIR), F32),
        ],
        compiler_params=params(),
        cost_estimate=pl.CostEstimate(
            flops=2 * slots * (keys * 2 + rows * 2) * width * width,
            bytes_accessed=14 << 20,
            transcendentals=slots * rows * keys * H,
        ),
        name="cross_forward",
    )(lims, x, o1, w23, gains, mem_full, c01, c01, c23)


def feed_forward_body(
    h1_ref, o2_ref, wo_ref, gain_ref, g_ref, w0_ref, w1_ref, wd_ref,
    out_ref, gh_ref, dgain_ref, dw0_ref, dw1_ref, dwd_ref, h_ref, a_ref, at_ref, acc_ref, da_ref,
):
    step = pl.program_id(0)

    @pl.when(step == 0)
    def _():
        h = h1_ref[...] + dot_nn(o2_ref[...], wo_ref[...])
        h_ref[...] = h
        a = normed(h, gain_ref[2:3, :])
        a_ref[...] = a
        at_ref[...] = a.T
        acc_ref[...] = h
        da_ref[...] = jnp.zeros_like(da_ref)

    a = a_ref[...]
    e = g_ref[...]
    gate = dot_nn(a, w0_ref[...])
    up = dot_nn(a, w1_ref[...])
    c = dot_nt(e, wd_ref[...])
    root = 0.7978845608028654
    square = gate * gate
    th = jnp.tanh(root * gate * (1.0 + 0.044715 * square))
    half = 0.5 * (1.0 + th)
    act = gate * half
    slope = half + 0.5 * gate * (1.0 - th * th) * (root * (1.0 + 3.0 * 0.044715 * square))
    hidden = (act * up).astype(BF)
    dgate = (c * up * slope).astype(BF)
    dup = (c * act).astype(BF)
    acc_ref[...] += dot_nn(hidden, wd_ref[...])
    dwd_ref[...] = dot_tn(hidden, e).astype(BF)
    dw0_ref[...] = dot_nn(at_ref[...], dgate).astype(BF)
    dw1_ref[...] = dot_nn(at_ref[...], dup).astype(BF)
    da_ref[...] += dot_nt(dgate, w0_ref[...]) + dot_nt(dup, w1_ref[...])

    @pl.when(step == pl.num_programs(0) - 1)
    def _():
        out_ref[...] = acc_ref[...].astype(BF)
        dv, dgain = normed_back(h_ref[...], gain_ref[2:3, :], da_ref[...])
        gh_ref[...] = e.astype(F32) + dv
        dgain_ref[...] = dgain


def feed_forward(h1, o2, c23, gains, cot, gate_full, down_full):
    tokens, width = h1.shape
    hidden = down_full.shape[0]
    tile = 512
    return pl.pallas_call(
        feed_forward_body,
        grid_spec=pltpu.PrefetchScalarGridSpec(
            num_scalar_prefetch=0,
            grid=(hidden // tile,),
            in_specs=[
                whole((tokens, width)),
                whole((tokens, width)),
                whole_of(1, (width, width)),
                whole(gains.shape),
                whole((tokens, width)),
                pl.BlockSpec((None, width, tile), lambda b: (0, 0, b)),
                pl.BlockSpec((None, width, tile), lambda b: (1, 0, b)),
                pl.BlockSpec((tile, width), lambda b: (b, 0)),
            ],
            out_specs=[
                result((tokens, width)),
                result((tokens, width)),
                result((1, width)),
                pl.BlockSpec((width, tile), lambda b: (0, b)),
                pl.BlockSpec((width, tile), lambda b: (0, b)),
                pl.BlockSpec((tile, width), lambda b: (b, 0)),
            ],
            scratch_shapes=[
                pltpu.VMEM((tokens, width), F32),
                pltpu.VMEM((tokens, width), BF),
                pltpu.VMEM((width, tokens), BF),
                pltpu.VMEM((tokens, width), F32),
                pltpu.VMEM((tokens, width), F32),
            ],
        ),
        out_shape=[
            jax.ShapeDtypeStruct((tokens, width), BF),
            jax.ShapeDtypeStruct((tokens, width), F32),
            jax.ShapeDtypeStruct((1, width), F32),
            jax.ShapeDtypeStruct((width, hidden), BF),
            jax.ShapeDtypeStruct((width, hidden), BF),
            jax.ShapeDtypeStruct((hidden, width), BF),
        ],
        compiler_params=params(),
        cost_estimate=pl.CostEstimate(
            flops=18 * tokens * hidden * width, bytes_accessed=24 << 20, transcendentals=tokens * hidden
        ),
        name="feed_forward",
    )(h1, o2, c23, gains, cot, gate_full, gate_full, down_full)


def cross_backward_body(
    lims, gh2_ref, h1_ref, o2_ref, wo_ref, gain_ref, mem_ref, q_ref, k_ref, v_ref, lse_ref, wq_ref, wk_ref, wv_ref,
    gh_ref, dgain_ref, dmem_ref, dwq_ref, dwk_ref, dwv_ref, dwo_ref,
    g_ref, at_ref, memt_ref, da_ref, dm_ref, dq_ref, dk_ref, dv_ref, s_ref, dp_ref, p_ref, ds_ref,
):
    step = pl.program_id(0)
    slots, keys, width = mem_ref.shape
    rows = q_ref.shape[1]

    @pl.when(step == 0)
    def _():
        e = gh2_ref[...].astype(BF)
        back = dot_nt(e, wo_ref[...]).astype(BF)
        for b in range(width // WIDE):
            for s in range(slots):
                g_ref[b, s] = back[s * rows : (s + 1) * rows, b * WIDE : (b + 1) * WIDE]
        dwo_ref[...] = dot_tn(o2_ref[...], e).astype(BF)
        at_ref[...] = normed(h1_ref[...], gain_ref[1:2, :]).T
        for s in range(slots):
            memt_ref[:, s * keys : (s + 1) * keys] = mem_ref[s].T
        da_ref[...] = jnp.zeros_like(da_ref)
        dm_ref[...] = jnp.zeros_like(dm_ref)

    counts = [lims[1 + s] for s in range(slots)]
    attend_back(
        q_ref, k_ref, v_ref, g_ref.at[step], lse_ref, dq_ref, dk_ref, dv_ref,
        None, None, s_ref, dp_ref, p_ref, ds_ref, 0, counts,
    )
    dwq_ref[...] = dot_nn(at_ref[...], dq_ref[...]).astype(BF)
    dwk_ref[...] = dot_nn(memt_ref[...], dk_ref[...]).astype(BF)
    dwv_ref[...] = dot_nn(memt_ref[...], dv_ref[...]).astype(BF)
    da_ref[...] += dot_nt(dq_ref[...], wq_ref[...])
    dm_ref[...] += dot_nt(dk_ref[...], wk_ref[...]) + dot_nt(dv_ref[...], wv_ref[...])

    @pl.when(step == pl.num_programs(0) - 1)
    def _():
        dv, dgain = normed_back(h1_ref[...], gain_ref[1:2, :], da_ref[...])
        gh_ref[...] = gh2_ref[...] + dv
        dgain_ref[...] = dgain
        dmem_ref[...] = dm_ref[...].astype(BF)


def cross_backward(lims, gh2, h1, o2, c01, c23, gains, mem_full, q, k, v, lse):
    slots, keys, width = mem_full.shape
    rows = q.shape[1]
    tokens = slots * rows
    blocks = width // WIDE
    square = jax.ShapeDtypeStruct((width, width), BF)
    return pl.pallas_call(
        cross_backward_body,
        grid_spec=pltpu.PrefetchScalarGridSpec(
            num_scalar_prefetch=1,
            grid=(blocks,),
            in_specs=[
                whole((tokens, width)),
                whole((tokens, width)),
                whole((tokens, width)),
                whole_of(1, (width, width)),
                whole(gains.shape),
                whole((slots, keys, width)),
                wide((slots, rows, width)),
                wide((slots, keys, width)),
                wide((slots, keys, width)),
                pl.BlockSpec((slots, 2, rows, PAIR), lambda b, *_: (0, b, 0, 0)),
                wide_of(0, (width, width)),
                wide_of(1, (width, width)),
                wide_of(0, (width, width)),
            ],
            out_specs=[
                result((tokens, width)),
                result((1, width)),
                result((slots * keys, width)),
                wide((width, width)),
                wide((width, width)),
                wide((width, width)),
                result((width, width)),
            ],
            scratch_shapes=[
                pltpu.VMEM((blocks, slots, rows, WIDE), BF),
                pltpu.VMEM((width, tokens), BF),
                pltpu.VMEM((width, slots * keys), BF),
                pltpu.VMEM((tokens, width), F32),
                pltpu.VMEM((slots * keys, width), F32),
                pltpu.VMEM((tokens, WIDE), BF),
                pltpu.VMEM((slots * keys, WIDE), BF),
                pltpu.VMEM((slots * keys, WIDE), BF),
                pltpu.VMEM((2, rows, keys), F32),
                pltpu.VMEM((2, rows, keys), F32),
                pltpu.VMEM((2, rows, keys), BF),
                pltpu.VMEM((2, rows, keys), BF),
            ],
        ),
        out_shape=[
            jax.ShapeDtypeStruct((tokens, width), F32),
            jax.ShapeDtypeStruct((1, width), F32),
            jax.ShapeDtypeStruct((slots * keys, width), BF),
            square,
            square,
            square,
            square,
        ],
        compiler_params=params(),
        cost_estimate=pl.CostEstimate(
            flops=2 * slots * (keys * 4 + rows * 4) * width * width,
            bytes_accessed=20 << 20,
            transcendentals=slots * rows * keys * H,
        ),
        name="cross_backward",
    )(lims, gh2, h1, o2, c23, gains, mem_full, q, k, v, lse, c01, c01, c23)


def self_backward_body(
    lims, gh1_ref, x_ref, o1_ref, wo_ref, gain_ref, line_ref, q_ref, k_ref, v_ref, lse_ref, wq_ref, wk_ref, wv_ref,
    dx_ref, table_ref, dwq_ref, dwk_ref, dwv_ref, dwo_ref,
    g_ref, at_ref, da_ref, dq_ref, dk_ref, dv_ref, bias_ref, sum_ref, s_ref, dp_ref, p_ref, ds_ref,
):
    step = pl.program_id(0)
    slots, keys, width = x_ref.shape
    rows = q_ref.shape[1]
    off = lims[0]

    @pl.when(step == 0)
    def _():
        e = gh1_ref[...].astype(BF)
        back = dot_nt(e, wo_ref[...]).astype(BF)
        for b in range(width // WIDE):
            for s in range(slots):
                g_ref[b, s] = back[s * rows : (s + 1) * rows, b * WIDE : (b + 1) * WIDE]
        dwo_ref[...] = dot_tn(o1_ref[...], e).astype(BF)
        for s in range(slots):
            at_ref[:, s * keys : (s + 1) * keys] = normed(x_ref[s].astype(F32), gain_ref[0:1, :]).T
        da_ref[...] = jnp.zeros_like(da_ref)

    for h in range(WIDE // DK):
        build_bias(line_ref[0, h : h + 1, :], off, bias_ref.at[h])
    counts = [lims[1 + s] for s in range(slots)]
    attend_back(
        q_ref, k_ref, v_ref, g_ref.at[step], lse_ref, dq_ref, dk_ref, dv_ref,
        bias_ref, sum_ref, s_ref, dp_ref, p_ref, ds_ref, off, counts,
    )
    for h in range(WIDE // DK):
        table_ref[0, h : h + 1, :] = sum_diagonals(sum_ref.at[h], off)
    dwq = None
    for s in range(slots):
        mine = pl.ds(pl.multiple_of(s * keys + off, 128), rows)
        dq = dq_ref[s * rows : (s + 1) * rows, :]
        part = dot_nn(at_ref[:, mine], dq)
        dwq = part if dwq is None else dwq + part
        da_ref[mine, :] += dot_nt(dq, wq_ref[...])
    dwq_ref[...] = dwq.astype(BF)
    dwk_ref[...] = dot_nn(at_ref[...], dk_ref[...]).astype(BF)
    dwv_ref[...] = dot_nn(at_ref[...], dv_ref[...]).astype(BF)
    da_ref[...] += dot_nt(dk_ref[...], wk_ref[...]) + dot_nt(dv_ref[...], wv_ref[...])

    @pl.when(step == pl.num_programs(0) - 1)
    def _():
        dx_ref[...] = da_ref[...].astype(BF)


def self_backward(lims, gh1, x_full, o1, w01, w23, gains, line, q, k, v, lse):
    slots, keys, width = x_full.shape
    rows = q.shape[1]
    tokens = slots * rows
    blocks = width // WIDE
    square = jax.ShapeDtypeStruct((width, width), BF)
    heads = WIDE // DK
    return pl.pallas_call(
        self_backward_body,
        grid_spec=pltpu.PrefetchScalarGridSpec(
            num_scalar_prefetch=1,
            grid=(blocks,),
            in_specs=[
                whole((tokens, width)),
                whole((slots, keys, width)),
                whole((tokens, width)),
                whole_of(1, (width, width)),
                whole(gains.shape),
                pl.BlockSpec((1, heads, keys), lambda b, *_: (b, 0, 0)),
                wide((slots, rows, width)),
                wide((slots, keys, width)),
                wide((slots, keys, width)),
                pl.BlockSpec((slots, 2, rows, PAIR), lambda b, *_: (0, b, 0, 0)),
                wide_of(0, (width, width)),
                wide_of(1, (width, width)),
                wide_of(0, (width, width)),
            ],
            out_specs=[
                result((slots * keys, width)),
                pl.BlockSpec((1, heads, keys), lambda b, *_: (b, 0, 0)),
                wide((width, width)),
                wide((width, width)),
                wide((width, width)),
                result((width, width)),
            ],
            scratch_shapes=[
                pltpu.VMEM((blocks, slots, rows, WIDE), BF),
                pltpu.VMEM((width, slots * keys), BF),
                pltpu.VMEM((slots * keys, width), F32),
                pltpu.VMEM((tokens, WIDE), BF),
                pltpu.VMEM((slots * keys, WIDE), BF),
                pltpu.VMEM((slots * keys, WIDE), BF),
                pltpu.VMEM((heads, rows, keys), F32),
                pltpu.VMEM((heads, rows, keys), F32),
                pltpu.VMEM((2, rows, keys), F32),
                pltpu.VMEM((2, rows, keys), F32),
                pltpu.VMEM((2, rows, keys), BF),
                pltpu.VMEM((2, rows, keys), BF),
            ],
        ),
        out_shape=[
            jax.ShapeDtypeStruct((slots * keys, width), BF),
            jax.ShapeDtypeStruct((blocks, heads, keys), F32),
            square,
            square,
            square,
            square,
        ],
        compiler_params=params(),
        cost_estimate=pl.CostEstimate(
            flops=2 * slots * (keys * 4 + rows * 4) * width * width,
            bytes_accessed=30 << 20,
            transcendentals=slots * rows * keys * H,
        ),
        name="self_backward",
    )(lims, gh1, x_full, o1, w23, gains, line, q, k, v, lse, w01, w01, w23)


class Cube:
    def __init__(self, mesh):
        self.sizes = {name: mesh.shape[name] for name in ("dp", "seq")}
        self.bits = {}
        for name, size in self.sizes.items():
            count = size.bit_length() - 1
            assert size == 1 << count
            self.bits[name] = [(name, b) for b in reversed(range(count))]
        self.all = self.bits["dp"] + self.bits["seq"]

    def partner(self, x, dim):
        name, b = dim
        return lax.ppermute(x, name, [(i, i ^ (1 << b)) for i in range(self.sizes[name])])

    def second(self, dim):
        name, b = dim
        return (lax.axis_index(name) >> b) & 1

    def gather(self, x, axis, dims, order):
        lead, tail = x.shape[:axis], x.shape[axis + 1 :]
        x = x.reshape(lead + (1,) * len(dims) + x.shape[axis:])
        for dim in order:
            at = axis + dims.index(dim)
            other = self.partner(x, dim)
            second = self.second(dim) == 1
            x = jnp.concatenate([jnp.where(second, other, x), jnp.where(second, x, other)], axis=at)
        return x.reshape(lead + (-1,) + tail)

    def scatter(self, x, axis, dims, order, last=F32):
        lead, tail = x.shape[:axis], x.shape[axis + 1 :]
        count = 1 << len(dims)
        x = x.reshape(lead + (2,) * len(dims) + (x.shape[axis] // count,) + tail)
        for n, dim in enumerate(order):
            at = axis + dims.index(dim)
            second = self.second(dim)
            send = lax.dynamic_slice_in_dim(x, 1 - second, 1, at)
            keep = lax.dynamic_slice_in_dim(x, second, 1, at)
            got = self.partner(send, dim)
            x = keep.astype(F32) + got.astype(F32)
            x = x.astype(last if n == len(order) - 1 else BF)
        return x.reshape(lead + (-1,) + tail)

    def total(self, x, dims):
        for dim in dims:
            x = x + self.partner(x, dim)
        return x


def per_device(
    mesh,
    dec_in,
    memory,
    cotangent,
    dec_lengths,
    mem_mask,
    bucket_map,
    self_weights,
    cross_weights,
    ffn_in,
    ffn_out,
    norm_gains,
    bias_table,
):
    cube = Cube(mesh)
    everyone = cube.all
    near = cube.bits["seq"]
    far = cube.bits["dp"]
    slots, rows, width = dec_in.shape
    tokens = slots * rows
    buckets = bias_table.shape[0]
    core, across, along = near[-1:], near[:-1], far[-1:]
    rest = far[:-1]
    order_a = rest + along + across + core
    order_b = across + rest + along + core

    gate_full = lax.all_gather(ffn_in, ("dp", "seq"), axis=1, tiled=True)
    x_full = cube.gather(dec_in, 1, near, across + core)
    w01 = cube.gather(self_weights[0:2], 1, everyone, order_a)
    w23 = cube.gather(self_weights[2:4], 1, everyone, order_b)
    mem_full = cube.gather(memory, 1, near, across + core)
    seen = cube.total(jnp.sum(mem_mask, axis=1), near)
    c01 = cube.gather(cross_weights[0:2], 1, everyone, order_a)
    c23 = cube.gather(cross_weights[2:4], 1, everyone, order_b)
    down_full = cube.gather(ffn_out, 0, everyone, order_a)

    positions = bucket_map.shape[0]
    hot = (bucket_map[::-1][None, :] == jnp.arange(buckets, dtype=jnp.int32)[:, None]).astype(F32)
    line = jnp.einsum("bh,bm->hm", bias_table, hot, precision=lax.Precision.HIGHEST)
    line = line.reshape(H * DK // WIDE, WIDE // DK, positions)
    start = (lax.axis_index("seq") * rows).astype(jnp.int32)
    lims = jnp.concatenate([start[None], dec_lengths])
    lims_cross = jnp.concatenate([start[None], seen])

    q1, k1, v1, o1, lse1 = self_forward(lims, x_full, norm_gains, w01, w23, line, rows)
    h1, q2, k2, v2, o2, lse2 = cross_forward(lims_cross, dec_in, o1, w23, norm_gains, mem_full, c01, c23)
    flat = (tokens, width)
    h1 = h1.reshape(flat)
    o1 = o1.reshape(flat)
    o2 = o2.reshape(flat)
    layer_out, gh2, gain_third, dw0, dw1, dwd = feed_forward(
        h1, o2, c23, norm_gains, cotangent.reshape(flat), gate_full, down_full
    )
    gate_part = jnp.stack([dw0, dw1])
    gate_shard = lax.psum_scatter(gate_part, ("dp", "seq"), scatter_dimension=1, tiled=True).astype(F32)
    order_c = core + across + along + rest
    order_d = core + along + rest + across
    down_shard = cube.scatter(dwd, 0, everyone, order_c)
    gh1, gain_second, dmem, cq, ck, cv, co = cross_backward(
        lims_cross, gh2, h1, o2, c01, c23, norm_gains, mem_full, q2, k2, v2, lse2
    )
    cross_shard = jnp.concatenate(
        [
            cube.scatter(jnp.stack([cq, ck]), 1, everyone, order_c),
            cube.scatter(jnp.stack([cv, co]), 1, everyone, order_d),
        ]
    )
    mem_grad = cube.scatter(dmem.reshape(mem_full.shape), 1, near, core + across)
    dx, table, sq, sk, sv, so = self_backward(
        lims, gh1, x_full, o1, w01, w23, norm_gains, line, q1, k1, v1, lse1
    )
    self_shard = jnp.concatenate(
        [
            cube.scatter(jnp.stack([sq, sk]), 1, everyone, order_c),
            cube.scatter(jnp.stack([sv, so]), 1, everyone, order_d),
        ]
    )
    c_first = cube.scatter(dx.reshape(x_full.shape), 1, near, core + across)
    dv, gain_first = normed_back(dec_in.astype(F32).reshape(flat), norm_gains[0:1], c_first.reshape(flat))
    dec_grad = (gh1 + dv).reshape(dec_in.shape)
    table_part = jnp.einsum("hm,bm->bh", table.reshape(H, positions), hot, precision=lax.Precision.HIGHEST)

    self_square = self_shard * self_shard
    cross_square = cross_shard * cross_shard
    gate_square = gate_shard * gate_shard
    down_square = down_shard * down_shard
    hidden = ffn_in.shape[2]
    terms = [
        jnp.concatenate([gain_first, gain_second, gain_third]),
        table_part,
        jnp.sum(self_square, axis=1) / width,
        jnp.sum(cross_square, axis=1) / width,
        jnp.sum(gate_square, axis=1) / width,
        jnp.sum(down_square, axis=0) / hidden,
    ]
    packed = jnp.concatenate([t.reshape(-1, 128) for t in terms])
    packed = cube.total(packed, near + far)
    sums = []
    at = 0
    for t in terms:
        count = t.size // 128
        sums.append(packed[at : at + count].reshape(t.shape))
        at += count
    gains_grad, table_grad, self_cols, cross_cols, gate_cols, down_cols = sums
    self_row_means = jnp.mean(self_square, axis=2)
    cross_row_means = jnp.mean(cross_square, axis=2)
    shard_rows = self_shard.shape[1]
    column_start = lax.axis_index(("dp", "seq")) * shard_rows
    self_col_piece = lax.dynamic_slice_in_dim(self_cols[3], column_start, shard_rows, 0)
    cross_col_piece = lax.dynamic_slice_in_dim(cross_cols[3], column_start, shard_rows, 0)
    out_proj_stats = jnp.stack(
        [
            jnp.stack([self_row_means[3], self_col_piece]),
            jnp.stack([cross_row_means[3], cross_col_piece]),
        ]
    )
    return (
        layer_out.reshape(dec_in.shape),
        dec_grad,
        mem_grad,
        self_shard,
        cross_shard,
        gate_shard,
        down_shard,
        gains_grad,
        table_grad,
        self_row_means[:3],
        self_cols[:3],
        cross_row_means[:3],
        cross_cols[:3],
        jnp.mean(gate_square, axis=2),
        gate_cols,
        jnp.mean(down_square, axis=1),
        down_cols,
        out_proj_stats,
    )


def solution(mesh):
    in_specs = (
        P("dp", "seq", None),
        P("dp", "seq", None),
        P("dp", "seq", None),
        P("dp"),
        P("dp", "seq"),
        P(),
        P(None, ("dp", "seq"), None),
        P(None, ("dp", "seq"), None),
        P(None, ("dp", "seq"), None),
        P(("dp", "seq"), None),
        P(),
        P(),
    )
    out_specs = (
        P("dp", "seq", None),
        P("dp", "seq", None),
        P("dp", "seq", None),
        P(None, ("dp", "seq"), None),
        P(None, ("dp", "seq"), None),
        P(None, ("dp", "seq"), None),
        P(("dp", "seq"), None),
        P(),
        P(),
        P(None, ("dp", "seq")),
        P(),
        P(None, ("dp", "seq")),
        P(),
        P(None, ("dp", "seq")),
        P(),
        P(("dp", "seq")),
        P(),
        P(None, None, ("dp", "seq")),
    )
    return jax.shard_map(
        functools.partial(per_device, mesh),
        mesh=mesh,
        in_specs=in_specs,
        out_specs=out_specs,
        check_vma=False,
    )
```

```python
import functools

import jax
import jax.numpy as jnp
from jax import lax
from jax.experimental import pallas as pl
from jax.experimental.pallas import tpu as pltpu
from jax.sharding import PartitionSpec as P

H = 12
DK = 64
PAIR = 2 * DK
WIDE = 4 * DK
TILE = 512
UNIT = 24
TAIL = 8
EPS = 1e-06
MASKED = -1000000000.0
BF = jnp.bfloat16
F32 = jnp.float32
BUDGET = 60 * 1024 * 1024
COST = pl.CostEstimate(flops=1000, bytes_accessed=1000, transcendentals=0)


def dot_nn(a, b):
    return lax.dot_general(a, b, (((1,), (0,)), ((), ())), preferred_element_type=F32)


def dot_nt(a, b):
    return lax.dot_general(a, b, (((1,), (1,)), ((), ())), preferred_element_type=F32)


def dot_tn(a, b):
    return lax.dot_general(a, b, (((0,), (0,)), ((), ())), preferred_element_type=F32)


def inverse_rms(v):
    return lax.rsqrt(jnp.mean(v * v, axis=-1, keepdims=True) + EPS)


def normed(v, gain):
    return (v * inverse_rms(v) * gain).astype(BF)


def normed_back(v, gain, c):
    r = inverse_rms(v)
    scaled = c * gain
    inner = jnp.mean(v * scaled, axis=-1, keepdims=True)
    dv = r * scaled - v * (r * r * r * inner)
    dgain = jnp.sum(c * v * r, axis=0, keepdims=True)
    return dv, dgain


def shear(rows, sign):
    keys = rows.shape[1]
    r = lax.broadcasted_iota(jnp.int32, (8, 1), 0)
    for bit in (1, 2, 4):
        turned = pltpu.roll(rows, bit if sign > 0 else keys - bit, 1)
        rows = jnp.where((r & bit) != 0, turned, rows)
    return rows


def build_bias(line, off, out_ref):
    count, keys = out_ref.shape
    base = shear(pltpu.roll(jnp.broadcast_to(line, (8, keys)), off + 1, 1), 1)
    for g in range(count // 8):
        out_ref[8 * g : 8 * g + 8, :] = pltpu.roll(base, (8 * g) % keys, 1) if g else base


def sum_diagonals(sum_ref, off):
    count, keys = sum_ref.shape
    total = sum_ref[0:8, :]
    for g in range(1, count // 8):
        total = total + pltpu.roll(sum_ref[8 * g : 8 * g + 8, :], (keys - 8 * g) % keys, 1)
    total = jnp.sum(shear(total, -1), axis=0, keepdims=True)
    return pltpu.roll(jnp.broadcast_to(total, (8, keys)), keys - 1 - off, 1)[0:1]


def low_lanes():
    return lax.broadcasted_iota(jnp.int32, (1, PAIR), 1) < DK


def head_part(x, head):
    low = low_lanes()
    mine = low if head % 2 == 0 else jnp.logical_not(low)
    return jnp.where(mine, x, jnp.zeros_like(x))


def row_limit(start, rows, count, causal):
    if not causal:
        return count
    seen = start + 1 + lax.broadcasted_iota(jnp.int32, (rows, 1), 0)
    return jnp.minimum(seen, count)


def attend(q_ref, k_ref, v_ref, o_ref, lse_ref, bias_ref, s_ref, p_ref, off, counts):
    slots, rows, _ = q_ref.shape
    keys = k_ref.shape[1]
    causal = bias_ref is not None
    cols = lax.broadcasted_iota(jnp.int32, (1, keys), 1)
    low = low_lanes()
    work = [(s, h) for s in range(slots) for h in range(WIDE // DK)]

    def lanes(h):
        return slice((h // 2) * PAIR, (h // 2) * PAIR + PAIR)

    def scores(n):
        s, h = work[n]
        s_ref[n % 2] = dot_nt(head_part(q_ref[s, :, lanes(h)], h), k_ref[s, :, lanes(h)])

    scores(0)
    kept = None
    for n, (s, h) in enumerate(work):
        if n + 1 < len(work):
            scores(n + 1)
        sc = s_ref[n % 2]
        if causal:
            sc = sc + bias_ref[h]
        sc = jnp.where(cols < row_limit(off, rows, counts[s], causal), sc, MASKED)
        top = jnp.max(sc, axis=1, keepdims=True)
        e = jnp.exp(sc - top)
        total = jnp.sum(e, axis=1, keepdims=True)
        p_ref[n % 2] = (e * (1.0 / total)).astype(BF)
        out = dot_nn(p_ref[n % 2], v_ref[s, :, lanes(h)])
        log_total = jnp.broadcast_to(top + jnp.log(total), (rows, PAIR))
        if h % 2 == 0:
            kept = (out, log_total)
        else:
            o_ref[s, :, lanes(h)] = jnp.where(low, kept[0], out).astype(BF)
            lse_ref[s, h // 2] = jnp.where(low, kept[1], log_total)


def attend_back(
    q_ref, k_ref, v_ref, g_ref, lse_ref, dq_ref, dk_ref, dv_ref,
    bias_ref, sum_ref, s_ref, dp_ref, p_ref, ds_ref, off, counts,
):
    slots, rows, _ = q_ref.shape
    keys = k_ref.shape[1]
    causal = bias_ref is not None
    cols = lax.broadcasted_iota(jnp.int32, (1, keys), 1)
    low = low_lanes()
    work = [(s, h) for s in range(slots) for h in range(WIDE // DK)]

    def lanes(h):
        return slice((h // 2) * PAIR, (h // 2) * PAIR + PAIR)

    def products(n):
        s, h = work[n]
        s_ref[n % 2] = dot_nt(head_part(q_ref[s, :, lanes(h)], h), k_ref[s, :, lanes(h)])
        dp_ref[n % 2] = dot_nt(head_part(g_ref[s, :, lanes(h)], h), v_ref[s, :, lanes(h)])

    products(0)
    kept = None
    for n, (s, h) in enumerate(work):
        if n + 1 < len(work):
            products(n + 1)
        sc = s_ref[n % 2]
        if causal:
            sc = sc + bias_ref[h]
        sc = jnp.where(cols < row_limit(off, rows, counts[s], causal), sc, MASKED)
        at = (h % 2) * DK
        p = jnp.exp(sc - lse_ref[s, h // 2, :, at : at + 1])
        dp = dp_ref[n % 2]
        inner = jnp.sum(p * dp, axis=1, keepdims=True)
        ds = (p * (dp - inner)).astype(BF)
        p_ref[n % 2] = p.astype(BF)
        ds_ref[n % 2] = ds
        if causal:
            if s == 0:
                sum_ref[h] = ds.astype(F32)
            else:
                sum_ref[h] += ds.astype(F32)
        ds = ds_ref[n % 2]
        dq = dot_nn(ds, k_ref[s, :, lanes(h)])
        dk = dot_tn(head_part(q_ref[s, :, lanes(h)], h), ds)
        dv = dot_tn(head_part(g_ref[s, :, lanes(h)], h), p_ref[n % 2])
        if h % 2 == 0:
            kept = (dq, dk, dv)
        else:
            dq_ref[s * rows : (s + 1) * rows, lanes(h)] = jnp.where(low, kept[0], dq).astype(BF)
            dk_ref[s * keys : (s + 1) * keys, lanes(h)] = (kept[1] + dk).astype(BF).T
            dv_ref[s * keys : (s + 1) * keys, lanes(h)] = (kept[2] + dv).astype(BF).T


def assemble(own_ref, got_ref, bit):
    own, got = own_ref[...].astype(F32), got_ref[...].astype(F32)
    both = jnp.stack([jnp.where(bit == 0, own, got), jnp.where(bit == 0, got, own)], axis=1)
    return both.reshape(-1, both.shape[-1]).astype(BF)


def row_counts(ms):
    counts = []
    for s in range(ms[0].shape[0]):
        count = sum(m_ref[s, -TAIL:, 0:PAIR].astype(F32)[0:1, 0:1] for m_ref in ms)
        counts.append(count.astype(jnp.int32))
    return counts


def part_blocks(x, pairs, bit, keep_ref, send_ref):
    x = x.reshape(pairs, 2, -1, x.shape[-1])
    first, second = x[:, 0], x[:, 1]
    keep_ref[...] = jnp.where(bit == 0, first, second).astype(BF)
    send_ref[...] = jnp.where(bit == 0, second, first).astype(BF)


def whole(shape):
    return pl.BlockSpec(shape, lambda b, *_: (0,) * len(shape), pipeline_mode=pl.Buffered(1))


def result(shape):
    return pl.BlockSpec(shape, lambda b, *_: (0,) * len(shape))


def wide(shape):
    return pl.BlockSpec(shape[:-1] + (WIDE,), lambda b, *_: (0,) * (len(shape) - 1) + (b,))


def halves(index, shape, lanes=WIDE):
    pairs, _, rows, width = shape
    if lanes == width:
        spec = pl.BlockSpec(
            (pairs, None, rows, width), lambda b, *_: (0, index, 0, 0), pipeline_mode=pl.Buffered(1)
        )
    else:
        spec = pl.BlockSpec((pairs, None, rows, lanes), lambda b, *_: (0, index, 0, b))
    return [spec, spec]


def params():
    return pltpu.CompilerParams(dimension_semantics=("arbitrary",), vmem_limit_bytes=BUDGET)


def self_forward_body(near, lims, *refs):
    xs = refs[: len(near)]
    (
        gain_ref, wq_own, wq_got, wk_own, wk_got, wv_own, wv_got, line_ref,
        q_ref, k_ref, v_ref, o_ref, lse_ref, a_ref, bias_ref, s_ref, p_ref,
    ) = refs[len(near) :]
    slots, rows, width = xs[0].shape
    keys = k_ref.shape[1]
    off, me, bit = lims[0], lims[1 + slots], lims[2 + slots]

    @pl.when(pl.program_id(0) == 0)
    def _():
        for r, x_ref in zip(near, xs, strict=True):
            for s in range(slots):
                at = pl.multiple_of(s * keys + (me ^ r) * rows, 128)
                a_ref[pl.ds(at, rows), :] = normed(x_ref[s].astype(F32), gain_ref[0:1, :])

    wq, wk, wv = assemble(wq_own, wq_got, bit), assemble(wk_own, wk_got, bit), assemble(wv_own, wv_got, bit)
    for s in range(slots):
        mine = pl.ds(pl.multiple_of(s * keys + off, 128), rows)
        q_ref[s] = dot_nn(a_ref[mine, :], wq).astype(BF)
        k_ref[s] = dot_nn(a_ref[s * keys : (s + 1) * keys, :], wk).astype(BF)
        v_ref[s] = dot_nn(a_ref[s * keys : (s + 1) * keys, :], wv).astype(BF)
    for h in range(WIDE // DK):
        build_bias(line_ref[0, h : h + 1, :], off, bias_ref.at[h])
    counts = [lims[1 + s] for s in range(slots)]
    attend(q_ref, k_ref, v_ref, o_ref, lse_ref, bias_ref, s_ref, p_ref, off, counts)


def self_forward(lims, near, xs, gains, own, got, line):
    slots, rows, width = xs[0].shape
    keys = rows * len(near)
    blocks = width // WIDE
    return pl.pallas_call(
        functools.partial(self_forward_body, near),
        grid_spec=pltpu.PrefetchScalarGridSpec(
            num_scalar_prefetch=1,
            grid=(blocks,),
            in_specs=[whole((slots, rows, width))] * len(near)
            + [whole(gains.shape)]
            + halves(0, own.shape)
            + halves(1, own.shape)
            + halves(2, own.shape)
            + [pl.BlockSpec((1, WIDE // DK, keys), lambda b, *_: (b, 0, 0))],
            out_specs=[
                wide((slots, rows, width)),
                wide((slots, keys, width)),
                wide((slots, keys, width)),
                wide((slots, rows, width)),
                pl.BlockSpec((slots, 2, rows, PAIR), lambda b, *_: (0, b, 0, 0)),
            ],
            scratch_shapes=[
                pltpu.VMEM((slots * keys, width), BF),
                pltpu.VMEM((WIDE // DK, rows, keys), F32),
                pltpu.VMEM((2, rows, keys), F32),
                pltpu.VMEM((2, rows, keys), BF),
            ],
        ),
        out_shape=[
            jax.ShapeDtypeStruct((slots, rows, width), BF),
            jax.ShapeDtypeStruct((slots, keys, width), BF),
            jax.ShapeDtypeStruct((slots, keys, width), BF),
            jax.ShapeDtypeStruct((slots, rows, width), BF),
            jax.ShapeDtypeStruct((slots, H // 2, rows, PAIR), F32),
        ],
        compiler_params=params(),
        cost_estimate=COST,
        name="self_forward",
    )(lims, *xs, gains, own, got, own, got, own, got, line)


def cross_forward_body(near, lims, *refs):
    ms = refs[: len(near)]
    (
        x_ref, o1_ref, wo_own, wo_got, gain_ref, wq_own, wq_got, wk_own, wk_got, wv_own, wv_got,
        h_ref, q_ref, k_ref, v_ref, o_ref, lse_ref, a_ref, mem_ref, s_ref, p_ref,
    ) = refs[len(near) :]
    slots, part, width = ms[0].shape
    part -= TAIL
    rows, keys = q_ref.shape[1], k_ref.shape[1]
    me, bit = lims[1 + slots], lims[2 + slots]

    @pl.when(pl.program_id(0) == 0)
    def _():
        wo = assemble(wo_own, wo_got, bit)
        for s in range(slots):
            h = x_ref[s].astype(F32) + dot_nn(o1_ref[s], wo)
            h_ref[s] = h
            a_ref[s * rows : (s + 1) * rows, :] = normed(h, gain_ref[1:2, :])
        for r, m_ref in zip(near, ms, strict=True):
            for s in range(slots):
                mem_ref[s, pl.ds(pl.multiple_of((me ^ r) * part, part), part), :] = m_ref[s, :part]

    wq, wk, wv = assemble(wq_own, wq_got, bit), assemble(wk_own, wk_got, bit), assemble(wv_own, wv_got, bit)
    for s in range(slots):
        q_ref[s] = dot_nn(a_ref[s * rows : (s + 1) * rows, :], wq).astype(BF)
        k_ref[s] = dot_nn(mem_ref[s], wk).astype(BF)
        v_ref[s] = dot_nn(mem_ref[s], wv).astype(BF)
    counts = row_counts(ms)
    attend(q_ref, k_ref, v_ref, o_ref, lse_ref, None, s_ref, p_ref, 0, counts)


def cross_forward(lims, near, ms, x, o1, own1, got1, gains, own, got):
    slots, part, width = ms[0].shape
    part -= TAIL
    keys = part * len(near)
    rows = x.shape[1]
    blocks = width // WIDE
    return pl.pallas_call(
        functools.partial(cross_forward_body, near),
        grid_spec=pltpu.PrefetchScalarGridSpec(
            num_scalar_prefetch=1,
            grid=(blocks,),
            in_specs=[whole((slots, part + TAIL, width))] * len(near)
            + [whole((slots, rows, width)), whole((slots, rows, width))]
            + halves(3, own1.shape, width)
            + [whole(gains.shape)]
            + halves(0, own.shape)
            + halves(1, own.shape)
            + halves(2, own.shape),
            out_specs=[
                result((slots, rows, width)),
                wide((slots, rows, width)),
                wide((slots, keys, width)),
                wide((slots, keys, width)),
                wide((slots, rows, width)),
                pl.BlockSpec((slots, 2, rows, PAIR), lambda b, *_: (0, b, 0, 0)),
            ],
            scratch_shapes=[
                pltpu.VMEM((slots * rows, width), BF),
                pltpu.VMEM((slots, keys, width), BF),
                pltpu.VMEM((2, rows, keys), F32),
                pltpu.VMEM((2, rows, keys), BF),
            ],
        ),
        out_shape=[
            jax.ShapeDtypeStruct((slots, rows, width), F32),
            jax.ShapeDtypeStruct((slots, rows, width), BF),
            jax.ShapeDtypeStruct((slots, keys, width), BF),
            jax.ShapeDtypeStruct((slots, keys, width), BF),
            jax.ShapeDtypeStruct((slots, rows, width), BF),
            jax.ShapeDtypeStruct((slots, H // 2, rows, PAIR), F32),
        ],
        compiler_params=params(),
        cost_estimate=COST,
        name="cross_forward",
    )(lims, *ms, x, o1, own1, got1, gains, own, got, own, got, own, got)


def feed_forward_body(
    lims, h1_ref, o2_ref, wo_own, wo_got, gain_ref, g_ref, w0_ref, w1_ref, wd_ref,
    out_ref, gh_ref, dgain_ref, dw_ref, dkeep_ref, dsend_ref, h_ref, a_ref, at_ref, acc_ref, da_ref,
):
    step = pl.program_id(0)
    bit = lims[lims.shape[0] - 1]

    @pl.when(step == 0)
    def _():
        h = h1_ref[...] + dot_nn(o2_ref[...], assemble(wo_own, wo_got, bit))
        h_ref[...] = h
        a = normed(h, gain_ref[2:3, :])
        a_ref[...] = a
        at_ref[...] = a.T
        acc_ref[...] = h
        da_ref[...] = jnp.zeros_like(da_ref)

    a = a_ref[...]
    e = g_ref[...]
    gate = dot_nn(a, w0_ref[...])
    up = dot_nn(a, w1_ref[...])
    c = dot_nt(e, wd_ref[...])
    root = 0.7978845608028654
    square = gate * gate
    th = jnp.tanh(root * gate * (1.0 + 0.044715 * square))
    half = 0.5 * (1.0 + th)
    act = gate * half
    slope = half + 0.5 * gate * (1.0 - th * th) * (root * (1.0 + 3.0 * 0.044715 * square))
    hidden = (act * up).astype(BF)
    dgate = (c * up * slope).astype(BF)
    dup = (c * act).astype(BF)
    acc_ref[...] += dot_nn(hidden, wd_ref[...])
    part_blocks(dot_tn(hidden, e), dkeep_ref.shape[0], bit, dkeep_ref, dsend_ref)
    tile = dgate.shape[1]
    dw_ref[:, :tile] = dot_nn(at_ref[...], dgate).astype(BF)
    dw_ref[:, tile:] = dot_nn(at_ref[...], dup).astype(BF)
    da_ref[...] += dot_nt(dgate, w0_ref[...]) + dot_nt(dup, w1_ref[...])

    @pl.when(step == pl.num_programs(0) - 1)
    def _():
        out_ref[...] = acc_ref[...].astype(BF)
        dv, dgain = normed_back(h_ref[...], gain_ref[2:3, :], da_ref[...])
        gh_ref[...] = e.astype(F32) + dv
        dgain_ref[...] = dgain


def feed_forward(lims, h1, o2, own, got, gains, cot, w0, w1, wd, pairs):
    tokens, width = h1.shape
    hidden = wd.shape[0]
    tile = TILE
    half = pl.BlockSpec((pairs * tile // hidden, hidden // (2 * pairs), width), lambda b, *_: (b, 0, 0))
    return pl.pallas_call(
        feed_forward_body,
        grid_spec=pltpu.PrefetchScalarGridSpec(
            num_scalar_prefetch=1,
            grid=(hidden // tile,),
            in_specs=[whole((tokens, width)), whole((tokens, width))]
            + halves(3, own.shape, width)
            + [
                whole(gains.shape),
                whole((tokens, width)),
                pl.BlockSpec((width, tile), lambda b, *_: (0, b)),
                pl.BlockSpec((width, tile), lambda b, *_: (0, b)),
                pl.BlockSpec((tile, width), lambda b, *_: (b, 0)),
            ],
            out_specs=[
                result((tokens, width)),
                result((tokens, width)),
                result((1, width)),
                pl.BlockSpec((width, 2 * tile), lambda b, *_: (0, b)),
                half,
                half,
            ],
            scratch_shapes=[
                pltpu.VMEM((tokens, width), F32),
                pltpu.VMEM((tokens, width), BF),
                pltpu.VMEM((width, tokens), BF),
                pltpu.VMEM((tokens, width), F32),
                pltpu.VMEM((tokens, width), F32),
            ],
        ),
        out_shape=[
            jax.ShapeDtypeStruct((tokens, width), BF),
            jax.ShapeDtypeStruct((tokens, width), F32),
            jax.ShapeDtypeStruct((1, width), F32),
            jax.ShapeDtypeStruct((width, 2 * hidden), BF),
            jax.ShapeDtypeStruct((pairs, hidden // (2 * pairs), width), BF),
            jax.ShapeDtypeStruct((pairs, hidden // (2 * pairs), width), BF),
        ],
        compiler_params=params(),
        cost_estimate=COST,
        name="feed_forward",
    )(lims, h1, o2, own, got, gains, cot, w0, w1, wd)


def cross_backward_body(near, lims, *refs):
    ms = refs[: len(near)]
    (
        gh2_ref, h1_ref, o1_ref, o2_ref, wo_own, wo_got, gain_ref, q_ref, k_ref, v_ref, lse_ref,
        wq_own, wq_got, wk_own, wk_got, wv_own, wv_got,
        gh_ref, dgain_ref, mkeep_ref, msend_ref, keep_ref, send_ref, skeep_ref, ssend_ref,
        g_ref, e_ref, at_ref, memt_ref, da_ref, dm_ref, dq_ref, dk_ref, dv_ref, s_ref, dp_ref, p_ref, ds_ref,
    ) = refs[len(near) :]
    step = pl.program_id(0)
    slots, part, width = ms[0].shape
    part -= TAIL
    rows, keys = q_ref.shape[1], k_ref.shape[1]
    me, bit = lims[1 + slots], lims[2 + slots]
    pairs = keep_ref.shape[0]

    @pl.when(step == 0)
    def _():
        e = gh2_ref[...].astype(BF)
        back = dot_nt(e, assemble(wo_own, wo_got, bit)).astype(BF)
        for b in range(width // WIDE):
            e_ref[b] = e[:, b * WIDE : (b + 1) * WIDE]
            for s in range(slots):
                g_ref[b, s] = back[s * rows : (s + 1) * rows, b * WIDE : (b + 1) * WIDE]
        at_ref[...] = normed(h1_ref[...], gain_ref[1:2, :]).T
        for r, m_ref in zip(near, ms, strict=True):
            for s in range(slots):
                at = pl.multiple_of(s * keys + (me ^ r) * part, part)
                memt_ref[pl.ds(at, part), :] = m_ref[s, :part]
        da_ref[...] = jnp.zeros_like(da_ref)
        dm_ref[...] = jnp.zeros_like(dm_ref)

    counts = row_counts(ms)
    attend_back(
        q_ref, k_ref, v_ref, g_ref.at[step], lse_ref, dq_ref, dk_ref, dv_ref,
        None, None, s_ref, dp_ref, p_ref, ds_ref, 0, counts,
    )
    for m, grad in enumerate(
        (
            dot_nn(at_ref[...], dq_ref[...]),
            dot_tn(memt_ref[...], dk_ref[...]),
            dot_tn(memt_ref[...], dv_ref[...]),
            dot_tn(o2_ref[...], e_ref[step]),
        )
    ):
        part_blocks(grad, pairs, bit, keep_ref.at[:, m], send_ref.at[:, m])
    da_ref[...] += dot_nt(dq_ref[...], assemble(wq_own, wq_got, bit))
    dm_ref[...] += dot_nt(dk_ref[...], assemble(wk_own, wk_got, bit)) + dot_nt(
        dv_ref[...], assemble(wv_own, wv_got, bit)
    )

    @pl.when(step == pl.num_programs(0) - 1)
    def _():
        dv, dgain = normed_back(h1_ref[...], gain_ref[1:2, :], da_ref[...])
        gh = gh2_ref[...] + dv
        gh_ref[...] = gh
        dgain_ref[...] = dgain
        part_blocks(dot_tn(o1_ref[...], gh.astype(BF)), pairs, bit, skeep_ref, ssend_ref)
        for s in range(slots):
            for n in range(len(near) // 2):
                keep = pl.multiple_of(s * keys + (2 * n + bit) * part, part)
                send = pl.multiple_of(s * keys + (2 * n + 1 - bit) * part, part)
                mkeep_ref[s * (len(near) // 2) + n] = dm_ref[pl.ds(keep, part), :].astype(BF)
                msend_ref[s * (len(near) // 2) + n] = dm_ref[pl.ds(send, part), :].astype(BF)


def cross_backward(lims, near, ms, gh2, h1, o1, o2, own, got, gains, q, k, v, lse):
    slots, part, width = ms[0].shape
    part -= TAIL
    keys = part * len(near)
    rows = q.shape[1]
    tokens = slots * rows
    blocks = width // WIDE
    pairs, count, unit, _ = own.shape
    half = jax.ShapeDtypeStruct((slots * len(near) // 2, part, width), BF)
    grads = pl.BlockSpec((pairs, count, unit, WIDE), lambda b, *_: (0, 0, 0, b))
    return pl.pallas_call(
        functools.partial(cross_backward_body, near),
        grid_spec=pltpu.PrefetchScalarGridSpec(
            num_scalar_prefetch=1,
            grid=(blocks,),
            in_specs=[whole((slots, part + TAIL, width))] * len(near)
            + [whole((tokens, width))] * 4
            + halves(3, own.shape, width)
            + [
                whole(gains.shape),
                wide((slots, rows, width)),
                wide((slots, keys, width)),
                wide((slots, keys, width)),
                pl.BlockSpec((slots, 2, rows, PAIR), lambda b, *_: (0, b, 0, 0)),
            ]
            + halves(0, own.shape)
            + halves(1, own.shape)
            + halves(2, own.shape),
            out_specs=[
                result((tokens, width)),
                result((1, width)),
                result(half.shape),
                result(half.shape),
                grads,
                grads,
                result((pairs, unit, width)),
                result((pairs, unit, width)),
            ],
            scratch_shapes=[
                pltpu.VMEM((blocks, slots, rows, WIDE), BF),
                pltpu.VMEM((blocks, tokens, WIDE), BF),
                pltpu.VMEM((width, tokens), BF),
                pltpu.VMEM((slots * keys, width), BF),
                pltpu.VMEM((tokens, width), F32),
                pltpu.VMEM((slots * keys, width), F32),
                pltpu.VMEM((tokens, WIDE), BF),
                pltpu.VMEM((slots * keys, WIDE), BF),
                pltpu.VMEM((slots * keys, WIDE), BF),
                pltpu.VMEM((2, rows, keys), F32),
                pltpu.VMEM((2, rows, keys), F32),
                pltpu.VMEM((2, rows, keys), BF),
                pltpu.VMEM((2, rows, keys), BF),
            ],
        ),
        out_shape=[
            jax.ShapeDtypeStruct((tokens, width), F32),
            jax.ShapeDtypeStruct((1, width), F32),
            half,
            half,
            jax.ShapeDtypeStruct(own.shape, BF),
            jax.ShapeDtypeStruct(own.shape, BF),
            jax.ShapeDtypeStruct((pairs, unit, width), BF),
            jax.ShapeDtypeStruct((pairs, unit, width), BF),
        ],
        compiler_params=params(),
        cost_estimate=COST,
        name="cross_backward",
    )(lims, *ms, gh2, h1, o1, o2, own, got, gains, q, k, v, lse, own, got, own, got, own, got)


def self_backward_body(near, lims, *refs):
    xs = refs[: len(near)]
    (
        gh1_ref, wo_own, wo_got, gain_ref, line_ref, q_ref, k_ref, v_ref, lse_ref,
        wq_own, wq_got, wk_own, wk_got, wv_own, wv_got,
        xkeep_ref, xsend_ref, table_ref, keep_ref, send_ref,
        g_ref, at_ref, da_ref, dq_ref, dk_ref, dv_ref, bias_ref, sum_ref, s_ref, dp_ref, p_ref, ds_ref,
    ) = refs[len(near) :]
    step = pl.program_id(0)
    slots, rows, width = xs[0].shape
    keys = k_ref.shape[1]
    off, me, bit = lims[0], lims[1 + slots], lims[2 + slots]
    pairs = keep_ref.shape[0]

    @pl.when(step == 0)
    def _():
        e = gh1_ref[...].astype(BF)
        back = dot_nt(e, assemble(wo_own, wo_got, bit)).astype(BF)
        for b in range(width // WIDE):
            for s in range(slots):
                g_ref[b, s] = back[s * rows : (s + 1) * rows, b * WIDE : (b + 1) * WIDE]
        for r, x_ref in zip(near, xs, strict=True):
            for s in range(slots):
                at = pl.multiple_of(s * keys + (me ^ r) * rows, 128)
                at_ref[:, pl.ds(at, rows)] = normed(x_ref[s].astype(F32), gain_ref[0:1, :]).T
        da_ref[...] = jnp.zeros_like(da_ref)

    for h in range(WIDE // DK):
        build_bias(line_ref[0, h : h + 1, :], off, bias_ref.at[h])
    counts = [lims[1 + s] for s in range(slots)]
    attend_back(
        q_ref, k_ref, v_ref, g_ref.at[step], lse_ref, dq_ref, dk_ref, dv_ref,
        bias_ref, sum_ref, s_ref, dp_ref, p_ref, ds_ref, off, counts,
    )
    for h in range(WIDE // DK):
        table_ref[0, h : h + 1, :] = sum_diagonals(sum_ref.at[h], off)
    wq = assemble(wq_own, wq_got, bit)
    dwq = None
    for s in range(slots):
        mine = pl.ds(pl.multiple_of(s * keys + off, 128), rows)
        dq = dq_ref[s * rows : (s + 1) * rows, :]
        part = dot_nn(at_ref[:, mine], dq)
        dwq = part if dwq is None else dwq + part
        da_ref[mine, :] += dot_nt(dq, wq)
    for m, grad in enumerate((dwq, dot_nn(at_ref[...], dk_ref[...]), dot_nn(at_ref[...], dv_ref[...]))):
        part_blocks(grad, pairs, bit, keep_ref.at[:, m], send_ref.at[:, m])
    da_ref[...] += dot_nt(dk_ref[...], assemble(wk_own, wk_got, bit)) + dot_nt(
        dv_ref[...], assemble(wv_own, wv_got, bit)
    )

    @pl.when(step == pl.num_programs(0) - 1)
    def _():
        for s in range(slots):
            for n in range(len(near) // 2):
                keep = pl.multiple_of(s * keys + (2 * n + bit) * rows, 128)
                send = pl.multiple_of(s * keys + (2 * n + 1 - bit) * rows, 128)
                xkeep_ref[s * (len(near) // 2) + n] = da_ref[pl.ds(keep, rows), :].astype(BF)
                xsend_ref[s * (len(near) // 2) + n] = da_ref[pl.ds(send, rows), :].astype(BF)


def self_backward(lims, near, xs, gh1, own, got, gains, line, q, k, v, lse):
    slots, rows, width = xs[0].shape
    keys = rows * len(near)
    tokens = slots * rows
    blocks = width // WIDE
    pairs, count, unit, _ = own.shape
    heads = WIDE // DK
    half = jax.ShapeDtypeStruct((slots * len(near) // 2, rows, width), BF)
    grads = pl.BlockSpec((pairs, count - 1, unit, WIDE), lambda b, *_: (0, 0, 0, b))
    return pl.pallas_call(
        functools.partial(self_backward_body, near),
        grid_spec=pltpu.PrefetchScalarGridSpec(
            num_scalar_prefetch=1,
            grid=(blocks,),
            in_specs=[whole((slots, rows, width))] * len(near)
            + [whole((tokens, width))]
            + halves(3, own.shape, width)
            + [
                whole(gains.shape),
                pl.BlockSpec((1, heads, keys), lambda b, *_: (b, 0, 0)),
                wide((slots, rows, width)),
                wide((slots, keys, width)),
                wide((slots, keys, width)),
                pl.BlockSpec((slots, 2, rows, PAIR), lambda b, *_: (0, b, 0, 0)),
            ]
            + halves(0, own.shape)
            + halves(1, own.shape)
            + halves(2, own.shape),
            out_specs=[
                result(half.shape),
                result(half.shape),
                pl.BlockSpec((1, heads, keys), lambda b, *_: (b, 0, 0)),
                grads,
                grads,
            ],
            scratch_shapes=[
                pltpu.VMEM((blocks, slots, rows, WIDE), BF),
                pltpu.VMEM((width, slots * keys), BF),
                pltpu.VMEM((slots * keys, width), F32),
                pltpu.VMEM((tokens, WIDE), BF),
                pltpu.VMEM((slots * keys, WIDE), BF),
                pltpu.VMEM((slots * keys, WIDE), BF),
                pltpu.VMEM((heads, rows, keys), F32),
                pltpu.VMEM((heads, rows, keys), F32),
                pltpu.VMEM((2, rows, keys), F32),
                pltpu.VMEM((2, rows, keys), F32),
                pltpu.VMEM((2, rows, keys), BF),
                pltpu.VMEM((2, rows, keys), BF),
            ],
        ),
        out_shape=[
            half,
            half,
            jax.ShapeDtypeStruct((blocks, heads, keys), F32),
            jax.ShapeDtypeStruct((pairs, count - 1, unit, width), BF),
            jax.ShapeDtypeStruct((pairs, count - 1, unit, width), BF),
        ],
        compiler_params=params(),
        cost_estimate=COST,
        name="self_backward",
    )(lims, *xs, gh1, own, got, gains, line, q, k, v, lse, own, got, own, got, own, got)


def to_tiles(w):
    m, r, c = w.shape
    return w.reshape(m, r // 8, 8, c // 128, 128).transpose(0, 1, 3, 2, 4).reshape(-1, 8, 128)


def from_tiles(g, shape):
    r, c = shape
    g = g.reshape(g.shape[0], r // 8, c // 128, 8, 128)
    return g.transpose(0, 1, 3, 2, 4).reshape(-1, c)


def place_body(ways, scalar_ref, *refs):
    for r in range(ways):

        @pl.when(pl.program_id(0) == r)
        def _():
            refs[ways][...] = refs[r][...]


def place_blocks(place, parts):
    ways = len(parts)
    outer, inner, tail = parts[0].shape[0], parts[0].shape[1], parts[0].shape[2:]
    rest = (0,) * len(tail)
    spec = pl.BlockSpec((outer, inner) + tail, lambda r, s: (0, 0) + rest)
    return pl.pallas_call(
        functools.partial(place_body, ways),
        grid_spec=pltpu.PrefetchScalarGridSpec(
            num_scalar_prefetch=1,
            grid=(ways,),
            in_specs=[spec] * ways,
            out_specs=pl.BlockSpec((outer, None, inner) + tail, lambda r, s: (0, s[0] ^ r, 0) + rest),
        ),
        out_shape=jax.ShapeDtypeStruct((outer, ways, inner) + tail, BF),
        compiler_params=params(),
        cost_estimate=COST,
        name="place_blocks",
    )(place.reshape(1), *parts)


def fold_body(groups, ways, last, *refs):
    refs = refs[1:]
    inputs = ways * sum(1 + terms for _, terms in groups)
    outs = refs[inputs:]
    n = 0
    for j in range(ways):
        at = 0
        for size, terms in groups:
            x = refs[n][...].astype(F32)
            for t in range(terms):
                x = x + refs[n + 1 + t][...].astype(F32)
            n += 1 + terms
            outs[j][:, :, at : at + size] = x if last else x.astype(BF)
            at += size


def fold(place, ways, inner, groups, last):
    outer, width = groups[0][0].shape[0] // (ways * inner), groups[0][0].shape[-1]
    sizes = [g[0].shape[1] for g in groups]
    total = sum(sizes)
    step = outer
    moved = sum(size * (len(g) + 1) for size, g in zip(sizes, groups, strict=True))
    while step > 1 and step * inner * ways * moved * 8 * width * 2 > 6 * 1024 * 1024:
        step //= 2

    def spec(j, size):
        return pl.BlockSpec((step, None, inner, size, 8, width), lambda g, s: (g, s[0] ^ j, 0, 0, 0, 0))

    in_specs, ins = [], []
    for j in range(ways):
        for size, terms in zip(sizes, groups, strict=True):
            in_specs += [spec(j, size)] * len(terms)
            ins += [t.reshape((outer, ways, inner) + t.shape[1:]) for t in terms]
    made = pl.pallas_call(
        functools.partial(fold_body, [(size, len(g) - 1) for size, g in zip(sizes, groups, strict=True)], ways, last),
        grid_spec=pltpu.PrefetchScalarGridSpec(
            num_scalar_prefetch=1,
            grid=(outer // step,),
            in_specs=in_specs,
            out_specs=[pl.BlockSpec((step, inner, total, 8, width), lambda g, s: (g, 0, 0, 0, 0))] * ways,
        ),
        out_shape=[jax.ShapeDtypeStruct((outer, inner, total, 8, width), F32 if last else BF)] * ways,
        compiler_params=params(),
        cost_estimate=COST,
        name="fold_blocks",
    )(place.reshape(1), *ins)
    return [x.reshape((outer * inner,) + x.shape[2:]) for x in made]


def in_halves(w):
    x = w.reshape(w.shape[0], -1, 2, UNIT, w.shape[-1]).transpose(2, 1, 0, 3, 4)
    return x[0], x[1]


def from_halves(first, second):
    x = jnp.stack([first, second], axis=1)
    return x.transpose(2, 0, 1, 3, 4).reshape(x.shape[2], -1, x.shape[-1])


def in_rows(x):
    return x.reshape(x.shape[0], -1, 8, x.shape[-1])


class Cube:
    axes = ("dp", "seq")

    def __init__(self, mesh):
        self.near = mesh.shape["seq"].bit_length() - 1
        self.count = mesh.shape["dp"] * mesh.shape["seq"]
        bits = self.count.bit_length() - 1
        assert self.count == 1 << bits
        self.core, self.y, self.x, self.xy, self.z = (0, 2), (1, 2), (2, 2), (1, 4), (3, 4)
        self.fits = self.near == 2 and bits == 5
        self.bits = [(b, 2) for b in range(bits)]
        self.near_groups = [(b, 2) for b in range(self.near)]

    def place(self, group):
        low, ways = group
        return (lax.axis_index(self.axes).astype(jnp.int32) >> low) & (ways - 1)

    def partner(self, x, group, r):
        low, _ = group
        return lax.ppermute(x, self.axes, [(i, i ^ (r << low)) for i in range(self.count)])

    def total(self, x, groups):
        for group in groups:
            terms = [x] + [self.partner(x, group, r) for r in range(1, group[1])]
            while len(terms) > 1:
                terms = [p + q for p, q in zip(terms[::2], terms[1::2], strict=True)]
            x = terms[0]
        return x


class Gather:
    def __init__(self, cube, x, groups):
        self.cube, self.x, self.groups, self.seen = cube, x[None], list(groups), []

    def send(self):
        group = self.groups[0]
        self.got = [self.cube.partner(self.x, group, r) for r in range(1, group[1])]

    def take(self):
        group = self.groups.pop(0)
        inner = 1
        for low, ways in self.seen:
            inner *= ways if low < group[0] else 1
        self.seen.append(group)
        parts = [x.reshape((-1, inner) + x.shape[1:]) for x in [self.x] + list(self.got)]
        x = place_blocks(self.cube.place(group), parts)
        self.x = x.reshape((-1,) + self.x.shape[1:])

    def left(self):
        return len(self.groups)


class Parts:
    def __init__(self, cube, x, groups):
        self.cube, self.parts, self.ids, self.groups = cube, [x], [0], list(groups)

    def send(self):
        self.got = [self.cube.partner(x, self.groups[0], 1) for x in self.parts]

    def take(self):
        low, _ = self.groups.pop(0)
        self.parts = self.parts + list(self.got)
        self.ids = self.ids + [i | 1 << low for i in self.ids]

    def left(self):
        return len(self.groups)


class Sum:
    def __init__(self, cube, keeps, sends, groups):
        self.cube, self.groups = cube, list(groups)
        self.keeps, self.sends = list(keeps), [list(sends)]

    def send(self):
        group = self.groups[0]
        self.got = [[self.cube.partner(x, group, r + 1) for x in xs] for r, xs in enumerate(self.sends)]

    def take(self):
        self.groups.pop(0)
        terms = [[keep] + [got[i] for got in self.got] for i, keep in enumerate(self.keeps)]
        if self.groups:
            low, ways = self.groups[0]
            inner = 1
            for other, count in self.groups[1:]:
                inner *= count if other < low else 1
            keep, *sends = fold(self.cube.place((low, ways)), ways, inner, terms, False)
            self.keeps, self.sends = [keep], [[x] for x in sends]
        else:
            (self.x,) = fold(jnp.zeros((), jnp.int32), 1, 1, terms, True)

    def left(self):
        return len(self.groups)


def after(first, then):
    return lax.optimization_barrier((first, then))[1]


def land(moves, values):
    held = lax.optimization_barrier(([m.got for m in moves], tuple(values)))
    for m, got in zip(moves, held[0], strict=True):
        m.got = got
    return held[1]


def arrive(moves, values=()):
    values = land(moves, values)
    for m in moves:
        m.take()
    return values


def per_device(
    mesh,
    dec_in,
    memory,
    cotangent,
    dec_lengths,
    mem_mask,
    bucket_map,
    self_weights,
    cross_weights,
    ffn_in,
    ffn_out,
    norm_gains,
    bias_table,
):
    cube = Cube(mesh)
    near_sums, near_gathers = cube.near_groups, cube.near_groups[::-1]
    slots, rows, width = dec_in.shape
    tokens = slots * rows
    buckets = bias_table.shape[0]
    hidden = ffn_in.shape[2]
    unit = self_weights.shape[1]
    exchange = unit == UNIT and cube.fits
    bit = lax.axis_index("seq").astype(jnp.int32) & 1

    assert memory.shape[1] <= 256
    count = jnp.sum(mem_mask, axis=1).astype(BF)
    memory = jnp.concatenate([memory, jnp.broadcast_to(count[:, None, None], (slots, TAIL, width))], axis=1)
    x_move = Parts(cube, dec_in, near_gathers)
    m_move = Parts(cube, memory, near_gathers)
    x_move.send()
    if exchange:
        w_move = Gather(cube, self_weights, [cube.z, cube.xy])
        c_move = Gather(cube, cross_weights, [cube.y, cube.z, cube.x])
        w_move.send()
        c_move.send()
        w_move.take()
        w_move.send()
        x_move.got, c_move.got, ffn_in, ffn_out = after(w_move.x, (x_move.got, c_move.got, ffn_in, ffn_out))
        c_move.take()
        c_move.send()
        packed = jnp.concatenate([to_tiles(ffn_in), to_tiles(ffn_out[None])])
        gathered = lax.all_gather(packed, ("dp", "seq"), axis=0, tiled=False)
        x_move.take()
        x_move.send()
        w_move.take()
        w_move.x = after(c_move.got, w_move.x)
        w_got = cube.partner(w_move.x, cube.core, 1)
        x_move.got, c_move.got = after(w_move.x, (x_move.got, c_move.got))
        x_move.take()
        c_move.take()
        c_move.send()
        m_move.parts[0] = after(c_move.x, m_move.parts[0])
        m_move.send()
        own1, got1 = after(c_move.x, (w_move.x, w_got))
        tiles = ffn_in[0].size // 1024
        w0 = from_tiles(gathered[:, :tiles], ffn_in.shape[1:])
        w1 = from_tiles(gathered[:, tiles : 2 * tiles], ffn_in.shape[1:])
        wd = from_tiles(gathered[:, 2 * tiles :], ffn_out.shape)
    else:
        bit = bit * 0
        for move in (x_move, m_move):
            if move is m_move:
                move.send()
            arrive([move])
            while move.left():
                move.send()
                arrive([move])
        own1, got1 = in_halves(lax.all_gather(self_weights, ("dp", "seq"), axis=1, tiled=True))
        own2, got2 = in_halves(lax.all_gather(cross_weights, ("dp", "seq"), axis=1, tiled=True))
        w0, w1 = lax.all_gather(ffn_in, ("dp", "seq"), axis=1, tiled=True)
        wd = lax.all_gather(ffn_out, ("dp", "seq"), axis=0, tiled=True)

    positions = bucket_map.shape[0]
    hot = (bucket_map[::-1][None, :] == jnp.arange(buckets, dtype=jnp.int32)[:, None]).astype(F32)
    line = jnp.einsum("bh,bm->hm", bias_table, hot, precision=lax.Precision.HIGHEST)
    line = line.reshape(H * DK // WIDE, WIDE // DK, positions)
    me = lax.axis_index("seq").astype(jnp.int32)
    lims = jnp.concatenate([(me * rows)[None], dec_lengths, me[None], bit[None]])

    near = tuple(x_move.ids)
    outs = self_forward(lims, near, x_move.parts, norm_gains, own1, got1, line)
    if exchange:
        outs = arrive([c_move, m_move], outs)
        own2, got2 = c_move.x, cube.partner(c_move.x, cube.core, 1)
        m_move.send()
        arrive([m_move])
    q1, k1, v1, o1, lse1 = outs
    h1, q2, k2, v2, o2, lse2 = cross_forward(
        lims, near, m_move.parts, dec_in, o1, own1, got1, norm_gains, own2, got2
    )
    flat = (tokens, width)
    h1 = h1.reshape(flat)
    o1 = o1.reshape(flat)
    o2 = o2.reshape(flat)
    layer_out, gh2, gain_third, dw, dkeep, dsend = feed_forward(
        lims, h1, o2, own2, got2, norm_gains, cotangent.reshape(flat), w0, w1, wd, cube.count // 2
    )
    gate_shard = lax.psum_scatter(dw, ("dp", "seq"), scatter_dimension=0, tiled=True)
    if exchange:
        downs = Sum(cube, [in_rows(dkeep)], [in_rows(dsend)], [cube.core, cube.z, cube.xy])
        downs.send()
    outs = cross_backward(lims, near, m_move.parts, gh2, h1, o1, o2, own2, got2, norm_gains, q2, k2, v2, lse2)
    gh1, gain_second, mkeep, msend, ckeep, csend, skeep, ssend = outs
    if exchange:
        (gh1, msend, ckeep, csend, skeep, ssend) = land([downs], (gh1, msend, ckeep, csend, skeep, ssend))
    mem = Sum(cube, [in_rows(mkeep)], [in_rows(msend)], near_sums)
    mem.send()
    if exchange:
        others = Sum(
            cube,
            [in_rows(ckeep), in_rows(skeep)],
            [in_rows(csend), in_rows(ssend)],
            [cube.core, cube.x, cube.y, cube.z],
        )
        others.send()
        downs.take()
        downs.send()
        (others.got, mem.got) = after(downs.sends, (others.got, mem.got))
        (gh1,) = arrive([others, mem], (gh1,))
        gh1 = after((others.sends, mem.sends), gh1)
        others.send()
    else:
        arrive([mem])
    mem.send()
    outs = self_backward(lims, near, x_move.parts, gh1, own1, got1, norm_gains, line, q1, k1, v1, lse1)
    xkeep, xsend, table, keep, send = outs
    if exchange:
        (xsend, send) = land([others, downs, mem], (xsend, send))
    first = Sum(cube, [in_rows(xkeep)], [in_rows(xsend)], near_sums)
    if exchange:
        own = Sum(cube, [in_rows(keep)], [in_rows(send)], [cube.core, cube.xy, cube.z])
        own.send()
        first.send()
        others.take()
        others.send()
        downs.take()
        downs.send()
        mem.take()
        (own.got, first.got) = after((others.sends, downs.sends), (own.got, first.got))
        own.take()
        own.send()
        first.got = after(own.sends, first.got)
        first.take()
        (others.got, downs.got) = after((own.sends, first.sends), (others.got, downs.got))
        others.take()
        others.send()
        downs.take()
        (own.got, gate_shard, first.sends) = after(others.sends, (own.got, gate_shard, first.sends))
        (gate_shard, first.sends) = land([own], (gate_shard, first.sends))
        own.take()
        own.send()
        first.send()
        others.got = after(own.sends, others.got)
        others.take()
        own.take()
        first.take()
        tiles = unit // 8
        pieces = others.x[0]
        *cross_shard, out1 = [pieces[tiles * m : tiles * (m + 1)].reshape(unit, width) for m in range(5)]
        down_shard = downs.x[0].reshape(-1, width)
        self_shard = own.x[0].reshape(3, unit, width)
        self_shard = jnp.concatenate([self_shard, out1[None]])
        cross_shard = jnp.stack(cross_shard)
    else:
        first.send()
        arrive([mem, first])
        while first.left():
            first.send()
            arrive([first])
        self_grad = jnp.concatenate([from_halves(keep, send), from_halves(skeep[:, None], ssend[:, None])])
        self_shard = lax.psum_scatter(self_grad, ("dp", "seq"), scatter_dimension=1, tiled=True).astype(F32)
        cross_grad = from_halves(ckeep, csend)
        cross_shard = lax.psum_scatter(cross_grad, ("dp", "seq"), scatter_dimension=1, tiled=True).astype(F32)
        down_grad = from_halves(dkeep[:, None], dsend[:, None])[0]
        down_shard = lax.psum_scatter(down_grad, ("dp", "seq"), scatter_dimension=0, tiled=True).astype(F32)
    while mem.left():
        mem.send()
        arrive([mem])
    mem_grad = mem.x.reshape(slots, -1, width)
    gate_shard = gate_shard.astype(F32).reshape(-1, ffn_in.shape[2] // TILE, 2, TILE)
    gate_shard = gate_shard.transpose(2, 0, 1, 3).reshape(ffn_in.shape)
    dv, gain_first = normed_back(dec_in.astype(F32).reshape(flat), norm_gains[0:1], first.x.reshape(flat))
    dec_grad = (gh1 + dv).reshape(dec_in.shape)
    table_part = jnp.einsum("hm,bm->bh", table.reshape(H, positions), hot, precision=lax.Precision.HIGHEST)

    self_square = self_shard * self_shard
    cross_square = cross_shard * cross_shard
    gate_square = gate_shard * gate_shard
    down_square = down_shard * down_shard
    hidden = ffn_in.shape[2]
    def summed(terms):
        packed = jnp.concatenate([t.reshape(-1, 128) for t in terms])
        packed = cube.total(packed, [cube.core, cube.xy, cube.z] if exchange else cube.bits)
        sums = []
        at = 0
        for t in terms:
            count = t.size // 128
            sums.append(packed[at : at + count].reshape(t.shape))
            at += count
        return sums

    gain_first, gain_second, gain_third, table_grad, self_cols, cross_cols, gate_cols, down_cols = summed(
        [
            gain_first,
            gain_second,
            gain_third,
            table_part,
            jnp.sum(self_square, axis=1) / width,
            jnp.sum(cross_square, axis=1) / width,
            jnp.sum(gate_square, axis=1) / width,
            jnp.sum(down_square, axis=0) / hidden,
        ]
    )
    gains_grad = jnp.concatenate([gain_first, gain_second, gain_third])
    self_row_means = jnp.mean(self_square, axis=2)
    cross_row_means = jnp.mean(cross_square, axis=2)
    shard_rows = self_shard.shape[1]
    column_start = lax.axis_index(("dp", "seq")) * shard_rows
    self_col_piece = lax.dynamic_slice_in_dim(self_cols[3], column_start, shard_rows, 0)
    cross_col_piece = lax.dynamic_slice_in_dim(cross_cols[3], column_start, shard_rows, 0)
    out_proj_stats = jnp.stack(
        [
            jnp.stack([self_row_means[3], self_col_piece]),
            jnp.stack([cross_row_means[3], cross_col_piece]),
        ]
    )
    return (
        layer_out.reshape(dec_in.shape),
        dec_grad,
        mem_grad,
        self_shard,
        cross_shard,
        gate_shard,
        down_shard,
        gains_grad,
        table_grad,
        self_row_means[:3],
        self_cols[:3],
        cross_row_means[:3],
        cross_cols[:3],
        jnp.mean(gate_square, axis=2),
        gate_cols,
        jnp.mean(down_square, axis=1),
        down_cols,
        out_proj_stats,
    )


def solution(mesh):
    in_specs = (
        P("dp", "seq", None),
        P("dp", "seq", None),
        P("dp", "seq", None),
        P("dp"),
        P("dp", "seq"),
        P(),
        P(None, ("dp", "seq"), None),
        P(None, ("dp", "seq"), None),
        P(None, ("dp", "seq"), None),
        P(("dp", "seq"), None),
        P(),
        P(),
    )
    out_specs = (
        P("dp", "seq", None),
        P("dp", "seq", None),
        P("dp", "seq", None),
        P(None, ("dp", "seq"), None),
        P(None, ("dp", "seq"), None),
        P(None, ("dp", "seq"), None),
        P(("dp", "seq"), None),
        P(),
        P(),
        P(None, ("dp", "seq")),
        P(),
        P(None, ("dp", "seq")),
        P(),
        P(None, ("dp", "seq")),
        P(),
        P(("dp", "seq")),
        P(),
        P(None, None, ("dp", "seq")),
    )
    return jax.shard_map(
        functools.partial(per_device, mesh),
        mesh=mesh,
        in_specs=in_specs,
        out_specs=out_specs,
        check_vma=False,
    )
```

```python
import functools

import jax
import jax.numpy as jnp
from jax import lax
from jax.experimental import pallas as pl
from jax.experimental.pallas import tpu as pltpu
from jax.sharding import PartitionSpec as P

H = 12
DK = 64
PAIR = 2 * DK
WIDE = 4 * DK
TILE = 512
UNIT = 24
TAIL = 8
EPS = 1e-06
MASKED = -1000000000.0
BF = jnp.bfloat16
F32 = jnp.float32
BUDGET = 60 * 1024 * 1024
COST = pl.CostEstimate(flops=1000, bytes_accessed=1000, transcendentals=0)


def dot_nn(a, b):
    return lax.dot_general(a, b, (((1,), (0,)), ((), ())), preferred_element_type=F32)


def dot_nt(a, b):
    return lax.dot_general(a, b, (((1,), (1,)), ((), ())), preferred_element_type=F32)


def dot_tn(a, b):
    return lax.dot_general(a, b, (((0,), (0,)), ((), ())), preferred_element_type=F32)


def inverse_rms(v):
    return lax.rsqrt(jnp.mean(v * v, axis=-1, keepdims=True) + EPS)


def normed(v, gain):
    return (v * inverse_rms(v) * gain).astype(BF)


def normed_back(v, gain, c):
    r = inverse_rms(v)
    scaled = c * gain
    inner = jnp.mean(v * scaled, axis=-1, keepdims=True)
    dv = r * scaled - v * (r * r * r * inner)
    dgain = jnp.sum(c * v * r, axis=0, keepdims=True)
    return dv, dgain


def shear(rows, sign):
    keys = rows.shape[1]
    r = lax.broadcasted_iota(jnp.int32, (8, 1), 0)
    for bit in (1, 2, 4):
        turned = pltpu.roll(rows, bit if sign > 0 else keys - bit, 1)
        rows = jnp.where((r & bit) != 0, turned, rows)
    return rows


def build_bias(line, off, out_ref):
    count, keys = out_ref.shape
    base = shear(pltpu.roll(jnp.broadcast_to(line, (8, keys)), off + 1, 1), 1)
    for g in range(count // 8):
        out_ref[8 * g : 8 * g + 8, :] = pltpu.roll(base, (8 * g) % keys, 1) if g else base


def sum_diagonals(sum_ref, off):
    count, keys = sum_ref.shape
    total = sum_ref[0:8, :]
    for g in range(1, count // 8):
        total = total + pltpu.roll(sum_ref[8 * g : 8 * g + 8, :], (keys - 8 * g) % keys, 1)
    total = jnp.sum(shear(total, -1), axis=0, keepdims=True)
    return pltpu.roll(jnp.broadcast_to(total, (8, keys)), keys - 1 - off, 1)[0:1]


def low_lanes():
    return lax.broadcasted_iota(jnp.int32, (1, PAIR), 1) < DK


def head_part(x, head):
    low = low_lanes()
    mine = low if head % 2 == 0 else jnp.logical_not(low)
    return jnp.where(mine, x, jnp.zeros_like(x))


def row_limit(start, rows, count, causal):
    if not causal:
        return count
    seen = start + 1 + lax.broadcasted_iota(jnp.int32, (rows, 1), 0)
    return jnp.minimum(seen, count)


def attend(q_ref, k_ref, v_ref, o_ref, lse_ref, bias_ref, s_ref, p_ref, off, counts):
    slots, rows, _ = q_ref.shape
    keys = k_ref.shape[1]
    causal = bias_ref is not None
    cols = lax.broadcasted_iota(jnp.int32, (1, keys), 1)
    low = low_lanes()
    work = [(s, h) for s in range(slots) for h in range(WIDE // DK)]

    def lanes(h):
        return slice((h // 2) * PAIR, (h // 2) * PAIR + PAIR)

    def scores(n):
        s, h = work[n]
        s_ref[n % 2] = dot_nt(head_part(q_ref[s, :, lanes(h)], h), k_ref[s, :, lanes(h)])

    scores(0)
    kept = None
    for n, (s, h) in enumerate(work):
        if n + 1 < len(work):
            scores(n + 1)
        sc = s_ref[n % 2]
        if causal:
            sc = sc + bias_ref[h]
        sc = jnp.where(cols < row_limit(off, rows, counts[s], causal), sc, MASKED)
        top = jnp.max(sc, axis=1, keepdims=True)
        e = jnp.exp(sc - top)
        total = jnp.sum(e, axis=1, keepdims=True)
        p_ref[n % 2] = (e * (1.0 / total)).astype(BF)
        out = dot_nn(p_ref[n % 2], v_ref[s, :, lanes(h)])
        log_total = jnp.broadcast_to(top + jnp.log(total), (rows, PAIR))
        if h % 2 == 0:
            kept = (out, log_total)
        else:
            o_ref[s, :, lanes(h)] = jnp.where(low, kept[0], out).astype(BF)
            lse_ref[s, h // 2] = jnp.where(low, kept[1], log_total)


def attend_back(
    q_ref, k_ref, v_ref, g_ref, lse_ref, dq_ref, dk_ref, dv_ref,
    bias_ref, sum_ref, s_ref, dp_ref, p_ref, ds_ref, off, counts,
):
    slots, rows, _ = q_ref.shape
    keys = k_ref.shape[1]
    causal = bias_ref is not None
    cols = lax.broadcasted_iota(jnp.int32, (1, keys), 1)
    low = low_lanes()
    work = [(s, h) for s in range(slots) for h in range(WIDE // DK)]

    def lanes(h):
        return slice((h // 2) * PAIR, (h // 2) * PAIR + PAIR)

    def products(n):
        s, h = work[n]
        s_ref[n % 2] = dot_nt(head_part(q_ref[s, :, lanes(h)], h), k_ref[s, :, lanes(h)])
        dp_ref[n % 2] = dot_nt(head_part(g_ref[s, :, lanes(h)], h), v_ref[s, :, lanes(h)])

    products(0)
    kept = None
    for n, (s, h) in enumerate(work):
        if n + 1 < len(work):
            products(n + 1)
        sc = s_ref[n % 2]
        if causal:
            sc = sc + bias_ref[h]
        sc = jnp.where(cols < row_limit(off, rows, counts[s], causal), sc, MASKED)
        at = (h % 2) * DK
        p = jnp.exp(sc - lse_ref[s, h // 2, :, at : at + 1])
        dp = dp_ref[n % 2]
        inner = jnp.sum(p * dp, axis=1, keepdims=True)
        ds = (p * (dp - inner)).astype(BF)
        p_ref[n % 2] = p.astype(BF)
        ds_ref[n % 2] = ds
        if causal:
            if s == 0:
                sum_ref[h] = ds.astype(F32)
            else:
                sum_ref[h] += ds.astype(F32)
        ds = ds_ref[n % 2]
        dq = dot_nn(ds, k_ref[s, :, lanes(h)])
        dk = dot_tn(head_part(q_ref[s, :, lanes(h)], h), ds)
        dv = dot_tn(head_part(g_ref[s, :, lanes(h)], h), p_ref[n % 2])
        if h % 2 == 0:
            kept = (dq, dk, dv)
        else:
            dq_ref[s * rows : (s + 1) * rows, lanes(h)] = jnp.where(low, kept[0], dq).astype(BF)
            dk_ref[s * keys : (s + 1) * keys, lanes(h)] = (kept[1] + dk).astype(BF).T
            dv_ref[s * keys : (s + 1) * keys, lanes(h)] = (kept[2] + dv).astype(BF).T


def assemble(own_ref, got_ref, bit):
    own, got = own_ref[...].astype(F32), got_ref[...].astype(F32)
    both = jnp.stack([jnp.where(bit == 0, own, got), jnp.where(bit == 0, got, own)], axis=1)
    return both.reshape(-1, both.shape[-1]).astype(BF)


def row_counts(ms):
    counts = []
    for s in range(ms[0].shape[0]):
        count = sum(m_ref[s, -TAIL:, 0:PAIR].astype(F32)[0:1, 0:1] for m_ref in ms)
        counts.append(count.astype(jnp.int32))
    return counts


def part_blocks(x, pairs, bit, keep_ref, send_ref):
    x = x.reshape(pairs, 2, -1, x.shape[-1])
    first, second = x[:, 0], x[:, 1]
    keep_ref[...] = jnp.where(bit == 0, first, second).astype(BF)
    send_ref[...] = jnp.where(bit == 0, second, first).astype(BF)


def whole(shape):
    return pl.BlockSpec(shape, lambda b, *_: (0,) * len(shape), pipeline_mode=pl.Buffered(1))


def result(shape):
    return pl.BlockSpec(shape, lambda b, *_: (0,) * len(shape))


def wide(shape):
    return pl.BlockSpec(shape[:-1] + (WIDE,), lambda b, *_: (0,) * (len(shape) - 1) + (b,))


def halves(index, shape, lanes=WIDE):
    pairs, _, rows, width = shape
    if lanes == width:
        spec = pl.BlockSpec(
            (pairs, None, rows, width), lambda b, *_: (0, index, 0, 0), pipeline_mode=pl.Buffered(1)
        )
    else:
        spec = pl.BlockSpec((pairs, None, rows, lanes), lambda b, *_: (0, index, 0, b))
    return [spec, spec]


def params():
    return pltpu.CompilerParams(dimension_semantics=("arbitrary",), vmem_limit_bytes=BUDGET)


def self_forward_body(near, lims, *refs):
    xs = refs[: len(near)]
    (
        gain_ref, wq_own, wq_got, wk_own, wk_got, wv_own, wv_got, line_ref,
        q_ref, k_ref, v_ref, o_ref, lse_ref, a_ref, bias_ref, s_ref, p_ref,
    ) = refs[len(near) :]
    slots, rows, width = xs[0].shape
    keys = k_ref.shape[1]
    off, me, bit = lims[0], lims[1 + slots], lims[2 + slots]

    @pl.when(pl.program_id(0) == 0)
    def _():
        for r, x_ref in zip(near, xs, strict=True):
            for s in range(slots):
                at = pl.multiple_of(s * keys + (me ^ r) * rows, 128)
                a_ref[pl.ds(at, rows), :] = normed(x_ref[s].astype(F32), gain_ref[0:1, :])

    wq, wk, wv = assemble(wq_own, wq_got, bit), assemble(wk_own, wk_got, bit), assemble(wv_own, wv_got, bit)
    for s in range(slots):
        mine = pl.ds(pl.multiple_of(s * keys + off, 128), rows)
        q_ref[s] = dot_nn(a_ref[mine, :], wq).astype(BF)
        k_ref[s] = dot_nn(a_ref[s * keys : (s + 1) * keys, :], wk).astype(BF)
        v_ref[s] = dot_nn(a_ref[s * keys : (s + 1) * keys, :], wv).astype(BF)
    for h in range(WIDE // DK):
        build_bias(line_ref[0, h : h + 1, :], off, bias_ref.at[h])
    counts = [lims[1 + s] for s in range(slots)]
    attend(q_ref, k_ref, v_ref, o_ref, lse_ref, bias_ref, s_ref, p_ref, off, counts)


def self_forward(lims, near, xs, gains, own, got, line):
    slots, rows, width = xs[0].shape
    keys = rows * len(near)
    blocks = width // WIDE
    return pl.pallas_call(
        functools.partial(self_forward_body, near),
        grid_spec=pltpu.PrefetchScalarGridSpec(
            num_scalar_prefetch=1,
            grid=(blocks,),
            in_specs=[whole((slots, rows, width))] * len(near)
            + [whole(gains.shape)]
            + halves(0, own.shape)
            + halves(1, own.shape)
            + halves(2, own.shape)
            + [pl.BlockSpec((1, WIDE // DK, keys), lambda b, *_: (b, 0, 0))],
            out_specs=[
                wide((slots, rows, width)),
                wide((slots, keys, width)),
                wide((slots, keys, width)),
                wide((slots, rows, width)),
                pl.BlockSpec((slots, 2, rows, PAIR), lambda b, *_: (0, b, 0, 0)),
            ],
            scratch_shapes=[
                pltpu.VMEM((slots * keys, width), BF),
                pltpu.VMEM((WIDE // DK, rows, keys), F32),
                pltpu.VMEM((2, rows, keys), F32),
                pltpu.VMEM((2, rows, keys), BF),
            ],
        ),
        out_shape=[
            jax.ShapeDtypeStruct((slots, rows, width), BF),
            jax.ShapeDtypeStruct((slots, keys, width), BF),
            jax.ShapeDtypeStruct((slots, keys, width), BF),
            jax.ShapeDtypeStruct((slots, rows, width), BF),
            jax.ShapeDtypeStruct((slots, H // 2, rows, PAIR), F32),
        ],
        compiler_params=params(),
        cost_estimate=COST,
        name="self_forward",
    )(lims, *xs, gains, own, got, own, got, own, got, line)


def cross_forward_body(near, lims, *refs):
    ms = refs[: len(near)]
    (
        x_ref, o1_ref, wo_own, wo_got, gain_ref, wq_own, wq_got, wk_own, wk_got, wv_own, wv_got,
        h_ref, q_ref, k_ref, v_ref, o_ref, lse_ref, a_ref, mem_ref, s_ref, p_ref,
    ) = refs[len(near) :]
    slots, part, width = ms[0].shape
    part -= TAIL
    rows, keys = q_ref.shape[1], k_ref.shape[1]
    me, bit = lims[1 + slots], lims[2 + slots]

    @pl.when(pl.program_id(0) == 0)
    def _():
        wo = assemble(wo_own, wo_got, bit)
        for s in range(slots):
            h = x_ref[s].astype(F32) + dot_nn(o1_ref[s], wo)
            h_ref[s] = h
            a_ref[s * rows : (s + 1) * rows, :] = normed(h, gain_ref[1:2, :])
        for r, m_ref in zip(near, ms, strict=True):
            for s in range(slots):
                mem_ref[s, pl.ds(pl.multiple_of((me ^ r) * part, part), part), :] = m_ref[s, :part]

    wq, wk, wv = assemble(wq_own, wq_got, bit), assemble(wk_own, wk_got, bit), assemble(wv_own, wv_got, bit)
    for s in range(slots):
        q_ref[s] = dot_nn(a_ref[s * rows : (s + 1) * rows, :], wq).astype(BF)
        k_ref[s] = dot_nn(mem_ref[s], wk).astype(BF)
        v_ref[s] = dot_nn(mem_ref[s], wv).astype(BF)
    counts = row_counts(ms)
    attend(q_ref, k_ref, v_ref, o_ref, lse_ref, None, s_ref, p_ref, 0, counts)


def cross_forward(lims, near, ms, x, o1, own1, got1, gains, own, got):
    slots, part, width = ms[0].shape
    part -= TAIL
    keys = part * len(near)
    rows = x.shape[1]
    blocks = width // WIDE
    return pl.pallas_call(
        functools.partial(cross_forward_body, near),
        grid_spec=pltpu.PrefetchScalarGridSpec(
            num_scalar_prefetch=1,
            grid=(blocks,),
            in_specs=[whole((slots, part + TAIL, width))] * len(near)
            + [whole((slots, rows, width)), whole((slots, rows, width))]
            + halves(3, own1.shape, width)
            + [whole(gains.shape)]
            + halves(0, own.shape)
            + halves(1, own.shape)
            + halves(2, own.shape),
            out_specs=[
                result((slots, rows, width)),
                wide((slots, rows, width)),
                wide((slots, keys, width)),
                wide((slots, keys, width)),
                wide((slots, rows, width)),
                pl.BlockSpec((slots, 2, rows, PAIR), lambda b, *_: (0, b, 0, 0)),
            ],
            scratch_shapes=[
                pltpu.VMEM((slots * rows, width), BF),
                pltpu.VMEM((slots, keys, width), BF),
                pltpu.VMEM((2, rows, keys), F32),
                pltpu.VMEM((2, rows, keys), BF),
            ],
        ),
        out_shape=[
            jax.ShapeDtypeStruct((slots, rows, width), F32),
            jax.ShapeDtypeStruct((slots, rows, width), BF),
            jax.ShapeDtypeStruct((slots, keys, width), BF),
            jax.ShapeDtypeStruct((slots, keys, width), BF),
            jax.ShapeDtypeStruct((slots, rows, width), BF),
            jax.ShapeDtypeStruct((slots, H // 2, rows, PAIR), F32),
        ],
        compiler_params=params(),
        cost_estimate=COST,
        name="cross_forward",
    )(lims, *ms, x, o1, own1, got1, gains, own, got, own, got, own, got)


def down_rows(x):
    width = x.shape[-1]
    lanes = width // 128
    x = x.reshape(-1, 8, 8, width)
    count = 8 * lanes
    across = count // (UNIT // 8)
    tiles = [x[:, q // lanes, :, (q % lanes) * 128 : (q % lanes + 1) * 128] for q in range(count)]
    rows = [jnp.concatenate(tiles[i * across : (i + 1) * across], axis=-1) for i in range(UNIT // 8)]
    x = jnp.stack(rows, axis=1)
    return x.reshape(-1, across * 128)


def down_back(x, width):
    lanes = width // 128
    x = x.reshape(-1, UNIT // 8, 8, x.shape[-1] // 128, 128).transpose(0, 1, 3, 2, 4)
    x = x.reshape(-1, 8, lanes, 8, 128).transpose(0, 1, 3, 2, 4)
    return x.reshape(-1, width)


def gradient_copies(wide_ref, down_ref, dw_ref, sems):
    steps, _, columns = wide_ref.shape
    rows, across = down_ref.shape[1:]
    return [
        (
            pltpu.make_async_copy(wide_ref.at[n], dw_ref.at[:, pl.ds(n * columns, columns)], sems.at[2 * n]),
            pltpu.make_async_copy(
                down_ref.at[n],
                dw_ref.at[pl.ds(n * rows, rows), pl.ds(steps * columns, across)],
                sems.at[2 * n + 1],
            ),
        )
        for n in range(steps)
    ]


def from_columns(ref):
    columns = []
    for n in range(ref.shape[2]):
        columns.append(ref[:, :, n].astype(F32).reshape(-1, 128))
    return jnp.concatenate(columns, axis=-1).astype(BF)


def from_rows(ref, width):
    lanes = width // 128
    across = ref.shape[2]
    count = ref.shape[1] * across
    tiles = [ref[:, q // across, q % across].astype(F32) for q in range(count)]
    rows = [jnp.concatenate(tiles[n * lanes : (n + 1) * lanes], axis=-1) for n in range(count // lanes)]
    return jnp.stack(rows, axis=1).reshape(-1, width).astype(BF)


def feed_forward_body(
    lims, h1_ref, o2_ref, wo_own, wo_got, gain_ref, g_ref, w0_tiles, w1_tiles, wd_tiles,
    out_ref, gh_ref, dgain_ref, dw_ref, h_ref, a_ref, at_ref, acc_ref, da_ref, wide_ref, down_ref, sems,
):
    step = pl.program_id(0)
    bit = lims[lims.shape[0] - 1]

    @pl.when(step == 0)
    def _():
        h = h1_ref[...] + dot_nn(o2_ref[...], assemble(wo_own, wo_got, bit))
        h_ref[...] = h
        a = normed(h, gain_ref[2:3, :])
        a_ref[...] = a
        at_ref[...] = a.T
        acc_ref[...] = h
        da_ref[...] = jnp.zeros_like(da_ref)

    a = a_ref[...]
    e = g_ref[...]
    w0, w1, wd = from_columns(w0_tiles), from_columns(w1_tiles), from_rows(wd_tiles, a.shape[1])
    gate = dot_nn(a, w0)
    up = dot_nn(a, w1)
    c = dot_nt(e, wd)
    root = 0.7978845608028654
    square = gate * gate
    th = jnp.tanh(root * gate * (1.0 + 0.044715 * square))
    half = 0.5 * (1.0 + th)
    act = gate * half
    slope = half + 0.5 * gate * (1.0 - th * th) * (root * (1.0 + 3.0 * 0.044715 * square))
    hidden = (act * up).astype(BF)
    dgate = (c * up * slope).astype(BF)
    dup = (c * act).astype(BF)
    acc_ref[...] += dot_nn(hidden, wd)
    tile = dgate.shape[1]
    wide_ref[step, :, :tile] = dot_nn(at_ref[...], dgate).astype(BF)
    wide_ref[step, :, tile:] = dot_nn(at_ref[...], dup).astype(BF)
    down_ref[step] = down_rows(dot_tn(hidden, e)).astype(BF)
    moves = gradient_copies(wide_ref, down_ref, dw_ref, sems)
    for n, pair in enumerate(moves):

        @pl.when(step == n)
        def _():
            for move in pair:
                move.start()

    da_ref[...] += dot_nt(dgate, w0) + dot_nt(dup, w1)

    @pl.when(step == pl.num_programs(0) - 1)
    def _():
        out_ref[...] = acc_ref[...].astype(BF)
        dv, dgain = normed_back(h_ref[...], gain_ref[2:3, :], da_ref[...])
        gh_ref[...] = e.astype(F32) + dv
        dgain_ref[...] = dgain
        for pair in moves:
            for move in pair:
                move.wait()


def feed_forward(lims, h1, o2, own, got, gains, cot, tiles):
    tokens, width = h1.shape
    devices, parts, across, _, _ = tiles.shape
    hidden = across * 128
    tile = TILE
    steps = hidden // tile
    assert hidden // 64 == width // UNIT == devices
    return pl.pallas_call(
        feed_forward_body,
        grid_spec=pltpu.PrefetchScalarGridSpec(
            num_scalar_prefetch=1,
            grid=(hidden // tile,),
            in_specs=[whole((tokens, width)), whole((tokens, width))]
            + halves(3, own.shape, width)
            + [
                whole(gains.shape),
                whole((tokens, width)),
                pl.BlockSpec((devices, parts // 3, tile // 128, 8, 128), lambda b, *_: (0, 0, b, 0, 0)),
                pl.BlockSpec((devices, parts // 3, tile // 128, 8, 128), lambda b, *_: (0, 1, b, 0, 0)),
                pl.BlockSpec((devices // steps, parts // 3, across, 8, 128), lambda b, *_: (b, 2, 0, 0, 0)),
            ],
            out_specs=[
                result((tokens, width)),
                result((tokens, width)),
                result((1, width)),
                pl.BlockSpec(memory_space=pl.ANY),
            ],
            scratch_shapes=[
                pltpu.VMEM((tokens, width), F32),
                pltpu.VMEM((tokens, width), BF),
                pltpu.VMEM((width, tokens), BF),
                pltpu.VMEM((tokens, width), F32),
                pltpu.VMEM((tokens, width), F32),
                pltpu.VMEM((steps, width, 2 * tile), BF),
                pltpu.VMEM((steps, width // steps, hidden), BF),
                pltpu.SemaphoreType.DMA((2 * steps,)),
            ],
        ),
        out_shape=[
            jax.ShapeDtypeStruct((tokens, width), BF),
            jax.ShapeDtypeStruct((tokens, width), F32),
            jax.ShapeDtypeStruct((1, width), F32),
            jax.ShapeDtypeStruct((width, 3 * hidden), BF),
        ],
        compiler_params=params(),
        cost_estimate=COST,
        name="feed_forward",
    )(lims, h1, o2, own, got, gains, cot, tiles, tiles, tiles)


def cross_backward_body(near, lims, *refs):
    ms = refs[: len(near)]
    (
        gh2_ref, h1_ref, o1_ref, o2_ref, wo_own, wo_got, gain_ref, q_ref, k_ref, v_ref, lse_ref,
        wq_own, wq_got, wk_own, wk_got, wv_own, wv_got,
        gh_ref, dgain_ref, mkeep_ref, msend_ref, keep_ref, send_ref, skeep_ref, ssend_ref,
        g_ref, e_ref, at_ref, memt_ref, da_ref, dm_ref, dq_ref, dk_ref, dv_ref, s_ref, dp_ref, p_ref, ds_ref,
    ) = refs[len(near) :]
    step = pl.program_id(0)
    slots, part, width = ms[0].shape
    part -= TAIL
    rows, keys = q_ref.shape[1], k_ref.shape[1]
    me, bit = lims[1 + slots], lims[2 + slots]
    pairs = keep_ref.shape[0]

    @pl.when(step == 0)
    def _():
        e = gh2_ref[...].astype(BF)
        back = dot_nt(e, assemble(wo_own, wo_got, bit)).astype(BF)
        for b in range(width // WIDE):
            e_ref[b] = e[:, b * WIDE : (b + 1) * WIDE]
            for s in range(slots):
                g_ref[b, s] = back[s * rows : (s + 1) * rows, b * WIDE : (b + 1) * WIDE]
        at_ref[...] = normed(h1_ref[...], gain_ref[1:2, :]).T
        for r, m_ref in zip(near, ms, strict=True):
            for s in range(slots):
                at = pl.multiple_of(s * keys + (me ^ r) * part, part)
                memt_ref[pl.ds(at, part), :] = m_ref[s, :part]
        da_ref[...] = jnp.zeros_like(da_ref)
        dm_ref[...] = jnp.zeros_like(dm_ref)

    counts = row_counts(ms)
    attend_back(
        q_ref, k_ref, v_ref, g_ref.at[step], lse_ref, dq_ref, dk_ref, dv_ref,
        None, None, s_ref, dp_ref, p_ref, ds_ref, 0, counts,
    )
    for m, grad in enumerate(
        (
            dot_nn(at_ref[...], dq_ref[...]),
            dot_tn(memt_ref[...], dk_ref[...]),
            dot_tn(memt_ref[...], dv_ref[...]),
            dot_tn(o2_ref[...], e_ref[step]),
        )
    ):
        part_blocks(grad, pairs, bit, keep_ref.at[:, m], send_ref.at[:, m])
    da_ref[...] += dot_nt(dq_ref[...], assemble(wq_own, wq_got, bit))
    dm_ref[...] += dot_nt(dk_ref[...], assemble(wk_own, wk_got, bit)) + dot_nt(
        dv_ref[...], assemble(wv_own, wv_got, bit)
    )

    @pl.when(step == pl.num_programs(0) - 1)
    def _():
        dv, dgain = normed_back(h1_ref[...], gain_ref[1:2, :], da_ref[...])
        gh = gh2_ref[...] + dv
        gh_ref[...] = gh
        dgain_ref[...] = dgain
        part_blocks(dot_tn(o1_ref[...], gh.astype(BF)), pairs, bit, skeep_ref, ssend_ref)
        for s in range(slots):
            for n in range(len(near) // 2):
                keep = pl.multiple_of(s * keys + (2 * n + bit) * part, part)
                send = pl.multiple_of(s * keys + (2 * n + 1 - bit) * part, part)
                mkeep_ref[s * (len(near) // 2) + n] = dm_ref[pl.ds(keep, part), :].astype(BF)
                msend_ref[s * (len(near) // 2) + n] = dm_ref[pl.ds(send, part), :].astype(BF)


def cross_backward(lims, near, ms, gh2, h1, o1, o2, own, got, gains, q, k, v, lse):
    slots, part, width = ms[0].shape
    part -= TAIL
    keys = part * len(near)
    rows = q.shape[1]
    tokens = slots * rows
    blocks = width // WIDE
    pairs, count, unit, _ = own.shape
    half = jax.ShapeDtypeStruct((slots * len(near) // 2, part, width), BF)
    grads = pl.BlockSpec((pairs, count, unit, WIDE), lambda b, *_: (0, 0, 0, b))
    return pl.pallas_call(
        functools.partial(cross_backward_body, near),
        grid_spec=pltpu.PrefetchScalarGridSpec(
            num_scalar_prefetch=1,
            grid=(blocks,),
            in_specs=[whole((slots, part + TAIL, width))] * len(near)
            + [whole((tokens, width))] * 4
            + halves(3, own.shape, width)
            + [
                whole(gains.shape),
                wide((slots, rows, width)),
                wide((slots, keys, width)),
                wide((slots, keys, width)),
                pl.BlockSpec((slots, 2, rows, PAIR), lambda b, *_: (0, b, 0, 0)),
            ]
            + halves(0, own.shape)
            + halves(1, own.shape)
            + halves(2, own.shape),
            out_specs=[
                result((tokens, width)),
                result((1, width)),
                result(half.shape),
                result(half.shape),
                grads,
                grads,
                result((pairs, unit, width)),
                result((pairs, unit, width)),
            ],
            scratch_shapes=[
                pltpu.VMEM((blocks, slots, rows, WIDE), BF),
                pltpu.VMEM((blocks, tokens, WIDE), BF),
                pltpu.VMEM((width, tokens), BF),
                pltpu.VMEM((slots * keys, width), BF),
                pltpu.VMEM((tokens, width), F32),
                pltpu.VMEM((slots * keys, width), F32),
                pltpu.VMEM((tokens, WIDE), BF),
                pltpu.VMEM((slots * keys, WIDE), BF),
                pltpu.VMEM((slots * keys, WIDE), BF),
                pltpu.VMEM((2, rows, keys), F32),
                pltpu.VMEM((2, rows, keys), F32),
                pltpu.VMEM((2, rows, keys), BF),
                pltpu.VMEM((2, rows, keys), BF),
            ],
        ),
        out_shape=[
            jax.ShapeDtypeStruct((tokens, width), F32),
            jax.ShapeDtypeStruct((1, width), F32),
            half,
            half,
            jax.ShapeDtypeStruct(own.shape, BF),
            jax.ShapeDtypeStruct(own.shape, BF),
            jax.ShapeDtypeStruct((pairs, unit, width), BF),
            jax.ShapeDtypeStruct((pairs, unit, width), BF),
        ],
        compiler_params=params(),
        cost_estimate=COST,
        name="cross_backward",
    )(lims, *ms, gh2, h1, o1, o2, own, got, gains, q, k, v, lse, own, got, own, got, own, got)


def self_backward_body(near, lims, *refs):
    xs = refs[: len(near)]
    (
        gh1_ref, wo_own, wo_got, gain_ref, line_ref, q_ref, k_ref, v_ref, lse_ref,
        wq_own, wq_got, wk_own, wk_got, wv_own, wv_got,
        xkeep_ref, xsend_ref, table_ref, keep_ref, send_ref,
        g_ref, at_ref, da_ref, dq_ref, dk_ref, dv_ref, bias_ref, sum_ref, s_ref, dp_ref, p_ref, ds_ref,
    ) = refs[len(near) :]
    step = pl.program_id(0)
    slots, rows, width = xs[0].shape
    keys = k_ref.shape[1]
    off, me, bit = lims[0], lims[1 + slots], lims[2 + slots]
    pairs = keep_ref.shape[0]

    @pl.when(step == 0)
    def _():
        e = gh1_ref[...].astype(BF)
        back = dot_nt(e, assemble(wo_own, wo_got, bit)).astype(BF)
        for b in range(width // WIDE):
            for s in range(slots):
                g_ref[b, s] = back[s * rows : (s + 1) * rows, b * WIDE : (b + 1) * WIDE]
        for r, x_ref in zip(near, xs, strict=True):
            for s in range(slots):
                at = pl.multiple_of(s * keys + (me ^ r) * rows, 128)
                at_ref[:, pl.ds(at, rows)] = normed(x_ref[s].astype(F32), gain_ref[0:1, :]).T
        da_ref[...] = jnp.zeros_like(da_ref)

    for h in range(WIDE // DK):
        build_bias(line_ref[0, h : h + 1, :], off, bias_ref.at[h])
    counts = [lims[1 + s] for s in range(slots)]
    attend_back(
        q_ref, k_ref, v_ref, g_ref.at[step], lse_ref, dq_ref, dk_ref, dv_ref,
        bias_ref, sum_ref, s_ref, dp_ref, p_ref, ds_ref, off, counts,
    )
    for h in range(WIDE // DK):
        table_ref[0, h : h + 1, :] = sum_diagonals(sum_ref.at[h], off)
    wq = assemble(wq_own, wq_got, bit)
    dwq = None
    for s in range(slots):
        mine = pl.ds(pl.multiple_of(s * keys + off, 128), rows)
        dq = dq_ref[s * rows : (s + 1) * rows, :]
        part = dot_nn(at_ref[:, mine], dq)
        dwq = part if dwq is None else dwq + part
        da_ref[mine, :] += dot_nt(dq, wq)
    for m, grad in enumerate((dwq, dot_nn(at_ref[...], dk_ref[...]), dot_nn(at_ref[...], dv_ref[...]))):
        part_blocks(grad, pairs, bit, keep_ref.at[:, m], send_ref.at[:, m])
    da_ref[...] += dot_nt(dk_ref[...], assemble(wk_own, wk_got, bit)) + dot_nt(
        dv_ref[...], assemble(wv_own, wv_got, bit)
    )

    @pl.when(step == pl.num_programs(0) - 1)
    def _():
        for s in range(slots):
            for n in range(len(near) // 2):
                keep = pl.multiple_of(s * keys + (2 * n + bit) * rows, 128)
                send = pl.multiple_of(s * keys + (2 * n + 1 - bit) * rows, 128)
                xkeep_ref[s * (len(near) // 2) + n] = da_ref[pl.ds(keep, rows), :].astype(BF)
                xsend_ref[s * (len(near) // 2) + n] = da_ref[pl.ds(send, rows), :].astype(BF)


def self_backward(lims, near, xs, gh1, own, got, gains, line, q, k, v, lse):
    slots, rows, width = xs[0].shape
    keys = rows * len(near)
    tokens = slots * rows
    blocks = width // WIDE
    pairs, count, unit, _ = own.shape
    heads = WIDE // DK
    half = jax.ShapeDtypeStruct((slots * len(near) // 2, rows, width), BF)
    grads = pl.BlockSpec((pairs, count - 1, unit, WIDE), lambda b, *_: (0, 0, 0, b))
    return pl.pallas_call(
        functools.partial(self_backward_body, near),
        grid_spec=pltpu.PrefetchScalarGridSpec(
            num_scalar_prefetch=1,
            grid=(blocks,),
            in_specs=[whole((slots, rows, width))] * len(near)
            + [whole((tokens, width))]
            + halves(3, own.shape, width)
            + [
                whole(gains.shape),
                pl.BlockSpec((1, heads, keys), lambda b, *_: (b, 0, 0)),
                wide((slots, rows, width)),
                wide((slots, keys, width)),
                wide((slots, keys, width)),
                pl.BlockSpec((slots, 2, rows, PAIR), lambda b, *_: (0, b, 0, 0)),
            ]
            + halves(0, own.shape)
            + halves(1, own.shape)
            + halves(2, own.shape),
            out_specs=[
                result(half.shape),
                result(half.shape),
                pl.BlockSpec((1, heads, keys), lambda b, *_: (b, 0, 0)),
                grads,
                grads,
            ],
            scratch_shapes=[
                pltpu.VMEM((blocks, slots, rows, WIDE), BF),
                pltpu.VMEM((width, slots * keys), BF),
                pltpu.VMEM((slots * keys, width), F32),
                pltpu.VMEM((tokens, WIDE), BF),
                pltpu.VMEM((slots * keys, WIDE), BF),
                pltpu.VMEM((slots * keys, WIDE), BF),
                pltpu.VMEM((heads, rows, keys), F32),
                pltpu.VMEM((heads, rows, keys), F32),
                pltpu.VMEM((2, rows, keys), F32),
                pltpu.VMEM((2, rows, keys), F32),
                pltpu.VMEM((2, rows, keys), BF),
                pltpu.VMEM((2, rows, keys), BF),
            ],
        ),
        out_shape=[
            half,
            half,
            jax.ShapeDtypeStruct((blocks, heads, keys), F32),
            jax.ShapeDtypeStruct((pairs, count - 1, unit, width), BF),
            jax.ShapeDtypeStruct((pairs, count - 1, unit, width), BF),
        ],
        compiler_params=params(),
        cost_estimate=COST,
        name="self_backward",
    )(lims, *xs, gh1, own, got, gains, line, q, k, v, lse, own, got, own, got, own, got)


def to_tiles(w):
    m, r, c = w.shape
    return w.reshape(m, r // 8, 8, c // 128, 128).transpose(0, 1, 3, 2, 4).reshape(-1, 8, 128)


def place_body(ways, scalar_ref, *refs):
    for r in range(ways):

        @pl.when(pl.program_id(0) == r)
        def _():
            refs[ways][...] = refs[r][...]


def place_blocks(place, parts):
    ways = len(parts)
    outer, inner, tail = parts[0].shape[0], parts[0].shape[1], parts[0].shape[2:]
    rest = (0,) * len(tail)
    spec = pl.BlockSpec((outer, inner) + tail, lambda r, s: (0, 0) + rest)
    return pl.pallas_call(
        functools.partial(place_body, ways),
        grid_spec=pltpu.PrefetchScalarGridSpec(
            num_scalar_prefetch=1,
            grid=(ways,),
            in_specs=[spec] * ways,
            out_specs=pl.BlockSpec((outer, None, inner) + tail, lambda r, s: (0, s[0] ^ r, 0) + rest),
        ),
        out_shape=jax.ShapeDtypeStruct((outer, ways, inner) + tail, BF),
        compiler_params=params(),
        cost_estimate=COST,
        name="place_blocks",
    )(place.reshape(1), *parts)


def fold_body(groups, ways, last, *refs):
    refs = refs[1:]
    inputs = ways * sum(1 + terms for _, terms in groups)
    outs = refs[inputs:]
    n = 0
    for j in range(ways):
        at = 0
        for size, terms in groups:
            x = refs[n][...].astype(F32)
            for t in range(terms):
                x = x + refs[n + 1 + t][...].astype(F32)
            n += 1 + terms
            outs[j][:, :, at : at + size] = x if last else x.astype(BF)
            at += size


def fold(place, ways, inner, groups, last):
    outer, width = groups[0][0].shape[0] // (ways * inner), groups[0][0].shape[-1]
    sizes = [g[0].shape[1] for g in groups]
    total = sum(sizes)
    step = outer
    moved = sum(size * (len(g) + 1) for size, g in zip(sizes, groups, strict=True))
    while step > 1 and step * inner * ways * moved * 8 * width * 2 > 6 * 1024 * 1024:
        step //= 2

    def spec(j, size):
        return pl.BlockSpec((step, None, inner, size, 8, width), lambda g, s: (g, s[0] ^ j, 0, 0, 0, 0))

    in_specs, ins = [], []
    for j in range(ways):
        for size, terms in zip(sizes, groups, strict=True):
            in_specs += [spec(j, size)] * len(terms)
            ins += [t.reshape((outer, ways, inner) + t.shape[1:]) for t in terms]
    made = pl.pallas_call(
        functools.partial(fold_body, [(size, len(g) - 1) for size, g in zip(sizes, groups, strict=True)], ways, last),
        grid_spec=pltpu.PrefetchScalarGridSpec(
            num_scalar_prefetch=1,
            grid=(outer // step,),
            in_specs=in_specs,
            out_specs=[pl.BlockSpec((step, inner, total, 8, width), lambda g, s: (g, 0, 0, 0, 0))] * ways,
        ),
        out_shape=[jax.ShapeDtypeStruct((outer, inner, total, 8, width), F32 if last else BF)] * ways,
        compiler_params=params(),
        cost_estimate=COST,
        name="fold_blocks",
    )(place.reshape(1), *ins)
    return [x.reshape((outer * inner,) + x.shape[2:]) for x in made]


def in_halves(w):
    x = w.reshape(w.shape[0], -1, 2, UNIT, w.shape[-1]).transpose(2, 1, 0, 3, 4)
    return x[0], x[1]


def from_halves(first, second):
    x = jnp.stack([first, second], axis=1)
    return x.transpose(2, 0, 1, 3, 4).reshape(x.shape[2], -1, x.shape[-1])


def in_rows(x):
    return x.reshape(x.shape[0], -1, 8, x.shape[-1])


class Cube:
    axes = ("dp", "seq")

    def __init__(self, mesh):
        self.near = mesh.shape["seq"].bit_length() - 1
        self.count = mesh.shape["dp"] * mesh.shape["seq"]
        bits = self.count.bit_length() - 1
        assert self.count == 1 << bits
        self.core, self.y, self.x, self.xy, self.z = (0, 2), (1, 2), (2, 2), (1, 4), (3, 4)
        self.fits = self.near == 2 and bits == 5
        self.bits = [(b, 2) for b in range(bits)]
        self.near_groups = [(b, 2) for b in range(self.near)]

    def place(self, group):
        low, ways = group
        return (lax.axis_index(self.axes).astype(jnp.int32) >> low) & (ways - 1)

    def partner(self, x, group, r):
        low, _ = group
        return lax.ppermute(x, self.axes, [(i, i ^ (r << low)) for i in range(self.count)])

    def total(self, x, groups):
        for group in groups:
            terms = [x] + [self.partner(x, group, r) for r in range(1, group[1])]
            while len(terms) > 1:
                terms = [p + q for p, q in zip(terms[::2], terms[1::2], strict=True)]
            x = terms[0]
        return x


class Gather:
    def __init__(self, cube, x, groups):
        self.cube, self.x, self.groups, self.seen = cube, x[None], list(groups), []

    def send(self):
        group = self.groups[0]
        self.got = [self.cube.partner(self.x, group, r) for r in range(1, group[1])]

    def take(self):
        group = self.groups.pop(0)
        inner = 1
        for low, ways in self.seen:
            inner *= ways if low < group[0] else 1
        self.seen.append(group)
        parts = [x.reshape((-1, inner) + x.shape[1:]) for x in [self.x] + list(self.got)]
        x = place_blocks(self.cube.place(group), parts)
        self.x = x.reshape((-1,) + self.x.shape[1:])

    def left(self):
        return len(self.groups)


class Parts:
    def __init__(self, cube, x, groups):
        self.cube, self.parts, self.ids, self.groups = cube, [x], [0], list(groups)

    def send(self):
        self.got = [self.cube.partner(x, self.groups[0], 1) for x in self.parts]

    def take(self):
        low, _ = self.groups.pop(0)
        self.parts = self.parts + list(self.got)
        self.ids = self.ids + [i | 1 << low for i in self.ids]

    def left(self):
        return len(self.groups)


class Sum:
    def __init__(self, cube, keeps, sends, groups):
        self.cube, self.groups = cube, list(groups)
        self.keeps, self.sends = list(keeps), [list(sends)]

    def send(self):
        group = self.groups[0]
        self.got = [[self.cube.partner(x, group, r + 1) for x in xs] for r, xs in enumerate(self.sends)]

    def take(self):
        self.groups.pop(0)
        terms = [[keep] + [got[i] for got in self.got] for i, keep in enumerate(self.keeps)]
        if self.groups:
            low, ways = self.groups[0]
            inner = 1
            for other, count in self.groups[1:]:
                inner *= count if other < low else 1
            keep, *sends = fold(self.cube.place((low, ways)), ways, inner, terms, False)
            self.keeps, self.sends = [keep], [[x] for x in sends]
        else:
            (self.x,) = fold(jnp.zeros((), jnp.int32), 1, 1, terms, True)

    def left(self):
        return len(self.groups)


def after(first, then):
    return lax.optimization_barrier((first, then))[1]


def land(moves, values):
    held = lax.optimization_barrier(([m.got for m in moves], tuple(values)))
    for m, got in zip(moves, held[0], strict=True):
        m.got = got
    return held[1]


def arrive(moves, values=()):
    values = land(moves, values)
    for m in moves:
        m.take()
    return values


def per_device(
    mesh,
    dec_in,
    memory,
    cotangent,
    dec_lengths,
    mem_mask,
    bucket_map,
    self_weights,
    cross_weights,
    ffn_in,
    ffn_out,
    norm_gains,
    bias_table,
):
    cube = Cube(mesh)
    near_sums, near_gathers = cube.near_groups, cube.near_groups[::-1]
    slots, rows, width = dec_in.shape
    tokens = slots * rows
    buckets = bias_table.shape[0]
    hidden = ffn_in.shape[2]
    unit = self_weights.shape[1]
    exchange = unit == UNIT and cube.fits
    bit = lax.axis_index("seq").astype(jnp.int32) & 1

    assert memory.shape[1] <= 256
    count = jnp.sum(mem_mask, axis=1).astype(BF)
    memory = jnp.concatenate([memory, jnp.broadcast_to(count[:, None, None], (slots, TAIL, width))], axis=1)
    x_move = Parts(cube, dec_in, near_gathers)
    m_move = Parts(cube, memory, near_gathers)
    x_move.send()
    if exchange:
        w_move = Gather(cube, self_weights, [cube.z, cube.xy])
        c_move = Gather(cube, cross_weights, [cube.y, cube.z, cube.x])
        w_move.send()
        c_move.send()
        w_move.take()
        w_move.send()
        x_move.got, c_move.got, ffn_in, ffn_out = after(w_move.x, (x_move.got, c_move.got, ffn_in, ffn_out))
        x_move.take()
        x_move.send()
        (c_move.got,) = arrive([x_move], (c_move.got,))
        c_move.take()
        c_move.send()
        packed = jnp.concatenate([to_tiles(ffn_in), to_tiles(ffn_out[None])])
        gathered = lax.all_gather(packed, ("dp", "seq"), axis=0, tiled=False)
        w_move.got = after(x_move.parts, w_move.got)
        w_move.take()
        w_move.x = after(c_move.got, w_move.x)
        w_got = cube.partner(w_move.x, cube.core, 1)
        c_move.got = after(w_move.x, c_move.got)
        c_move.take()
        c_move.send()
        m_move.parts[0] = after(c_move.x, m_move.parts[0])
        m_move.send()
        own1, got1 = after(c_move.x, (w_move.x, w_got))
        ffn_tiles = gathered.reshape(cube.count, 3 * UNIT // 8, hidden // 128, 8, 128)
    else:
        bit = bit * 0
        for move in (x_move, m_move):
            if move is m_move:
                move.send()
            arrive([move])
            while move.left():
                move.send()
                arrive([move])
        own1, got1 = in_halves(lax.all_gather(self_weights, ("dp", "seq"), axis=1, tiled=True))
        own2, got2 = in_halves(lax.all_gather(cross_weights, ("dp", "seq"), axis=1, tiled=True))
        w01 = lax.all_gather(ffn_in, ("dp", "seq"), axis=1, tiled=True)
        w2 = lax.all_gather(ffn_out, ("dp", "seq"), axis=0, tiled=True)
        w01 = w01.reshape(2, -1, UNIT // 8, 8, hidden // 128, 128).transpose(1, 0, 2, 4, 3, 5)
        w01 = w01.reshape(w01.shape[0], -1, hidden // 128, 8, 128)
        w2 = w2.reshape(w01.shape[0], -1, 8, width // 128, 128).transpose(0, 1, 3, 2, 4)
        w2 = w2.reshape(w01.shape[0], -1, hidden // 128, 8, 128)
        ffn_tiles = jnp.concatenate([w01, w2], axis=1)

    positions = bucket_map.shape[0]
    hot = (bucket_map[::-1][None, :] == jnp.arange(buckets, dtype=jnp.int32)[:, None]).astype(F32)
    line = jnp.einsum("bh,bm->hm", bias_table, hot, precision=lax.Precision.HIGHEST)
    line = line.reshape(H * DK // WIDE, WIDE // DK, positions)
    me = lax.axis_index("seq").astype(jnp.int32)
    lims = jnp.concatenate([(me * rows)[None], dec_lengths, me[None], bit[None]])

    near = tuple(x_move.ids)
    outs = self_forward(lims, near, x_move.parts, norm_gains, own1, got1, line)
    if exchange:
        outs = arrive([c_move, m_move], outs)
        own2, got2 = c_move.x, cube.partner(c_move.x, cube.core, 1)
        m_move.send()
        arrive([m_move])
    q1, k1, v1, o1, lse1 = outs
    h1, q2, k2, v2, o2, lse2 = cross_forward(
        lims, near, m_move.parts, dec_in, o1, own1, got1, norm_gains, own2, got2
    )
    flat = (tokens, width)
    h1 = h1.reshape(flat)
    o1 = o1.reshape(flat)
    o2 = o2.reshape(flat)
    layer_out, gh2, gain_third, dw = feed_forward(
        lims, h1, o2, own2, got2, norm_gains, cotangent.reshape(flat), ffn_tiles
    )
    if exchange:
        ffn_shard = lax.psum_scatter(dw, ("dp", "seq"), scatter_dimension=0, tiled=True)
    outs = cross_backward(lims, near, m_move.parts, gh2, h1, o1, o2, own2, got2, norm_gains, q2, k2, v2, lse2)
    gh1, gain_second, mkeep, msend, ckeep, csend, skeep, ssend = outs
    mem = Sum(cube, [in_rows(mkeep)], [in_rows(msend)], near_sums)
    mem.send()
    if exchange:
        others = Sum(
            cube,
            [in_rows(ckeep), in_rows(skeep)],
            [in_rows(csend), in_rows(ssend)],
            [cube.core, cube.xy, cube.z],
        )
        others.send()
        (gh1,) = arrive([others, mem], (gh1,))
        gh1 = after((others.sends, mem.sends), gh1)
        others.send()
    else:
        arrive([mem])
    mem.send()
    outs = self_backward(lims, near, x_move.parts, gh1, own1, got1, norm_gains, line, q1, k1, v1, lse1)
    xkeep, xsend, table, keep, send = outs
    if exchange:
        (xsend, send) = land([others, mem], (xsend, send))
    first = Sum(cube, [in_rows(xkeep)], [in_rows(xsend)], near_sums)
    if exchange:
        own = Sum(cube, [in_rows(keep)], [in_rows(send)], [cube.core, cube.xy, cube.z])
        own.send()
        first.send()
        others.take()
        others.send()
        own.got = after(others.sends, own.got)
        own.take()
        own.send()
        (first.got, mem.got, others.got) = after(own.sends, (first.got, mem.got, others.got))
        mem.take()
        first.take()
        (own.got, first.sends) = after((first.sends, mem.x), (own.got, first.sends))
        (first.sends,) = land([own], (first.sends,))
        own.take()
        own.send()
        first.send()
        others.got = after(own.sends, others.got)
        others.take()
        (first.got,) = land([own], (first.got,))
        own.take()
        first.take()
        tiles = unit // 8
        pieces = others.x[0]
        *cross_shard, out1 = [pieces[tiles * m : tiles * (m + 1)].reshape(unit, width) for m in range(5)]
        gate_shard, down_shard = ffn_shard[:, : 2 * hidden], down_back(ffn_shard[:, 2 * hidden :], width)
        self_shard = own.x[0].reshape(3, unit, width)
        self_shard = jnp.concatenate([self_shard, out1[None]])
        cross_shard = jnp.stack(cross_shard)
    else:
        first.send()
        arrive([mem, first])
        while first.left():
            first.send()
            arrive([first])
        self_grad = jnp.concatenate([from_halves(keep, send), from_halves(skeep[:, None], ssend[:, None])])
        self_shard = lax.psum_scatter(self_grad, ("dp", "seq"), scatter_dimension=1, tiled=True).astype(F32)
        cross_grad = from_halves(ckeep, csend)
        cross_shard = lax.psum_scatter(cross_grad, ("dp", "seq"), scatter_dimension=1, tiled=True).astype(F32)
        gate_shard = lax.psum_scatter(dw[:, : 2 * hidden], ("dp", "seq"), scatter_dimension=0, tiled=True)
        down_grad = down_back(dw[:, 2 * hidden :], width)
        down_shard = lax.psum_scatter(down_grad, ("dp", "seq"), scatter_dimension=0, tiled=True)
    while mem.left():
        mem.send()
        arrive([mem])
    mem_grad = mem.x.reshape(slots, -1, width)
    down_shard = down_shard.astype(F32)
    gate_shard = gate_shard.astype(F32).reshape(-1, ffn_in.shape[2] // TILE, 2, TILE)
    gate_shard = gate_shard.transpose(2, 0, 1, 3).reshape(ffn_in.shape)
    dv, gain_first = normed_back(dec_in.astype(F32).reshape(flat), norm_gains[0:1], first.x.reshape(flat))
    dec_grad = (gh1 + dv).reshape(dec_in.shape)
    table_part = jnp.einsum("hm,bm->bh", table.reshape(H, positions), hot, precision=lax.Precision.HIGHEST)

    self_square = self_shard * self_shard
    cross_square = cross_shard * cross_shard
    gate_square = gate_shard * gate_shard
    down_square = down_shard * down_shard
    hidden = ffn_in.shape[2]
    def summed(terms):
        packed = jnp.concatenate([t.reshape(-1, 128) for t in terms])
        packed = cube.total(packed, [cube.core, cube.xy, cube.z] if exchange else cube.bits)
        sums = []
        at = 0
        for t in terms:
            count = t.size // 128
            sums.append(packed[at : at + count].reshape(t.shape))
            at += count
        return sums

    gain_first, gain_second, gain_third, table_grad, self_cols, cross_cols, gate_cols, down_cols = summed(
        [
            gain_first,
            gain_second,
            gain_third,
            table_part,
            jnp.sum(self_square, axis=1) / width,
            jnp.sum(cross_square, axis=1) / width,
            jnp.sum(gate_square, axis=1) / width,
            jnp.sum(down_square, axis=0) / hidden,
        ]
    )
    gains_grad = jnp.concatenate([gain_first, gain_second, gain_third])
    self_row_means = jnp.mean(self_square, axis=2)
    cross_row_means = jnp.mean(cross_square, axis=2)
    shard_rows = self_shard.shape[1]
    column_start = lax.axis_index(("dp", "seq")) * shard_rows
    self_col_piece = lax.dynamic_slice_in_dim(self_cols[3], column_start, shard_rows, 0)
    cross_col_piece = lax.dynamic_slice_in_dim(cross_cols[3], column_start, shard_rows, 0)
    out_proj_stats = jnp.stack(
        [
            jnp.stack([self_row_means[3], self_col_piece]),
            jnp.stack([cross_row_means[3], cross_col_piece]),
        ]
    )
    return (
        layer_out.reshape(dec_in.shape),
        dec_grad,
        mem_grad,
        self_shard,
        cross_shard,
        gate_shard,
        down_shard,
        gains_grad,
        table_grad,
        self_row_means[:3],
        self_cols[:3],
        cross_row_means[:3],
        cross_cols[:3],
        jnp.mean(gate_square, axis=2),
        gate_cols,
        jnp.mean(down_square, axis=1),
        down_cols,
        out_proj_stats,
    )


def solution(mesh):
    in_specs = (
        P("dp", "seq", None),
        P("dp", "seq", None),
        P("dp", "seq", None),
        P("dp"),
        P("dp", "seq"),
        P(),
        P(None, ("dp", "seq"), None),
        P(None, ("dp", "seq"), None),
        P(None, ("dp", "seq"), None),
        P(("dp", "seq"), None),
        P(),
        P(),
    )
    out_specs = (
        P("dp", "seq", None),
        P("dp", "seq", None),
        P("dp", "seq", None),
        P(None, ("dp", "seq"), None),
        P(None, ("dp", "seq"), None),
        P(None, ("dp", "seq"), None),
        P(("dp", "seq"), None),
        P(),
        P(),
        P(None, ("dp", "seq")),
        P(),
        P(None, ("dp", "seq")),
        P(),
        P(None, ("dp", "seq")),
        P(),
        P(("dp", "seq")),
        P(),
        P(None, None, ("dp", "seq")),
    )
    return jax.shard_map(
        functools.partial(per_device, mesh),
        mesh=mesh,
        in_specs=in_specs,
        out_specs=out_specs,
        check_vma=False,
    )
```

```python
import functools

import jax
import jax.numpy as jnp
from jax import lax
from jax.experimental import pallas as pl
from jax.experimental.pallas import tpu as pltpu
from jax.sharding import PartitionSpec as P

H = 12
DK = 64
PAIR = 2 * DK
WIDE = 4 * DK
TILE = 512
UNIT = 24
TAIL = 8
EPS = 1e-06
MASKED = -1000000000.0
BF = jnp.bfloat16
F32 = jnp.float32
BUDGET = 60 * 1024 * 1024
COST = pl.CostEstimate(flops=1000, bytes_accessed=1000, transcendentals=0)


def dot_nn(a, b):
    return lax.dot_general(a, b, (((1,), (0,)), ((), ())), preferred_element_type=F32)


def dot_nt(a, b):
    return lax.dot_general(a, b, (((1,), (1,)), ((), ())), preferred_element_type=F32)


def dot_tn(a, b):
    return lax.dot_general(a, b, (((0,), (0,)), ((), ())), preferred_element_type=F32)


def inverse_rms(v):
    return lax.rsqrt(jnp.mean(v * v, axis=-1, keepdims=True) + EPS)


def normed(v, gain):
    return (v * inverse_rms(v) * gain).astype(BF)


def normed_back(v, gain, c):
    r = inverse_rms(v)
    scaled = c * gain
    inner = jnp.mean(v * scaled, axis=-1, keepdims=True)
    dv = r * scaled - v * (r * r * r * inner)
    dgain = jnp.sum(c * v * r, axis=0, keepdims=True)
    return dv, dgain


def shear(rows, sign):
    keys = rows.shape[1]
    r = lax.broadcasted_iota(jnp.int32, (8, 1), 0)
    for bit in (1, 2, 4):
        turned = pltpu.roll(rows, bit if sign > 0 else keys - bit, 1)
        rows = jnp.where((r & bit) != 0, turned, rows)
    return rows


def build_bias(line, off, out_ref):
    count, keys = out_ref.shape
    base = shear(pltpu.roll(jnp.broadcast_to(line, (8, keys)), off + 1, 1), 1)
    for g in range(count // 8):
        out_ref[8 * g : 8 * g + 8, :] = pltpu.roll(base, (8 * g) % keys, 1) if g else base


def sum_diagonals(sum_ref, off):
    count, keys = sum_ref.shape
    total = sum_ref[0:8, :]
    for g in range(1, count // 8):
        total = total + pltpu.roll(sum_ref[8 * g : 8 * g + 8, :], (keys - 8 * g) % keys, 1)
    total = jnp.sum(shear(total, -1), axis=0, keepdims=True)
    return pltpu.roll(jnp.broadcast_to(total, (8, keys)), keys - 1 - off, 1)[0:1]


def low_lanes():
    return lax.broadcasted_iota(jnp.int32, (1, PAIR), 1) < DK


def head_part(x, head):
    low = low_lanes()
    mine = low if head % 2 == 0 else jnp.logical_not(low)
    return jnp.where(mine, x, jnp.zeros_like(x))


def row_limit(start, rows, count, causal):
    if not causal:
        return count
    seen = start + 1 + lax.broadcasted_iota(jnp.int32, (rows, 1), 0)
    return jnp.minimum(seen, count)


def attend(q_ref, k_ref, v_ref, o_ref, lse_ref, bias_ref, s_ref, p_ref, off, counts):
    slots, rows, _ = q_ref.shape
    keys = k_ref.shape[1]
    causal = bias_ref is not None
    cols = lax.broadcasted_iota(jnp.int32, (1, keys), 1)
    low = low_lanes()
    work = [(s, h) for s in range(slots) for h in range(WIDE // DK)]

    def lanes(h):
        return slice((h // 2) * PAIR, (h // 2) * PAIR + PAIR)

    def scores(n):
        s, h = work[n]
        s_ref[n % 2] = dot_nt(head_part(q_ref[s, :, lanes(h)], h), k_ref[s, :, lanes(h)])

    scores(0)
    kept = None
    for n, (s, h) in enumerate(work):
        if n + 1 < len(work):
            scores(n + 1)
        sc = s_ref[n % 2]
        if causal:
            sc = sc + bias_ref[h]
        sc = jnp.where(cols < row_limit(off, rows, counts[s], causal), sc, MASKED)
        top = jnp.max(sc, axis=1, keepdims=True)
        e = jnp.exp(sc - top)
        total = jnp.sum(e, axis=1, keepdims=True)
        p_ref[n % 2] = (e * (1.0 / total)).astype(BF)
        out = dot_nn(p_ref[n % 2], v_ref[s, :, lanes(h)])
        log_total = jnp.broadcast_to(top + jnp.log(total), (rows, PAIR))
        if h % 2 == 0:
            kept = (out, log_total)
        else:
            o_ref[s, :, lanes(h)] = jnp.where(low, kept[0], out).astype(BF)
            lse_ref[s, h // 2] = jnp.where(low, kept[1], log_total)


def attend_back(
    q_ref, k_ref, v_ref, g_ref, lse_ref, dq_ref, dk_ref, dv_ref,
    bias_ref, sum_ref, s_ref, dp_ref, p_ref, ds_ref, off, counts,
):
    slots, rows, _ = q_ref.shape
    keys = k_ref.shape[1]
    causal = bias_ref is not None
    cols = lax.broadcasted_iota(jnp.int32, (1, keys), 1)
    low = low_lanes()
    work = [(s, h) for s in range(slots) for h in range(WIDE // DK)]

    def lanes(h):
        return slice((h // 2) * PAIR, (h // 2) * PAIR + PAIR)

    def products(n):
        s, h = work[n]
        s_ref[n % 2] = dot_nt(head_part(q_ref[s, :, lanes(h)], h), k_ref[s, :, lanes(h)])
        dp_ref[n % 2] = dot_nt(head_part(g_ref[s, :, lanes(h)], h), v_ref[s, :, lanes(h)])

    products(0)
    kept = None
    for n, (s, h) in enumerate(work):
        if n + 1 < len(work):
            products(n + 1)
        sc = s_ref[n % 2]
        if causal:
            sc = sc + bias_ref[h]
        sc = jnp.where(cols < row_limit(off, rows, counts[s], causal), sc, MASKED)
        at = (h % 2) * DK
        p = jnp.exp(sc - lse_ref[s, h // 2, :, at : at + 1])
        dp = dp_ref[n % 2]
        inner = jnp.sum(p * dp, axis=1, keepdims=True)
        ds = (p * (dp - inner)).astype(BF)
        p_ref[n % 2] = p.astype(BF)
        ds_ref[n % 2] = ds
        if causal:
            if s == 0:
                sum_ref[h] = ds.astype(F32)
            else:
                sum_ref[h] += ds.astype(F32)
        ds = ds_ref[n % 2]
        dq = dot_nn(ds, k_ref[s, :, lanes(h)])
        dk = dot_tn(head_part(q_ref[s, :, lanes(h)], h), ds)
        dv = dot_tn(head_part(g_ref[s, :, lanes(h)], h), p_ref[n % 2])
        if h % 2 == 0:
            kept = (dq, dk, dv)
        else:
            dq_ref[s * rows : (s + 1) * rows, lanes(h)] = jnp.where(low, kept[0], dq).astype(BF)
            dk_ref[s * keys : (s + 1) * keys, lanes(h)] = (kept[1] + dk).astype(BF).T
            dv_ref[s * keys : (s + 1) * keys, lanes(h)] = (kept[2] + dv).astype(BF).T


def assemble(own_ref, got_ref, bit):
    own, got = own_ref[...].astype(F32), got_ref[...].astype(F32)
    both = jnp.stack([jnp.where(bit == 0, own, got), jnp.where(bit == 0, got, own)], axis=1)
    return both.reshape(-1, both.shape[-1]).astype(BF)


def row_counts(ms):
    counts = []
    for s in range(ms[0].shape[0]):
        count = sum(m_ref[s, -TAIL:, 0:PAIR].astype(F32)[0:1, 0:1] for m_ref in ms)
        counts.append(count.astype(jnp.int32))
    return counts


def part_blocks(x, pairs, bit, keep_ref, send_ref):
    x = x.reshape(pairs, 2, -1, x.shape[-1])
    first, second = x[:, 0], x[:, 1]
    keep_ref[...] = jnp.where(bit == 0, first, second).astype(BF)
    send_ref[...] = jnp.where(bit == 0, second, first).astype(BF)


def whole(shape):
    return pl.BlockSpec(shape, lambda b, *_: (0,) * len(shape), pipeline_mode=pl.Buffered(1))


def result(shape):
    return pl.BlockSpec(shape, lambda b, *_: (0,) * len(shape))


def wide(shape):
    return pl.BlockSpec(shape[:-1] + (WIDE,), lambda b, *_: (0,) * (len(shape) - 1) + (b,))


def halves(index, shape, lanes=WIDE):
    pairs, _, rows, width = shape
    if lanes == width:
        spec = pl.BlockSpec(
            (pairs, None, rows, width), lambda b, *_: (0, index, 0, 0), pipeline_mode=pl.Buffered(1)
        )
    else:
        spec = pl.BlockSpec((pairs, None, rows, lanes), lambda b, *_: (0, index, 0, b))
    return [spec, spec]


def params():
    return pltpu.CompilerParams(dimension_semantics=("arbitrary",), vmem_limit_bytes=BUDGET)


def self_forward_body(near, lims, *refs):
    xs = refs[: len(near)]
    (
        gain_ref, wq_own, wq_got, wk_own, wk_got, wv_own, wv_got, line_ref,
        q_ref, k_ref, v_ref, o_ref, lse_ref, a_ref, bias_ref, s_ref, p_ref,
    ) = refs[len(near) :]
    slots, rows, width = xs[0].shape
    keys = k_ref.shape[1]
    off, me, bit = lims[0], lims[1 + slots], lims[2 + slots]

    @pl.when(pl.program_id(0) == 0)
    def _():
        for r, x_ref in zip(near, xs, strict=True):
            for s in range(slots):
                at = pl.multiple_of(s * keys + (me ^ r) * rows, 128)
                a_ref[pl.ds(at, rows), :] = normed(x_ref[s].astype(F32), gain_ref[0:1, :])

    wq, wk, wv = assemble(wq_own, wq_got, bit), assemble(wk_own, wk_got, bit), assemble(wv_own, wv_got, bit)
    for s in range(slots):
        mine = pl.ds(pl.multiple_of(s * keys + off, 128), rows)
        q_ref[s] = dot_nn(a_ref[mine, :], wq).astype(BF)
        k_ref[s] = dot_nn(a_ref[s * keys : (s + 1) * keys, :], wk).astype(BF)
        v_ref[s] = dot_nn(a_ref[s * keys : (s + 1) * keys, :], wv).astype(BF)
    for h in range(WIDE // DK):
        build_bias(line_ref[0, h : h + 1, :], off, bias_ref.at[h])
    counts = [lims[1 + s] for s in range(slots)]
    attend(q_ref, k_ref, v_ref, o_ref, lse_ref, bias_ref, s_ref, p_ref, off, counts)


def self_forward(lims, near, xs, gains, own, got, line):
    slots, rows, width = xs[0].shape
    keys = rows * len(near)
    blocks = width // WIDE
    return pl.pallas_call(
        functools.partial(self_forward_body, near),
        grid_spec=pltpu.PrefetchScalarGridSpec(
            num_scalar_prefetch=1,
            grid=(blocks,),
            in_specs=[whole((slots, rows, width))] * len(near)
            + [whole(gains.shape)]
            + halves(0, own.shape)
            + halves(1, own.shape)
            + halves(2, own.shape)
            + [pl.BlockSpec((1, WIDE // DK, keys), lambda b, *_: (b, 0, 0))],
            out_specs=[
                wide((slots, rows, width)),
                wide((slots, keys, width)),
                wide((slots, keys, width)),
                wide((slots, rows, width)),
                pl.BlockSpec((slots, 2, rows, PAIR), lambda b, *_: (0, b, 0, 0)),
            ],
            scratch_shapes=[
                pltpu.VMEM((slots * keys, width), BF),
                pltpu.VMEM((WIDE // DK, rows, keys), F32),
                pltpu.VMEM((2, rows, keys), F32),
                pltpu.VMEM((2, rows, keys), BF),
            ],
        ),
        out_shape=[
            jax.ShapeDtypeStruct((slots, rows, width), BF),
            jax.ShapeDtypeStruct((slots, keys, width), BF),
            jax.ShapeDtypeStruct((slots, keys, width), BF),
            jax.ShapeDtypeStruct((slots, rows, width), BF),
            jax.ShapeDtypeStruct((slots, H // 2, rows, PAIR), F32),
        ],
        compiler_params=params(),
        cost_estimate=COST,
        name="self_forward",
    )(lims, *xs, gains, own, got, own, got, own, got, line)


def cross_forward_body(near, lims, *refs):
    ms = refs[: len(near)]
    (
        x_ref, o1_ref, wo_own, wo_got, gain_ref, wq_own, wq_got, wk_own, wk_got, wv_own, wv_got,
        h_ref, q_ref, k_ref, v_ref, o_ref, lse_ref, a_ref, mem_ref, s_ref, p_ref,
    ) = refs[len(near) :]
    slots, part, width = ms[0].shape
    part -= TAIL
    rows, keys = q_ref.shape[1], k_ref.shape[1]
    me, bit = lims[1 + slots], lims[2 + slots]

    @pl.when(pl.program_id(0) == 0)
    def _():
        wo = assemble(wo_own, wo_got, bit)
        for s in range(slots):
            h = x_ref[s].astype(F32) + dot_nn(o1_ref[s], wo)
            h_ref[s] = h
            a_ref[s * rows : (s + 1) * rows, :] = normed(h, gain_ref[1:2, :])
        for r, m_ref in zip(near, ms, strict=True):
            for s in range(slots):
                mem_ref[s, pl.ds(pl.multiple_of((me ^ r) * part, part), part), :] = m_ref[s, :part]

    wq, wk, wv = assemble(wq_own, wq_got, bit), assemble(wk_own, wk_got, bit), assemble(wv_own, wv_got, bit)
    for s in range(slots):
        q_ref[s] = dot_nn(a_ref[s * rows : (s + 1) * rows, :], wq).astype(BF)
        k_ref[s] = dot_nn(mem_ref[s], wk).astype(BF)
        v_ref[s] = dot_nn(mem_ref[s], wv).astype(BF)
    counts = row_counts(ms)
    attend(q_ref, k_ref, v_ref, o_ref, lse_ref, None, s_ref, p_ref, 0, counts)


def cross_forward(lims, near, ms, x, o1, own1, got1, gains, own, got):
    slots, part, width = ms[0].shape
    part -= TAIL
    keys = part * len(near)
    rows = x.shape[1]
    blocks = width // WIDE
    return pl.pallas_call(
        functools.partial(cross_forward_body, near),
        grid_spec=pltpu.PrefetchScalarGridSpec(
            num_scalar_prefetch=1,
            grid=(blocks,),
            in_specs=[whole((slots, part + TAIL, width))] * len(near)
            + [whole((slots, rows, width)), whole((slots, rows, width))]
            + halves(3, own1.shape, width)
            + [whole(gains.shape)]
            + halves(0, own.shape)
            + halves(1, own.shape)
            + halves(2, own.shape),
            out_specs=[
                result((slots, rows, width)),
                wide((slots, rows, width)),
                wide((slots, keys, width)),
                wide((slots, keys, width)),
                wide((slots, rows, width)),
                pl.BlockSpec((slots, 2, rows, PAIR), lambda b, *_: (0, b, 0, 0)),
            ],
            scratch_shapes=[
                pltpu.VMEM((slots * rows, width), BF),
                pltpu.VMEM((slots, keys, width), BF),
                pltpu.VMEM((2, rows, keys), F32),
                pltpu.VMEM((2, rows, keys), BF),
            ],
        ),
        out_shape=[
            jax.ShapeDtypeStruct((slots, rows, width), F32),
            jax.ShapeDtypeStruct((slots, rows, width), BF),
            jax.ShapeDtypeStruct((slots, keys, width), BF),
            jax.ShapeDtypeStruct((slots, keys, width), BF),
            jax.ShapeDtypeStruct((slots, rows, width), BF),
            jax.ShapeDtypeStruct((slots, H // 2, rows, PAIR), F32),
        ],
        compiler_params=params(),
        cost_estimate=COST,
        name="cross_forward",
    )(lims, *ms, x, o1, own1, got1, gains, own, got, own, got, own, got)


def down_rows(x):
    width = x.shape[-1]
    lanes = width // 128
    x = x.reshape(-1, 8, 8, width)
    count = 8 * lanes
    across = count // (UNIT // 8)
    tiles = [x[:, q // lanes, :, (q % lanes) * 128 : (q % lanes + 1) * 128] for q in range(count)]
    rows = [jnp.concatenate(tiles[i * across : (i + 1) * across], axis=-1) for i in range(UNIT // 8)]
    x = jnp.stack(rows, axis=1)
    return x.reshape(-1, across * 128)


def down_back(x, width):
    lanes = width // 128
    x = x.reshape(-1, UNIT // 8, 8, x.shape[-1] // 128, 128).transpose(0, 1, 3, 2, 4)
    x = x.reshape(-1, 8, lanes, 8, 128).transpose(0, 1, 3, 2, 4)
    return x.reshape(-1, width)


def gradient_copies(wide_ref, down_ref, dw_ref, sems):
    steps, _, columns = wide_ref.shape
    rows, across = down_ref.shape[1:]
    return [
        (
            pltpu.make_async_copy(wide_ref.at[n], dw_ref.at[:, pl.ds(n * columns, columns)], sems.at[2 * n]),
            pltpu.make_async_copy(
                down_ref.at[n],
                dw_ref.at[pl.ds(n * rows, rows), pl.ds(steps * columns, across)],
                sems.at[2 * n + 1],
            ),
        )
        for n in range(steps)
    ]


def from_columns(ref):
    columns = []
    for n in range(ref.shape[2]):
        columns.append(ref[:, :, n].astype(F32).reshape(-1, 128))
    return jnp.concatenate(columns, axis=-1).astype(BF)


def from_rows(ref, width):
    lanes = width // 128
    across = ref.shape[2]
    count = ref.shape[1] * across
    tiles = [ref[:, q // across, q % across].astype(F32) for q in range(count)]
    rows = [jnp.concatenate(tiles[n * lanes : (n + 1) * lanes], axis=-1) for n in range(count // lanes)]
    return jnp.stack(rows, axis=1).reshape(-1, width).astype(BF)


def feed_forward_body(
    lims, h1_ref, o2_ref, wo_own, wo_got, gain_ref, g_ref, w0_tiles, w1_tiles, wd_tiles,
    out_ref, gh_ref, dgain_ref, dw_ref, h_ref, a_ref, at_ref, acc_ref, da_ref, wide_ref, down_ref, sems,
):
    step = pl.program_id(0)
    bit = lims[lims.shape[0] - 1]

    @pl.when(step == 0)
    def _():
        h = h1_ref[...] + dot_nn(o2_ref[...], assemble(wo_own, wo_got, bit))
        h_ref[...] = h
        a = normed(h, gain_ref[2:3, :])
        a_ref[...] = a
        at_ref[...] = a.T
        acc_ref[...] = h
        da_ref[...] = jnp.zeros_like(da_ref)

    a = a_ref[...]
    e = g_ref[...]
    w0, w1, wd = from_columns(w0_tiles), from_columns(w1_tiles), from_rows(wd_tiles, a.shape[1])
    gate = dot_nn(a, w0)
    up = dot_nn(a, w1)
    c = dot_nt(e, wd)
    root = 0.7978845608028654
    square = gate * gate
    th = jnp.tanh(root * gate * (1.0 + 0.044715 * square))
    half = 0.5 * (1.0 + th)
    act = gate * half
    slope = half + 0.5 * gate * (1.0 - th * th) * (root * (1.0 + 3.0 * 0.044715 * square))
    hidden = (act * up).astype(BF)
    dgate = (c * up * slope).astype(BF)
    dup = (c * act).astype(BF)
    acc_ref[...] += dot_nn(hidden, wd)
    tile = dgate.shape[1]
    wide_ref[step, :, :tile] = dot_nn(at_ref[...], dgate).astype(BF)
    wide_ref[step, :, tile:] = dot_nn(at_ref[...], dup).astype(BF)
    down_ref[step] = down_rows(dot_tn(hidden, e)).astype(BF)
    moves = gradient_copies(wide_ref, down_ref, dw_ref, sems)
    for n, pair in enumerate(moves):

        @pl.when(step == n)
        def _():
            for move in pair:
                move.start()

    da_ref[...] += dot_nt(dgate, w0) + dot_nt(dup, w1)

    @pl.when(step == pl.num_programs(0) - 1)
    def _():
        out_ref[...] = acc_ref[...].astype(BF)
        dv, dgain = normed_back(h_ref[...], gain_ref[2:3, :], da_ref[...])
        gh_ref[...] = e.astype(F32) + dv
        dgain_ref[...] = dgain
        for pair in moves:
            for move in pair:
                move.wait()


def feed_forward(lims, h1, o2, own, got, gains, cot, tiles):
    tokens, width = h1.shape
    devices, parts, across, _, _ = tiles.shape
    hidden = across * 128
    tile = TILE
    steps = hidden // tile
    assert hidden // 64 == width // UNIT == devices
    return pl.pallas_call(
        feed_forward_body,
        grid_spec=pltpu.PrefetchScalarGridSpec(
            num_scalar_prefetch=1,
            grid=(hidden // tile,),
            in_specs=[whole((tokens, width)), whole((tokens, width))]
            + halves(3, own.shape, width)
            + [
                whole(gains.shape),
                whole((tokens, width)),
                pl.BlockSpec((devices, parts // 3, tile // 128, 8, 128), lambda b, *_: (0, 0, b, 0, 0)),
                pl.BlockSpec((devices, parts // 3, tile // 128, 8, 128), lambda b, *_: (0, 1, b, 0, 0)),
                pl.BlockSpec((devices // steps, parts // 3, across, 8, 128), lambda b, *_: (b, 2, 0, 0, 0)),
            ],
            out_specs=[
                result((tokens, width)),
                result((tokens, width)),
                result((1, width)),
                pl.BlockSpec(memory_space=pl.ANY),
            ],
            scratch_shapes=[
                pltpu.VMEM((tokens, width), F32),
                pltpu.VMEM((tokens, width), BF),
                pltpu.VMEM((width, tokens), BF),
                pltpu.VMEM((tokens, width), F32),
                pltpu.VMEM((tokens, width), F32),
                pltpu.VMEM((steps, width, 2 * tile), BF),
                pltpu.VMEM((steps, width // steps, hidden), BF),
                pltpu.SemaphoreType.DMA((2 * steps,)),
            ],
        ),
        out_shape=[
            jax.ShapeDtypeStruct((tokens, width), BF),
            jax.ShapeDtypeStruct((tokens, width), F32),
            jax.ShapeDtypeStruct((1, width), F32),
            jax.ShapeDtypeStruct((width, 3 * hidden), BF),
        ],
        compiler_params=params(),
        cost_estimate=COST,
        name="feed_forward",
    )(lims, h1, o2, own, got, gains, cot, tiles, tiles, tiles)


def cross_backward_body(near, lims, *refs):
    ms = refs[: len(near)]
    (
        gh2_ref, h1_ref, o1_ref, o2_ref, wo_own, wo_got, gain_ref, q_ref, k_ref, v_ref, lse_ref,
        wq_own, wq_got, wk_own, wk_got, wv_own, wv_got,
        gh_ref, dgain_ref, mkeep_ref, msend_ref, keep_ref, send_ref, skeep_ref, ssend_ref,
        g_ref, e_ref, at_ref, memt_ref, da_ref, dm_ref, dq_ref, dk_ref, dv_ref, s_ref, dp_ref, p_ref, ds_ref,
    ) = refs[len(near) :]
    step = pl.program_id(0)
    slots, part, width = ms[0].shape
    part -= TAIL
    rows, keys = q_ref.shape[1], k_ref.shape[1]
    me, bit = lims[1 + slots], lims[2 + slots]
    pairs = keep_ref.shape[0]

    @pl.when(step == 0)
    def _():
        e = gh2_ref[...].astype(BF)
        back = dot_nt(e, assemble(wo_own, wo_got, bit)).astype(BF)
        for b in range(width // WIDE):
            e_ref[b] = e[:, b * WIDE : (b + 1) * WIDE]
            for s in range(slots):
                g_ref[b, s] = back[s * rows : (s + 1) * rows, b * WIDE : (b + 1) * WIDE]
        at_ref[...] = normed(h1_ref[...], gain_ref[1:2, :]).T
        for r, m_ref in zip(near, ms, strict=True):
            for s in range(slots):
                at = pl.multiple_of(s * keys + (me ^ r) * part, part)
                memt_ref[pl.ds(at, part), :] = m_ref[s, :part]
        da_ref[...] = jnp.zeros_like(da_ref)
        dm_ref[...] = jnp.zeros_like(dm_ref)

    counts = row_counts(ms)
    attend_back(
        q_ref, k_ref, v_ref, g_ref.at[step], lse_ref, dq_ref, dk_ref, dv_ref,
        None, None, s_ref, dp_ref, p_ref, ds_ref, 0, counts,
    )
    for m, grad in enumerate(
        (
            dot_nn(at_ref[...], dq_ref[...]),
            dot_tn(memt_ref[...], dk_ref[...]),
            dot_tn(memt_ref[...], dv_ref[...]),
            dot_tn(o2_ref[...], e_ref[step]),
        )
    ):
        part_blocks(grad, pairs, bit, keep_ref.at[:, m], send_ref.at[:, m])
    da_ref[...] += dot_nt(dq_ref[...], assemble(wq_own, wq_got, bit))
    dm_ref[...] += dot_nt(dk_ref[...], assemble(wk_own, wk_got, bit)) + dot_nt(
        dv_ref[...], assemble(wv_own, wv_got, bit)
    )

    @pl.when(step == pl.num_programs(0) - 1)
    def _():
        dv, dgain = normed_back(h1_ref[...], gain_ref[1:2, :], da_ref[...])
        gh = gh2_ref[...] + dv
        gh_ref[...] = gh
        dgain_ref[...] = dgain
        part_blocks(dot_tn(o1_ref[...], gh.astype(BF)), pairs, bit, skeep_ref, ssend_ref)
        for s in range(slots):
            for n in range(len(near) // 2):
                keep = pl.multiple_of(s * keys + (2 * n + bit) * part, part)
                send = pl.multiple_of(s * keys + (2 * n + 1 - bit) * part, part)
                mkeep_ref[s * (len(near) // 2) + n] = dm_ref[pl.ds(keep, part), :].astype(BF)
                msend_ref[s * (len(near) // 2) + n] = dm_ref[pl.ds(send, part), :].astype(BF)


def cross_backward(lims, near, ms, gh2, h1, o1, o2, own, got, gains, q, k, v, lse):
    slots, part, width = ms[0].shape
    part -= TAIL
    keys = part * len(near)
    rows = q.shape[1]
    tokens = slots * rows
    blocks = width // WIDE
    pairs, count, unit, _ = own.shape
    half = jax.ShapeDtypeStruct((slots * len(near) // 2, part, width), BF)
    grads = pl.BlockSpec((pairs, count, unit, WIDE), lambda b, *_: (0, 0, 0, b))
    return pl.pallas_call(
        functools.partial(cross_backward_body, near),
        grid_spec=pltpu.PrefetchScalarGridSpec(
            num_scalar_prefetch=1,
            grid=(blocks,),
            in_specs=[whole((slots, part + TAIL, width))] * len(near)
            + [whole((tokens, width))] * 4
            + halves(3, own.shape, width)
            + [
                whole(gains.shape),
                wide((slots, rows, width)),
                wide((slots, keys, width)),
                wide((slots, keys, width)),
                pl.BlockSpec((slots, 2, rows, PAIR), lambda b, *_: (0, b, 0, 0)),
            ]
            + halves(0, own.shape)
            + halves(1, own.shape)
            + halves(2, own.shape),
            out_specs=[
                result((tokens, width)),
                result((1, width)),
                result(half.shape),
                result(half.shape),
                grads,
                grads,
                result((pairs, unit, width)),
                result((pairs, unit, width)),
            ],
            scratch_shapes=[
                pltpu.VMEM((blocks, slots, rows, WIDE), BF),
                pltpu.VMEM((blocks, tokens, WIDE), BF),
                pltpu.VMEM((width, tokens), BF),
                pltpu.VMEM((slots * keys, width), BF),
                pltpu.VMEM((tokens, width), F32),
                pltpu.VMEM((slots * keys, width), F32),
                pltpu.VMEM((tokens, WIDE), BF),
                pltpu.VMEM((slots * keys, WIDE), BF),
                pltpu.VMEM((slots * keys, WIDE), BF),
                pltpu.VMEM((2, rows, keys), F32),
                pltpu.VMEM((2, rows, keys), F32),
                pltpu.VMEM((2, rows, keys), BF),
                pltpu.VMEM((2, rows, keys), BF),
            ],
        ),
        out_shape=[
            jax.ShapeDtypeStruct((tokens, width), F32),
            jax.ShapeDtypeStruct((1, width), F32),
            half,
            half,
            jax.ShapeDtypeStruct(own.shape, BF),
            jax.ShapeDtypeStruct(own.shape, BF),
            jax.ShapeDtypeStruct((pairs, unit, width), BF),
            jax.ShapeDtypeStruct((pairs, unit, width), BF),
        ],
        compiler_params=params(),
        cost_estimate=COST,
        name="cross_backward",
    )(lims, *ms, gh2, h1, o1, o2, own, got, gains, q, k, v, lse, own, got, own, got, own, got)


def self_backward_body(near, lims, *refs):
    xs = refs[: len(near)]
    (
        gh1_ref, wo_own, wo_got, gain_ref, line_ref, q_ref, k_ref, v_ref, lse_ref,
        wq_own, wq_got, wk_own, wk_got, wv_own, wv_got,
        xkeep_ref, xsend_ref, table_ref, keep_ref, send_ref,
        g_ref, at_ref, da_ref, dq_ref, dk_ref, dv_ref, bias_ref, sum_ref, s_ref, dp_ref, p_ref, ds_ref,
    ) = refs[len(near) :]
    step = pl.program_id(0)
    slots, rows, width = xs[0].shape
    keys = k_ref.shape[1]
    off, me, bit = lims[0], lims[1 + slots], lims[2 + slots]
    pairs = keep_ref.shape[0]

    @pl.when(step == 0)
    def _():
        e = gh1_ref[...].astype(BF)
        back = dot_nt(e, assemble(wo_own, wo_got, bit)).astype(BF)
        for b in range(width // WIDE):
            for s in range(slots):
                g_ref[b, s] = back[s * rows : (s + 1) * rows, b * WIDE : (b + 1) * WIDE]
        for r, x_ref in zip(near, xs, strict=True):
            for s in range(slots):
                at = pl.multiple_of(s * keys + (me ^ r) * rows, 128)
                at_ref[:, pl.ds(at, rows)] = normed(x_ref[s].astype(F32), gain_ref[0:1, :]).T
        da_ref[...] = jnp.zeros_like(da_ref)

    for h in range(WIDE // DK):
        build_bias(line_ref[0, h : h + 1, :], off, bias_ref.at[h])
    counts = [lims[1 + s] for s in range(slots)]
    attend_back(
        q_ref, k_ref, v_ref, g_ref.at[step], lse_ref, dq_ref, dk_ref, dv_ref,
        bias_ref, sum_ref, s_ref, dp_ref, p_ref, ds_ref, off, counts,
    )
    for h in range(WIDE // DK):
        table_ref[0, h : h + 1, :] = sum_diagonals(sum_ref.at[h], off)
    wq = assemble(wq_own, wq_got, bit)
    dwq = None
    for s in range(slots):
        mine = pl.ds(pl.multiple_of(s * keys + off, 128), rows)
        dq = dq_ref[s * rows : (s + 1) * rows, :]
        part = dot_nn(at_ref[:, mine], dq)
        dwq = part if dwq is None else dwq + part
        da_ref[mine, :] += dot_nt(dq, wq)
    for m, grad in enumerate((dwq, dot_nn(at_ref[...], dk_ref[...]), dot_nn(at_ref[...], dv_ref[...]))):
        part_blocks(grad, pairs, bit, keep_ref.at[:, m], send_ref.at[:, m])
    da_ref[...] += dot_nt(dk_ref[...], assemble(wk_own, wk_got, bit)) + dot_nt(
        dv_ref[...], assemble(wv_own, wv_got, bit)
    )

    @pl.when(step == pl.num_programs(0) - 1)
    def _():
        for s in range(slots):
            for n in range(len(near) // 2):
                keep = pl.multiple_of(s * keys + (2 * n + bit) * rows, 128)
                send = pl.multiple_of(s * keys + (2 * n + 1 - bit) * rows, 128)
                xkeep_ref[s * (len(near) // 2) + n] = da_ref[pl.ds(keep, rows), :].astype(BF)
                xsend_ref[s * (len(near) // 2) + n] = da_ref[pl.ds(send, rows), :].astype(BF)


def self_backward(lims, near, xs, gh1, own, got, gains, line, q, k, v, lse):
    slots, rows, width = xs[0].shape
    keys = rows * len(near)
    tokens = slots * rows
    blocks = width // WIDE
    pairs, count, unit, _ = own.shape
    heads = WIDE // DK
    half = jax.ShapeDtypeStruct((slots * len(near) // 2, rows, width), BF)
    grads = pl.BlockSpec((pairs, count - 1, unit, WIDE), lambda b, *_: (0, 0, 0, b))
    return pl.pallas_call(
        functools.partial(self_backward_body, near),
        grid_spec=pltpu.PrefetchScalarGridSpec(
            num_scalar_prefetch=1,
            grid=(blocks,),
            in_specs=[whole((slots, rows, width))] * len(near)
            + [whole((tokens, width))]
            + halves(3, own.shape, width)
            + [
                whole(gains.shape),
                pl.BlockSpec((1, heads, keys), lambda b, *_: (b, 0, 0)),
                wide((slots, rows, width)),
                wide((slots, keys, width)),
                wide((slots, keys, width)),
                pl.BlockSpec((slots, 2, rows, PAIR), lambda b, *_: (0, b, 0, 0)),
            ]
            + halves(0, own.shape)
            + halves(1, own.shape)
            + halves(2, own.shape),
            out_specs=[
                result(half.shape),
                result(half.shape),
                pl.BlockSpec((1, heads, keys), lambda b, *_: (b, 0, 0)),
                grads,
                grads,
            ],
            scratch_shapes=[
                pltpu.VMEM((blocks, slots, rows, WIDE), BF),
                pltpu.VMEM((width, slots * keys), BF),
                pltpu.VMEM((slots * keys, width), F32),
                pltpu.VMEM((tokens, WIDE), BF),
                pltpu.VMEM((slots * keys, WIDE), BF),
                pltpu.VMEM((slots * keys, WIDE), BF),
                pltpu.VMEM((heads, rows, keys), F32),
                pltpu.VMEM((heads, rows, keys), F32),
                pltpu.VMEM((2, rows, keys), F32),
                pltpu.VMEM((2, rows, keys), F32),
                pltpu.VMEM((2, rows, keys), BF),
                pltpu.VMEM((2, rows, keys), BF),
            ],
        ),
        out_shape=[
            half,
            half,
            jax.ShapeDtypeStruct((blocks, heads, keys), F32),
            jax.ShapeDtypeStruct((pairs, count - 1, unit, width), BF),
            jax.ShapeDtypeStruct((pairs, count - 1, unit, width), BF),
        ],
        compiler_params=params(),
        cost_estimate=COST,
        name="self_backward",
    )(lims, *xs, gh1, own, got, gains, line, q, k, v, lse, own, got, own, got, own, got)


def to_tiles(w):
    m, r, c = w.shape
    return w.reshape(m, r // 8, 8, c // 128, 128).transpose(0, 1, 3, 2, 4).reshape(-1, 8, 128)


def place_body(ways, scalar_ref, *refs):
    for r in range(ways):

        @pl.when(pl.program_id(0) == r)
        def _():
            refs[ways][...] = refs[r][...]


def place_blocks(place, parts):
    ways = len(parts)
    outer, inner, tail = parts[0].shape[0], parts[0].shape[1], parts[0].shape[2:]
    rest = (0,) * len(tail)
    spec = pl.BlockSpec((outer, inner) + tail, lambda r, s: (0, 0) + rest)
    return pl.pallas_call(
        functools.partial(place_body, ways),
        grid_spec=pltpu.PrefetchScalarGridSpec(
            num_scalar_prefetch=1,
            grid=(ways,),
            in_specs=[spec] * ways,
            out_specs=pl.BlockSpec((outer, None, inner) + tail, lambda r, s: (0, s[0] ^ r, 0) + rest),
        ),
        out_shape=jax.ShapeDtypeStruct((outer, ways, inner) + tail, BF),
        compiler_params=params(),
        cost_estimate=COST,
        name="place_blocks",
    )(place.reshape(1), *parts)


def fold_body(groups, ways, last, *refs):
    refs = refs[1:]
    inputs = ways * sum(1 + terms for _, terms in groups)
    outs = refs[inputs:]
    n = 0
    for j in range(ways):
        at = 0
        for size, terms in groups:
            x = refs[n][...].astype(F32)
            for t in range(terms):
                x = x + refs[n + 1 + t][...].astype(F32)
            n += 1 + terms
            outs[j][:, :, at : at + size] = x if last else x.astype(BF)
            at += size


def fold(place, ways, inner, groups, last):
    outer, width = groups[0][0].shape[0] // (ways * inner), groups[0][0].shape[-1]
    sizes = [g[0].shape[1] for g in groups]
    total = sum(sizes)
    step = outer
    moved = sum(size * (len(g) + 1) for size, g in zip(sizes, groups, strict=True))
    while step > 1 and step * inner * ways * moved * 8 * width * 2 > 6 * 1024 * 1024:
        step //= 2

    def spec(j, size):
        return pl.BlockSpec((step, None, inner, size, 8, width), lambda g, s: (g, s[0] ^ j, 0, 0, 0, 0))

    in_specs, ins = [], []
    for j in range(ways):
        for size, terms in zip(sizes, groups, strict=True):
            in_specs += [spec(j, size)] * len(terms)
            ins += [t.reshape((outer, ways, inner) + t.shape[1:]) for t in terms]
    made = pl.pallas_call(
        functools.partial(fold_body, [(size, len(g) - 1) for size, g in zip(sizes, groups, strict=True)], ways, last),
        grid_spec=pltpu.PrefetchScalarGridSpec(
            num_scalar_prefetch=1,
            grid=(outer // step,),
            in_specs=in_specs,
            out_specs=[pl.BlockSpec((step, inner, total, 8, width), lambda g, s: (g, 0, 0, 0, 0))] * ways,
        ),
        out_shape=[jax.ShapeDtypeStruct((outer, inner, total, 8, width), F32 if last else BF)] * ways,
        compiler_params=params(),
        cost_estimate=COST,
        name="fold_blocks",
    )(place.reshape(1), *ins)
    return [x.reshape((outer * inner,) + x.shape[2:]) for x in made]


def in_halves(w):
    x = w.reshape(w.shape[0], -1, 2, UNIT, w.shape[-1]).transpose(2, 1, 0, 3, 4)
    return x[0], x[1]


def from_halves(first, second):
    x = jnp.stack([first, second], axis=1)
    return x.transpose(2, 0, 1, 3, 4).reshape(x.shape[2], -1, x.shape[-1])


def in_rows(x):
    return x.reshape(x.shape[0], -1, 8, x.shape[-1])


class Cube:
    axes = ("dp", "seq")

    def __init__(self, mesh):
        self.near = mesh.shape["seq"].bit_length() - 1
        self.count = mesh.shape["dp"] * mesh.shape["seq"]
        bits = self.count.bit_length() - 1
        assert self.count == 1 << bits
        self.core, self.y, self.x, self.xy, self.z = (0, 2), (1, 2), (2, 2), (1, 4), (3, 4)
        self.z_near, self.z_far = (3, 2), (4, 2)
        self.fits = self.near == 2 and bits == 5
        self.bits = [(b, 2) for b in range(bits)]
        self.near_groups = [(b, 2) for b in range(self.near)]

    def place(self, group):
        low, ways = group
        return (lax.axis_index(self.axes).astype(jnp.int32) >> low) & (ways - 1)

    def partner(self, x, group, r):
        low, _ = group
        return lax.ppermute(x, self.axes, [(i, i ^ (r << low)) for i in range(self.count)])

    def total(self, x, groups):
        for group in groups:
            terms = [x] + [self.partner(x, group, r) for r in range(1, group[1])]
            while len(terms) > 1:
                terms = [p + q for p, q in zip(terms[::2], terms[1::2], strict=True)]
            x = terms[0]
        return x


class Gather:
    def __init__(self, cube, x, groups):
        self.cube, self.x, self.groups, self.seen = cube, x[None], list(groups), []

    def send(self):
        group = self.groups[0]
        self.got = [self.cube.partner(self.x, group, r) for r in range(1, group[1])]

    def take(self):
        group = self.groups.pop(0)
        inner = 1
        for low, ways in self.seen:
            inner *= ways if low < group[0] else 1
        self.seen.append(group)
        parts = [x.reshape((-1, inner) + x.shape[1:]) for x in [self.x] + list(self.got)]
        x = place_blocks(self.cube.place(group), parts)
        self.x = x.reshape((-1,) + self.x.shape[1:])

    def left(self):
        return len(self.groups)


class Parts:
    def __init__(self, cube, x, groups):
        self.cube, self.parts, self.ids, self.groups = cube, [x], [0], list(groups)

    def send(self):
        self.got = [self.cube.partner(x, self.groups[0], 1) for x in self.parts]

    def take(self):
        low, _ = self.groups.pop(0)
        self.parts = self.parts + list(self.got)
        self.ids = self.ids + [i | 1 << low for i in self.ids]

    def left(self):
        return len(self.groups)


class Sum:
    def __init__(self, cube, keeps, sends, groups):
        self.cube, self.groups = cube, list(groups)
        self.keeps, self.sends = list(keeps), [list(sends)]

    def send(self):
        group = self.groups[0]
        self.got = [[self.cube.partner(x, group, r + 1) for x in xs] for r, xs in enumerate(self.sends)]

    def take(self):
        self.groups.pop(0)
        terms = [[keep] + [got[i] for got in self.got] for i, keep in enumerate(self.keeps)]
        if self.groups:
            low, ways = self.groups[0]
            inner = 1
            for other, count in self.groups[1:]:
                inner *= count if other < low else 1
            keep, *sends = fold(self.cube.place((low, ways)), ways, inner, terms, False)
            self.keeps, self.sends = [keep], [[x] for x in sends]
        else:
            (self.x,) = fold(jnp.zeros((), jnp.int32), 1, 1, terms, True)

    def left(self):
        return len(self.groups)


def after(first, then):
    return lax.optimization_barrier((first, then))[1]


def land(moves, values):
    held = lax.optimization_barrier(([m.got for m in moves], tuple(values)))
    for m, got in zip(moves, held[0], strict=True):
        m.got = got
    return held[1]


def arrive(moves, values=()):
    values = land(moves, values)
    for m in moves:
        m.take()
    return values


def per_device(
    mesh,
    dec_in,
    memory,
    cotangent,
    dec_lengths,
    mem_mask,
    bucket_map,
    self_weights,
    cross_weights,
    ffn_in,
    ffn_out,
    norm_gains,
    bias_table,
):
    cube = Cube(mesh)
    near_sums, near_gathers = cube.near_groups, cube.near_groups[::-1]
    slots, rows, width = dec_in.shape
    tokens = slots * rows
    buckets = bias_table.shape[0]
    hidden = ffn_in.shape[2]
    unit = self_weights.shape[1]
    exchange = unit == UNIT and cube.fits
    bit = lax.axis_index("seq").astype(jnp.int32) & 1

    assert memory.shape[1] <= 256
    count = jnp.sum(mem_mask, axis=1).astype(BF)
    memory = jnp.concatenate([memory, jnp.broadcast_to(count[:, None, None], (slots, TAIL, width))], axis=1)
    x_move = Parts(cube, dec_in, near_gathers)
    m_move = Parts(cube, memory, near_gathers)
    x_move.send()
    if exchange:
        w_move = Gather(cube, self_weights, [cube.z, cube.xy])
        c_move = Gather(cube, cross_weights, [cube.y, cube.z, cube.x])
        w_move.send()
        c_move.send()
        w_move.take()
        w_move.send()
        x_move.got, c_move.got, ffn_in, ffn_out = after(w_move.x, (x_move.got, c_move.got, ffn_in, ffn_out))
        x_move.take()
        x_move.send()
        (c_move.got,) = arrive([x_move], (c_move.got,))
        c_move.take()
        c_move.send()
        packed = jnp.concatenate([to_tiles(ffn_in), to_tiles(ffn_out[None])])
        gathered = lax.all_gather(packed, ("dp", "seq"), axis=0, tiled=False)
        w_move.got = after(x_move.parts, w_move.got)
        w_move.take()
        w_move.x = after(c_move.got, w_move.x)
        w_got = cube.partner(w_move.x, cube.core, 1)
        c_move.got = after(w_move.x, c_move.got)
        c_move.take()
        c_move.send()
        m_move.parts[0] = after(c_move.x, m_move.parts[0])
        m_move.send()
        own1, got1 = after(c_move.x, (w_move.x, w_got))
        ffn_tiles = gathered.reshape(cube.count, 3 * UNIT // 8, hidden // 128, 8, 128)
    else:
        bit = bit * 0
        for move in (x_move, m_move):
            if move is m_move:
                move.send()
            arrive([move])
            while move.left():
                move.send()
                arrive([move])
        own1, got1 = in_halves(lax.all_gather(self_weights, ("dp", "seq"), axis=1, tiled=True))
        own2, got2 = in_halves(lax.all_gather(cross_weights, ("dp", "seq"), axis=1, tiled=True))
        w01 = lax.all_gather(ffn_in, ("dp", "seq"), axis=1, tiled=True)
        w2 = lax.all_gather(ffn_out, ("dp", "seq"), axis=0, tiled=True)
        w01 = w01.reshape(2, -1, UNIT // 8, 8, hidden // 128, 128).transpose(1, 0, 2, 4, 3, 5)
        w01 = w01.reshape(w01.shape[0], -1, hidden // 128, 8, 128)
        w2 = w2.reshape(w01.shape[0], -1, 8, width // 128, 128).transpose(0, 1, 3, 2, 4)
        w2 = w2.reshape(w01.shape[0], -1, hidden // 128, 8, 128)
        ffn_tiles = jnp.concatenate([w01, w2], axis=1)

    positions = bucket_map.shape[0]
    hot = (bucket_map[::-1][None, :] == jnp.arange(buckets, dtype=jnp.int32)[:, None]).astype(F32)
    line = jnp.einsum("bh,bm->hm", bias_table, hot, precision=lax.Precision.HIGHEST)
    line = line.reshape(H * DK // WIDE, WIDE // DK, positions)
    me = lax.axis_index("seq").astype(jnp.int32)
    lims = jnp.concatenate([(me * rows)[None], dec_lengths, me[None], bit[None]])

    near = tuple(x_move.ids)
    outs = self_forward(lims, near, x_move.parts, norm_gains, own1, got1, line)
    if exchange:
        outs = arrive([c_move, m_move], outs)
        own2, got2 = c_move.x, cube.partner(c_move.x, cube.core, 1)
        m_move.send()
        arrive([m_move])
    q1, k1, v1, o1, lse1 = outs
    h1, q2, k2, v2, o2, lse2 = cross_forward(
        lims, near, m_move.parts, dec_in, o1, own1, got1, norm_gains, own2, got2
    )
    flat = (tokens, width)
    h1 = h1.reshape(flat)
    o1 = o1.reshape(flat)
    o2 = o2.reshape(flat)
    layer_out, gh2, gain_third, dw = feed_forward(
        lims, h1, o2, own2, got2, norm_gains, cotangent.reshape(flat), ffn_tiles
    )
    if exchange:
        ffn_shard = lax.psum_scatter(dw, ("dp", "seq"), scatter_dimension=0, tiled=True)
    outs = cross_backward(lims, near, m_move.parts, gh2, h1, o1, o2, own2, got2, norm_gains, q2, k2, v2, lse2)
    gh1, gain_second, mkeep, msend, ckeep, csend, skeep, ssend = outs
    mem = Sum(cube, [in_rows(mkeep)], [in_rows(msend)], near_sums)
    mem.send()
    if exchange:
        others = Sum(
            cube,
            [in_rows(ckeep), in_rows(skeep)],
            [in_rows(csend), in_rows(ssend)],
            [cube.core, cube.xy, cube.z_near, cube.z_far],
        )
        others.send()
        (gh1,) = arrive([others], (gh1,))
        gh1 = after(others.sends, gh1)
        others.send()
    else:
        arrive([mem])
        mem.send()
    outs = self_backward(lims, near, x_move.parts, gh1, own1, got1, norm_gains, line, q1, k1, v1, lse1)
    xkeep, xsend, table, keep, send = outs
    if exchange:
        (xsend, send) = land([others, mem], (xsend, send))
    first = Sum(cube, [in_rows(xkeep)], [in_rows(xsend)], near_sums)
    if exchange:
        own = Sum(cube, [in_rows(keep)], [in_rows(send)], [cube.core, cube.xy, cube.z])
        own.send()
        first.send()
        others.take()
        others.send()
        mem.take()
        mem.send()
        own.got = after((others.sends, mem.sends), own.got)
        own.take()
        own.send()
        (first.got, others.got, mem.got) = after(own.sends, (first.got, others.got, mem.got))
        first.take()
        others.take()
        others.send()
        (own.got, first.sends) = after((first.sends, others.sends), (own.got, first.sends))
        (first.sends,) = land([own], (first.sends,))
        own.take()
        own.send()
        first.send()
        (others.got, mem.got) = after(own.sends, (others.got, mem.got))
        others.take()
        mem.take()
        own.take()
        first.take()
        tiles = unit // 8
        pieces = others.x[0]
        *cross_shard, out1 = [pieces[tiles * m : tiles * (m + 1)].reshape(unit, width) for m in range(5)]
        gate_shard, down_shard = ffn_shard[:, : 2 * hidden], down_back(ffn_shard[:, 2 * hidden :], width)
        self_shard = own.x[0].reshape(3, unit, width)
        self_shard = jnp.concatenate([self_shard, out1[None]])
        cross_shard = jnp.stack(cross_shard)
    else:
        first.send()
        arrive([mem, first])
        while first.left():
            first.send()
            arrive([first])
        self_grad = jnp.concatenate([from_halves(keep, send), from_halves(skeep[:, None], ssend[:, None])])
        self_shard = lax.psum_scatter(self_grad, ("dp", "seq"), scatter_dimension=1, tiled=True).astype(F32)
        cross_grad = from_halves(ckeep, csend)
        cross_shard = lax.psum_scatter(cross_grad, ("dp", "seq"), scatter_dimension=1, tiled=True).astype(F32)
        gate_shard = lax.psum_scatter(dw[:, : 2 * hidden], ("dp", "seq"), scatter_dimension=0, tiled=True)
        down_grad = down_back(dw[:, 2 * hidden :], width)
        down_shard = lax.psum_scatter(down_grad, ("dp", "seq"), scatter_dimension=0, tiled=True)
    while mem.left():
        mem.send()
        arrive([mem])
    mem_grad = mem.x.reshape(slots, -1, width)
    down_shard = down_shard.astype(F32)
    gate_shard = gate_shard.astype(F32).reshape(-1, ffn_in.shape[2] // TILE, 2, TILE)
    gate_shard = gate_shard.transpose(2, 0, 1, 3).reshape(ffn_in.shape)
    dv, gain_first = normed_back(dec_in.astype(F32).reshape(flat), norm_gains[0:1], first.x.reshape(flat))
    dec_grad = (gh1 + dv).reshape(dec_in.shape)
    table_part = jnp.einsum("hm,bm->bh", table.reshape(H, positions), hot, precision=lax.Precision.HIGHEST)

    self_square = self_shard * self_shard
    cross_square = cross_shard * cross_shard
    gate_square = gate_shard * gate_shard
    down_square = down_shard * down_shard
    hidden = ffn_in.shape[2]
    def summed(terms):
        packed = jnp.concatenate([t.reshape(-1, 128) for t in terms])
        packed = cube.total(packed, [cube.core, cube.xy, cube.z] if exchange else cube.bits)
        sums = []
        at = 0
        for t in terms:
            count = t.size // 128
            sums.append(packed[at : at + count].reshape(t.shape))
            at += count
        return sums

    gain_first, gain_second, gain_third, table_grad, self_cols, cross_cols, gate_cols, down_cols = summed(
        [
            gain_first,
            gain_second,
            gain_third,
            table_part,
            jnp.sum(self_square, axis=1) / width,
            jnp.sum(cross_square, axis=1) / width,
            jnp.sum(gate_square, axis=1) / width,
            jnp.sum(down_square, axis=0) / hidden,
        ]
    )
    gains_grad = jnp.concatenate([gain_first, gain_second, gain_third])
    self_row_means = jnp.mean(self_square, axis=2)
    cross_row_means = jnp.mean(cross_square, axis=2)
    shard_rows = self_shard.shape[1]
    column_start = lax.axis_index(("dp", "seq")) * shard_rows
    self_col_piece = lax.dynamic_slice_in_dim(self_cols[3], column_start, shard_rows, 0)
    cross_col_piece = lax.dynamic_slice_in_dim(cross_cols[3], column_start, shard_rows, 0)
    out_proj_stats = jnp.stack(
        [
            jnp.stack([self_row_means[3], self_col_piece]),
            jnp.stack([cross_row_means[3], cross_col_piece]),
        ]
    )
    return (
        layer_out.reshape(dec_in.shape),
        dec_grad,
        mem_grad,
        self_shard,
        cross_shard,
        gate_shard,
        down_shard,
        gains_grad,
        table_grad,
        self_row_means[:3],
        self_cols[:3],
        cross_row_means[:3],
        cross_cols[:3],
        jnp.mean(gate_square, axis=2),
        gate_cols,
        jnp.mean(down_square, axis=1),
        down_cols,
        out_proj_stats,
    )


def solution(mesh):
    in_specs = (
        P("dp", "seq", None),
        P("dp", "seq", None),
        P("dp", "seq", None),
        P("dp"),
        P("dp", "seq"),
        P(),
        P(None, ("dp", "seq"), None),
        P(None, ("dp", "seq"), None),
        P(None, ("dp", "seq"), None),
        P(("dp", "seq"), None),
        P(),
        P(),
    )
    out_specs = (
        P("dp", "seq", None),
        P("dp", "seq", None),
        P("dp", "seq", None),
        P(None, ("dp", "seq"), None),
        P(None, ("dp", "seq"), None),
        P(None, ("dp", "seq"), None),
        P(("dp", "seq"), None),
        P(),
        P(),
        P(None, ("dp", "seq")),
        P(),
        P(None, ("dp", "seq")),
        P(),
        P(None, ("dp", "seq")),
        P(),
        P(("dp", "seq")),
        P(),
        P(None, None, ("dp", "seq")),
    )
    return jax.shard_map(
        functools.partial(per_device, mesh),
        mesh=mesh,
        in_specs=in_specs,
        out_specs=out_specs,
        check_vma=False,
    )
```

```python
import functools

import jax
import jax.numpy as jnp
from jax import lax
from jax.experimental import pallas as pl
from jax.experimental.pallas import tpu as pltpu
from jax.sharding import PartitionSpec as P

H = 12
DK = 64
PAIR = 2 * DK
WIDE = 4 * DK
TILE = 512
UNIT = 24
TAIL = 8
EPS = 1e-06
MASKED = -1000000000.0
BF = jnp.bfloat16
F32 = jnp.float32
BUDGET = 60 * 1024 * 1024
MIDDLE = 20 * 1024 * 1024
SMALL = 4 * 1024 * 1024
COST = pl.CostEstimate(flops=1000, bytes_accessed=1000, transcendentals=0)


def dot_nn(a, b):
    return lax.dot_general(a, b, (((1,), (0,)), ((), ())), preferred_element_type=F32)


def dot_nt(a, b):
    return lax.dot_general(a, b, (((1,), (1,)), ((), ())), preferred_element_type=F32)


def dot_tn(a, b):
    return lax.dot_general(a, b, (((0,), (0,)), ((), ())), preferred_element_type=F32)


def inverse_rms(v):
    return lax.rsqrt(jnp.mean(v * v, axis=-1, keepdims=True) + EPS)


def normed(v, gain):
    return (v * inverse_rms(v) * gain).astype(BF)


def normed_back(v, gain, c):
    r = inverse_rms(v)
    scaled = c * gain
    inner = jnp.mean(v * scaled, axis=-1, keepdims=True)
    dv = r * scaled - v * (r * r * r * inner)
    dgain = jnp.sum(c * v * r, axis=0, keepdims=True)
    return dv, dgain


def shear(rows, sign):
    keys = rows.shape[1]
    r = lax.broadcasted_iota(jnp.int32, (8, 1), 0)
    for bit in (1, 2, 4):
        turned = pltpu.roll(rows, bit if sign > 0 else keys - bit, 1)
        rows = jnp.where((r & bit) != 0, turned, rows)
    return rows


def build_bias(line, off, out_ref):
    count, keys = out_ref.shape
    base = shear(pltpu.roll(jnp.broadcast_to(line, (8, keys)), off + 1, 1), 1)
    for g in range(count // 8):
        out_ref[8 * g : 8 * g + 8, :] = pltpu.roll(base, (8 * g) % keys, 1) if g else base


def sum_diagonals(sum_ref, off):
    count, keys = sum_ref.shape
    total = sum_ref[0:8, :]
    for g in range(1, count // 8):
        total = total + pltpu.roll(sum_ref[8 * g : 8 * g + 8, :], (keys - 8 * g) % keys, 1)
    total = jnp.sum(shear(total, -1), axis=0, keepdims=True)
    return pltpu.roll(jnp.broadcast_to(total, (8, keys)), keys - 1 - off, 1)[0:1]


def low_lanes():
    return lax.broadcasted_iota(jnp.int32, (1, PAIR), 1) < DK


def head_part(x, head):
    low = low_lanes()
    mine = low if head % 2 == 0 else jnp.logical_not(low)
    return jnp.where(mine, x, jnp.zeros_like(x))


def row_limit(start, rows, count, causal):
    if not causal:
        return count
    seen = start + 1 + lax.broadcasted_iota(jnp.int32, (rows, 1), 0)
    return jnp.minimum(seen, count)


def attend(q_ref, k_ref, v_ref, o_ref, lse_ref, bias_ref, s_ref, p_ref, off, counts):
    slots, rows, _ = q_ref.shape
    keys = k_ref.shape[1]
    causal = bias_ref is not None
    cols = lax.broadcasted_iota(jnp.int32, (1, keys), 1)
    low = low_lanes()
    work = [(s, h) for s in range(slots) for h in range(WIDE // DK)]

    def lanes(h):
        return slice((h // 2) * PAIR, (h // 2) * PAIR + PAIR)

    def scores(n):
        s, h = work[n]
        s_ref[n % 2] = dot_nt(head_part(q_ref[s, :, lanes(h)], h), k_ref[s, :, lanes(h)])

    scores(0)
    kept = None
    for n, (s, h) in enumerate(work):
        if n + 1 < len(work):
            scores(n + 1)
        sc = s_ref[n % 2]
        if causal:
            sc = sc + bias_ref[h]
        sc = jnp.where(cols < row_limit(off, rows, counts[s], causal), sc, MASKED)
        top = jnp.max(sc, axis=1, keepdims=True)
        e = jnp.exp(sc - top)
        total = jnp.sum(e, axis=1, keepdims=True)
        p_ref[n % 2] = (e * (1.0 / total)).astype(BF)
        out = dot_nn(p_ref[n % 2], v_ref[s, :, lanes(h)])
        log_total = jnp.broadcast_to(top + jnp.log(total), (rows, PAIR))
        if h % 2 == 0:
            kept = (out, log_total)
        else:
            o_ref[s, :, lanes(h)] = jnp.where(low, kept[0], out).astype(BF)
            lse_ref[s, h // 2] = jnp.where(low, kept[1], log_total)


def attend_back(
    q_ref, k_ref, v_ref, g_ref, lse_ref, dq_ref, dk_ref, dv_ref,
    bias_ref, sum_ref, s_ref, dp_ref, p_ref, ds_ref, off, counts,
):
    slots, rows, _ = q_ref.shape
    keys = k_ref.shape[1]
    causal = bias_ref is not None
    cols = lax.broadcasted_iota(jnp.int32, (1, keys), 1)
    low = low_lanes()
    work = [(s, h) for s in range(slots) for h in range(WIDE // DK)]

    def lanes(h):
        return slice((h // 2) * PAIR, (h // 2) * PAIR + PAIR)

    def products(n):
        s, h = work[n]
        s_ref[n % 2] = dot_nt(head_part(q_ref[s, :, lanes(h)], h), k_ref[s, :, lanes(h)])
        dp_ref[n % 2] = dot_nt(head_part(g_ref[s, :, lanes(h)], h), v_ref[s, :, lanes(h)])

    products(0)
    kept = None
    for n, (s, h) in enumerate(work):
        if n + 1 < len(work):
            products(n + 1)
        sc = s_ref[n % 2]
        if causal:
            sc = sc + bias_ref[h]
        sc = jnp.where(cols < row_limit(off, rows, counts[s], causal), sc, MASKED)
        at = (h % 2) * DK
        p = jnp.exp(sc - lse_ref[s, h // 2, :, at : at + 1])
        dp = dp_ref[n % 2]
        inner = jnp.sum(p * dp, axis=1, keepdims=True)
        ds = (p * (dp - inner)).astype(BF)
        p_ref[n % 2] = p.astype(BF)
        ds_ref[n % 2] = ds
        if causal:
            if s == 0:
                sum_ref[h] = ds.astype(F32)
            else:
                sum_ref[h] += ds.astype(F32)
        ds = ds_ref[n % 2]
        dq = dot_nn(ds, k_ref[s, :, lanes(h)])
        dk = dot_tn(head_part(q_ref[s, :, lanes(h)], h), ds)
        dv = dot_tn(head_part(g_ref[s, :, lanes(h)], h), p_ref[n % 2])
        if h % 2 == 0:
            kept = (dq, dk, dv)
        else:
            dq_ref[s * rows : (s + 1) * rows, lanes(h)] = jnp.where(low, kept[0], dq).astype(BF)
            dk_ref[s * keys : (s + 1) * keys, lanes(h)] = (kept[1] + dk).astype(BF).T
            dv_ref[s * keys : (s + 1) * keys, lanes(h)] = (kept[2] + dv).astype(BF).T


def assemble(own_ref, got_ref, bit):
    own, got = own_ref[...].astype(F32), got_ref[...].astype(F32)
    both = jnp.stack([jnp.where(bit == 0, own, got), jnp.where(bit == 0, got, own)], axis=1)
    return both.reshape(-1, both.shape[-1]).astype(BF)


def row_counts(ms):
    counts = []
    for s in range(ms[0].shape[0]):
        count = sum(m_ref[s, -TAIL:, 0:PAIR].astype(F32)[0:1, 0:1] for m_ref in ms)
        counts.append(count.astype(jnp.int32))
    return counts


def part_blocks(x, pairs, bit, keep_ref, send_ref):
    x = x.reshape(pairs, 2, -1, x.shape[-1])
    first, second = x[:, 0], x[:, 1]
    keep_ref[...] = jnp.where(bit == 0, first, second).astype(BF)
    send_ref[...] = jnp.where(bit == 0, second, first).astype(BF)


def whole(shape):
    return pl.BlockSpec(shape, lambda b, *_: (0,) * len(shape), pipeline_mode=pl.Buffered(1))


def result(shape):
    return pl.BlockSpec(shape, lambda b, *_: (0,) * len(shape))


def wide(shape):
    return pl.BlockSpec(shape[:-1] + (WIDE,), lambda b, *_: (0,) * (len(shape) - 1) + (b,))


def halves(index, shape, lanes=WIDE):
    pairs, _, rows, width = shape
    if lanes == width:
        spec = pl.BlockSpec(
            (pairs, None, rows, width), lambda b, *_: (0, index, 0, 0), pipeline_mode=pl.Buffered(1)
        )
    else:
        spec = pl.BlockSpec((pairs, None, rows, lanes), lambda b, *_: (0, index, 0, b))
    return [spec, spec]


def params(budget=BUDGET):
    return pltpu.CompilerParams(dimension_semantics=("arbitrary",), vmem_limit_bytes=budget)


def self_forward_body(near, lims, *refs):
    xs = refs[: len(near)]
    (
        gain_ref, wq_own, wq_got, wk_own, wk_got, wv_own, wv_got, line_ref,
        q_ref, k_ref, v_ref, o_ref, lse_ref, a_ref, bias_ref, s_ref, p_ref,
    ) = refs[len(near) :]
    slots, rows, width = xs[0].shape
    keys = k_ref.shape[1]
    off, me, bit = lims[0], lims[1 + slots], lims[2 + slots]

    @pl.when(pl.program_id(0) == 0)
    def _():
        for r, x_ref in zip(near, xs, strict=True):
            for s in range(slots):
                at = pl.multiple_of(s * keys + (me ^ r) * rows, 128)
                a_ref[pl.ds(at, rows), :] = normed(x_ref[s].astype(F32), gain_ref[0:1, :])

    wq, wk, wv = assemble(wq_own, wq_got, bit), assemble(wk_own, wk_got, bit), assemble(wv_own, wv_got, bit)
    for s in range(slots):
        mine = pl.ds(pl.multiple_of(s * keys + off, 128), rows)
        q_ref[s] = dot_nn(a_ref[mine, :], wq).astype(BF)
        k_ref[s] = dot_nn(a_ref[s * keys : (s + 1) * keys, :], wk).astype(BF)
        v_ref[s] = dot_nn(a_ref[s * keys : (s + 1) * keys, :], wv).astype(BF)
    for h in range(WIDE // DK):
        build_bias(line_ref[0, h : h + 1, :], off, bias_ref.at[h])
    counts = [lims[1 + s] for s in range(slots)]
    attend(q_ref, k_ref, v_ref, o_ref, lse_ref, bias_ref, s_ref, p_ref, off, counts)


def self_forward(lims, near, xs, gains, own, got, line):
    slots, rows, width = xs[0].shape
    keys = rows * len(near)
    blocks = width // WIDE
    return pl.pallas_call(
        functools.partial(self_forward_body, near),
        grid_spec=pltpu.PrefetchScalarGridSpec(
            num_scalar_prefetch=1,
            grid=(blocks,),
            in_specs=[whole((slots, rows, width))] * len(near)
            + [whole(gains.shape)]
            + halves(0, own.shape)
            + halves(1, own.shape)
            + halves(2, own.shape)
            + [pl.BlockSpec((1, WIDE // DK, keys), lambda b, *_: (b, 0, 0))],
            out_specs=[
                wide((slots, rows, width)),
                wide((slots, keys, width)),
                wide((slots, keys, width)),
                wide((slots, rows, width)),
                pl.BlockSpec((slots, 2, rows, PAIR), lambda b, *_: (0, b, 0, 0)),
            ],
            scratch_shapes=[
                pltpu.VMEM((slots * keys, width), BF),
                pltpu.VMEM((WIDE // DK, rows, keys), F32),
                pltpu.VMEM((2, rows, keys), F32),
                pltpu.VMEM((2, rows, keys), BF),
            ],
        ),
        out_shape=[
            jax.ShapeDtypeStruct((slots, rows, width), BF),
            jax.ShapeDtypeStruct((slots, keys, width), BF),
            jax.ShapeDtypeStruct((slots, keys, width), BF),
            jax.ShapeDtypeStruct((slots, rows, width), BF),
            jax.ShapeDtypeStruct((slots, H // 2, rows, PAIR), F32),
        ],
        compiler_params=params(),
        cost_estimate=COST,
        name="self_forward",
    )(lims, *xs, gains, own, got, own, got, own, got, line)


def cross_forward_body(near, lims, *refs):
    ms = refs[: len(near)]
    (
        x_ref, o1_ref, wo_own, wo_got, gain_ref, wq_own, wq_got, wk_own, wk_got, wv_own, wv_got,
        h_ref, q_ref, k_ref, v_ref, o_ref, lse_ref, a_ref, mem_ref, s_ref, p_ref,
    ) = refs[len(near) :]
    slots, part, width = ms[0].shape
    part -= TAIL
    rows, keys = q_ref.shape[1], k_ref.shape[1]
    me, bit = lims[1 + slots], lims[2 + slots]

    @pl.when(pl.program_id(0) == 0)
    def _():
        wo = assemble(wo_own, wo_got, bit)
        for s in range(slots):
            h = x_ref[s].astype(F32) + dot_nn(o1_ref[s], wo)
            h_ref[s] = h
            a_ref[s * rows : (s + 1) * rows, :] = normed(h, gain_ref[1:2, :])
        for r, m_ref in zip(near, ms, strict=True):
            for s in range(slots):
                mem_ref[s, pl.ds(pl.multiple_of((me ^ r) * part, part), part), :] = m_ref[s, :part]

    wq, wk, wv = assemble(wq_own, wq_got, bit), assemble(wk_own, wk_got, bit), assemble(wv_own, wv_got, bit)
    for s in range(slots):
        q_ref[s] = dot_nn(a_ref[s * rows : (s + 1) * rows, :], wq).astype(BF)
        k_ref[s] = dot_nn(mem_ref[s], wk).astype(BF)
        v_ref[s] = dot_nn(mem_ref[s], wv).astype(BF)
    counts = row_counts(ms)
    attend(q_ref, k_ref, v_ref, o_ref, lse_ref, None, s_ref, p_ref, 0, counts)


def cross_forward(lims, near, ms, x, o1, own1, got1, gains, own, got):
    slots, part, width = ms[0].shape
    part -= TAIL
    keys = part * len(near)
    rows = x.shape[1]
    blocks = width // WIDE
    return pl.pallas_call(
        functools.partial(cross_forward_body, near),
        grid_spec=pltpu.PrefetchScalarGridSpec(
            num_scalar_prefetch=1,
            grid=(blocks,),
            in_specs=[whole((slots, part + TAIL, width))] * len(near)
            + [whole((slots, rows, width)), whole((slots, rows, width))]
            + halves(3, own1.shape, width)
            + [whole(gains.shape)]
            + halves(0, own.shape)
            + halves(1, own.shape)
            + halves(2, own.shape),
            out_specs=[
                result((slots, rows, width)),
                wide((slots, rows, width)),
                wide((slots, keys, width)),
                wide((slots, keys, width)),
                wide((slots, rows, width)),
                pl.BlockSpec((slots, 2, rows, PAIR), lambda b, *_: (0, b, 0, 0)),
            ],
            scratch_shapes=[
                pltpu.VMEM((slots * rows, width), BF),
                pltpu.VMEM((slots, keys, width), BF),
                pltpu.VMEM((2, rows, keys), F32),
                pltpu.VMEM((2, rows, keys), BF),
            ],
        ),
        out_shape=[
            jax.ShapeDtypeStruct((slots, rows, width), F32),
            jax.ShapeDtypeStruct((slots, rows, width), BF),
            jax.ShapeDtypeStruct((slots, keys, width), BF),
            jax.ShapeDtypeStruct((slots, keys, width), BF),
            jax.ShapeDtypeStruct((slots, rows, width), BF),
            jax.ShapeDtypeStruct((slots, H // 2, rows, PAIR), F32),
        ],
        compiler_params=params(),
        cost_estimate=COST,
        name="cross_forward",
    )(lims, *ms, x, o1, own1, got1, gains, own, got, own, got, own, got)


def down_rows(x):
    width = x.shape[-1]
    lanes = width // 128
    x = x.reshape(-1, 8, 8, width)
    count = 8 * lanes
    across = count // (UNIT // 8)
    tiles = [x[:, q // lanes, :, (q % lanes) * 128 : (q % lanes + 1) * 128] for q in range(count)]
    rows = [jnp.concatenate(tiles[i * across : (i + 1) * across], axis=-1) for i in range(UNIT // 8)]
    x = jnp.stack(rows, axis=1)
    return x.reshape(-1, across * 128)


def down_back(x, width):
    lanes = width // 128
    x = x.reshape(-1, UNIT // 8, 8, x.shape[-1] // 128, 128).transpose(0, 1, 3, 2, 4)
    x = x.reshape(-1, 8, lanes, 8, 128).transpose(0, 1, 3, 2, 4)
    return x.reshape(-1, width)


def gradient_copies(wide_ref, down_ref, dw_ref, sems):
    steps, _, columns = wide_ref.shape
    rows, hidden = down_ref.shape[1:]
    tile = columns // 2
    moves = []
    for n in range(steps):
        pairs = [
            (wide_ref.at[n, :, pl.ds(0, tile)], dw_ref.at[:, pl.ds(n * tile, tile)]),
            (wide_ref.at[n, :, pl.ds(tile, tile)], dw_ref.at[:, pl.ds(hidden + n * tile, tile)]),
            (down_ref.at[n], dw_ref.at[pl.ds(n * rows, rows), pl.ds(2 * hidden, hidden)]),
        ]
        moves.append([pltpu.make_async_copy(x, y, sems.at[3 * n + i]) for i, (x, y) in enumerate(pairs)])
    return moves


def from_columns(ref):
    columns = []
    for n in range(ref.shape[2]):
        columns.append(ref[:, :, n].astype(F32).reshape(-1, 128))
    return jnp.concatenate(columns, axis=-1).astype(BF)


def from_rows(ref, width):
    lanes = width // 128
    across = ref.shape[2]
    count = ref.shape[1] * across
    tiles = [ref[:, q // across, q % across].astype(F32) for q in range(count)]
    rows = [jnp.concatenate(tiles[n * lanes : (n + 1) * lanes], axis=-1) for n in range(count // lanes)]
    return jnp.stack(rows, axis=1).reshape(-1, width).astype(BF)


def feed_forward_body(
    lims, h1_ref, o2_ref, wo_own, wo_got, gain_ref, g_ref, w0_tiles, w1_tiles, wd_tiles,
    out_ref, gh_ref, dgain_ref, dw_ref, h_ref, a_ref, at_ref, acc_ref, da_ref, wide_ref, down_ref, sems,
):
    step = pl.program_id(0)
    bit = lims[lims.shape[0] - 1]

    @pl.when(step == 0)
    def _():
        h = h1_ref[...] + dot_nn(o2_ref[...], assemble(wo_own, wo_got, bit))
        h_ref[...] = h
        a = normed(h, gain_ref[2:3, :])
        a_ref[...] = a
        at_ref[...] = a.T
        acc_ref[...] = h
        da_ref[...] = jnp.zeros_like(da_ref)

    a = a_ref[...]
    e = g_ref[...]
    w0, w1, wd = from_columns(w0_tiles), from_columns(w1_tiles), from_rows(wd_tiles, a.shape[1])
    gate = dot_nn(a, w0)
    up = dot_nn(a, w1)
    c = dot_nt(e, wd)
    root = 0.7978845608028654
    square = gate * gate
    th = jnp.tanh(root * gate * (1.0 + 0.044715 * square))
    half = 0.5 * (1.0 + th)
    act = gate * half
    slope = half + 0.5 * gate * (1.0 - th * th) * (root * (1.0 + 3.0 * 0.044715 * square))
    hidden = (act * up).astype(BF)
    dgate = (c * up * slope).astype(BF)
    dup = (c * act).astype(BF)
    acc_ref[...] += dot_nn(hidden, wd)
    tile = dgate.shape[1]
    wide_ref[step, :, :tile] = dot_nn(at_ref[...], dgate).astype(BF)
    wide_ref[step, :, tile:] = dot_nn(at_ref[...], dup).astype(BF)
    down_ref[step] = down_rows(dot_tn(hidden, e)).astype(BF)
    moves = gradient_copies(wide_ref, down_ref, dw_ref, sems)
    for n, pair in enumerate(moves):

        @pl.when(step == n)
        def _():
            for move in pair:
                move.start()

    da_ref[...] += dot_nt(dgate, w0) + dot_nt(dup, w1)

    @pl.when(step == pl.num_programs(0) - 1)
    def _():
        out_ref[...] = acc_ref[...].astype(BF)
        dv, dgain = normed_back(h_ref[...], gain_ref[2:3, :], da_ref[...])
        gh_ref[...] = e.astype(F32) + dv
        dgain_ref[...] = dgain
        for pair in moves:
            for move in pair:
                move.wait()


def feed_forward(lims, h1, o2, own, got, gains, cot, tiles):
    tokens, width = h1.shape
    devices, parts, across, _, _ = tiles.shape
    hidden = across * 128
    tile = TILE
    steps = hidden // tile
    assert hidden // 64 == width // UNIT == devices
    return pl.pallas_call(
        feed_forward_body,
        grid_spec=pltpu.PrefetchScalarGridSpec(
            num_scalar_prefetch=1,
            grid=(hidden // tile,),
            in_specs=[whole((tokens, width)), whole((tokens, width))]
            + halves(3, own.shape, width)
            + [
                whole(gains.shape),
                whole((tokens, width)),
                pl.BlockSpec((devices, parts // 3, tile // 128, 8, 128), lambda b, *_: (0, 0, b, 0, 0)),
                pl.BlockSpec((devices, parts // 3, tile // 128, 8, 128), lambda b, *_: (0, 1, b, 0, 0)),
                pl.BlockSpec((devices // steps, parts // 3, across, 8, 128), lambda b, *_: (b, 2, 0, 0, 0)),
            ],
            out_specs=[
                result((tokens, width)),
                result((tokens, width)),
                result((1, width)),
                pl.BlockSpec(memory_space=pl.ANY),
            ],
            scratch_shapes=[
                pltpu.VMEM((tokens, width), F32),
                pltpu.VMEM((tokens, width), BF),
                pltpu.VMEM((width, tokens), BF),
                pltpu.VMEM((tokens, width), F32),
                pltpu.VMEM((tokens, width), F32),
                pltpu.VMEM((steps, width, 2 * tile), BF),
                pltpu.VMEM((steps, width // steps, hidden), BF),
                pltpu.SemaphoreType.DMA((3 * steps,)),
            ],
        ),
        out_shape=[
            jax.ShapeDtypeStruct((tokens, width), BF),
            jax.ShapeDtypeStruct((tokens, width), F32),
            jax.ShapeDtypeStruct((1, width), F32),
            jax.ShapeDtypeStruct((width, 3 * hidden), BF),
        ],
        compiler_params=params(),
        cost_estimate=COST,
        name="feed_forward",
    )(lims, h1, o2, own, got, gains, cot, tiles, tiles, tiles)


def cross_backward_body(near, lims, *refs):
    ms = refs[: len(near)]
    (
        gh2_ref, h1_ref, o1_ref, o2_ref, wo_own, wo_got, gain_ref, q_ref, k_ref, v_ref, lse_ref,
        wq_own, wq_got, wk_own, wk_got, wv_own, wv_got,
        gh_ref, dgain_ref, mkeep_ref, msend_ref, keep_ref, send_ref, skeep_ref, ssend_ref,
        g_ref, e_ref, at_ref, memt_ref, da_ref, dm_ref, dq_ref, dk_ref, dv_ref, s_ref, dp_ref, p_ref, ds_ref,
    ) = refs[len(near) :]
    step = pl.program_id(0)
    slots, part, width = ms[0].shape
    part -= TAIL
    rows, keys = q_ref.shape[1], k_ref.shape[1]
    me, bit = lims[1 + slots], lims[2 + slots]
    pairs = keep_ref.shape[0]

    @pl.when(step == 0)
    def _():
        e = gh2_ref[...].astype(BF)
        back = dot_nt(e, assemble(wo_own, wo_got, bit)).astype(BF)
        for b in range(width // WIDE):
            e_ref[b] = e[:, b * WIDE : (b + 1) * WIDE]
            for s in range(slots):
                g_ref[b, s] = back[s * rows : (s + 1) * rows, b * WIDE : (b + 1) * WIDE]
        at_ref[...] = normed(h1_ref[...], gain_ref[1:2, :]).T
        for r, m_ref in zip(near, ms, strict=True):
            for s in range(slots):
                at = pl.multiple_of(s * keys + (me ^ r) * part, part)
                memt_ref[pl.ds(at, part), :] = m_ref[s, :part]
        da_ref[...] = jnp.zeros_like(da_ref)
        dm_ref[...] = jnp.zeros_like(dm_ref)

    counts = row_counts(ms)
    attend_back(
        q_ref, k_ref, v_ref, g_ref.at[step], lse_ref, dq_ref, dk_ref, dv_ref,
        None, None, s_ref, dp_ref, p_ref, ds_ref, 0, counts,
    )
    for m, grad in enumerate(
        (
            dot_nn(at_ref[...], dq_ref[...]),
            dot_tn(memt_ref[...], dk_ref[...]),
            dot_tn(memt_ref[...], dv_ref[...]),
            dot_tn(o2_ref[...], e_ref[step]),
        )
    ):
        part_blocks(grad, pairs, bit, keep_ref.at[:, m], send_ref.at[:, m])
    da_ref[...] += dot_nt(dq_ref[...], assemble(wq_own, wq_got, bit))
    dm_ref[...] += dot_nt(dk_ref[...], assemble(wk_own, wk_got, bit)) + dot_nt(
        dv_ref[...], assemble(wv_own, wv_got, bit)
    )

    @pl.when(step == pl.num_programs(0) - 1)
    def _():
        dv, dgain = normed_back(h1_ref[...], gain_ref[1:2, :], da_ref[...])
        gh = gh2_ref[...] + dv
        gh_ref[...] = gh
        dgain_ref[...] = dgain
        part_blocks(dot_tn(o1_ref[...], gh.astype(BF)), pairs, bit, skeep_ref, ssend_ref)
        for s in range(slots):
            for n in range(len(near) // 2):
                keep = pl.multiple_of(s * keys + (2 * n + bit) * part, part)
                send = pl.multiple_of(s * keys + (2 * n + 1 - bit) * part, part)
                mkeep_ref[s * (len(near) // 2) + n] = dm_ref[pl.ds(keep, part), :].astype(BF)
                msend_ref[s * (len(near) // 2) + n] = dm_ref[pl.ds(send, part), :].astype(BF)


def cross_backward(lims, near, ms, gh2, h1, o1, o2, own, got, gains, q, k, v, lse):
    slots, part, width = ms[0].shape
    part -= TAIL
    keys = part * len(near)
    rows = q.shape[1]
    tokens = slots * rows
    blocks = width // WIDE
    pairs, count, unit, _ = own.shape
    half = jax.ShapeDtypeStruct((slots * len(near) // 2, part, width), BF)
    grads = pl.BlockSpec((pairs, count, unit, WIDE), lambda b, *_: (0, 0, 0, b))
    return pl.pallas_call(
        functools.partial(cross_backward_body, near),
        grid_spec=pltpu.PrefetchScalarGridSpec(
            num_scalar_prefetch=1,
            grid=(blocks,),
            in_specs=[whole((slots, part + TAIL, width))] * len(near)
            + [whole((tokens, width))] * 4
            + halves(3, own.shape, width)
            + [
                whole(gains.shape),
                wide((slots, rows, width)),
                wide((slots, keys, width)),
                wide((slots, keys, width)),
                pl.BlockSpec((slots, 2, rows, PAIR), lambda b, *_: (0, b, 0, 0)),
            ]
            + halves(0, own.shape)
            + halves(1, own.shape)
            + halves(2, own.shape),
            out_specs=[
                result((tokens, width)),
                result((1, width)),
                result(half.shape),
                result(half.shape),
                grads,
                grads,
                result((pairs, unit, width)),
                result((pairs, unit, width)),
            ],
            scratch_shapes=[
                pltpu.VMEM((blocks, slots, rows, WIDE), BF),
                pltpu.VMEM((blocks, tokens, WIDE), BF),
                pltpu.VMEM((width, tokens), BF),
                pltpu.VMEM((slots * keys, width), BF),
                pltpu.VMEM((tokens, width), F32),
                pltpu.VMEM((slots * keys, width), F32),
                pltpu.VMEM((tokens, WIDE), BF),
                pltpu.VMEM((slots * keys, WIDE), BF),
                pltpu.VMEM((slots * keys, WIDE), BF),
                pltpu.VMEM((2, rows, keys), F32),
                pltpu.VMEM((2, rows, keys), F32),
                pltpu.VMEM((2, rows, keys), BF),
                pltpu.VMEM((2, rows, keys), BF),
            ],
        ),
        out_shape=[
            jax.ShapeDtypeStruct((tokens, width), F32),
            jax.ShapeDtypeStruct((1, width), F32),
            half,
            half,
            jax.ShapeDtypeStruct(own.shape, BF),
            jax.ShapeDtypeStruct(own.shape, BF),
            jax.ShapeDtypeStruct((pairs, unit, width), BF),
            jax.ShapeDtypeStruct((pairs, unit, width), BF),
        ],
        compiler_params=params(),
        cost_estimate=COST,
        name="cross_backward",
    )(lims, *ms, gh2, h1, o1, o2, own, got, gains, q, k, v, lse, own, got, own, got, own, got)


def self_backward_body(near, lims, *refs):
    xs = refs[: len(near)]
    (
        gh1_ref, wo_own, wo_got, gain_ref, line_ref, q_ref, k_ref, v_ref, lse_ref,
        wq_own, wq_got, wk_own, wk_got, wv_own, wv_got,
        xkeep_ref, xsend_ref, table_ref, keep_ref, send_ref,
        g_ref, at_ref, da_ref, dq_ref, dk_ref, dv_ref, bias_ref, sum_ref, s_ref, dp_ref, p_ref, ds_ref,
    ) = refs[len(near) :]
    step = pl.program_id(0)
    slots, rows, width = xs[0].shape
    keys = k_ref.shape[1]
    off, me, bit = lims[0], lims[1 + slots], lims[2 + slots]
    pairs = keep_ref.shape[0]

    @pl.when(step == 0)
    def _():
        e = gh1_ref[...].astype(BF)
        back = dot_nt(e, assemble(wo_own, wo_got, bit)).astype(BF)
        for b in range(width // WIDE):
            for s in range(slots):
                g_ref[b, s] = back[s * rows : (s + 1) * rows, b * WIDE : (b + 1) * WIDE]
        for r, x_ref in zip(near, xs, strict=True):
            for s in range(slots):
                at = pl.multiple_of(s * keys + (me ^ r) * rows, 128)
                at_ref[:, pl.ds(at, rows)] = normed(x_ref[s].astype(F32), gain_ref[0:1, :]).T
        da_ref[...] = jnp.zeros_like(da_ref)

    for h in range(WIDE // DK):
        build_bias(line_ref[0, h : h + 1, :], off, bias_ref.at[h])
    counts = [lims[1 + s] for s in range(slots)]
    attend_back(
        q_ref, k_ref, v_ref, g_ref.at[step], lse_ref, dq_ref, dk_ref, dv_ref,
        bias_ref, sum_ref, s_ref, dp_ref, p_ref, ds_ref, off, counts,
    )
    for h in range(WIDE // DK):
        table_ref[0, h : h + 1, :] = sum_diagonals(sum_ref.at[h], off)
    wq = assemble(wq_own, wq_got, bit)
    dwq = None
    for s in range(slots):
        mine = pl.ds(pl.multiple_of(s * keys + off, 128), rows)
        dq = dq_ref[s * rows : (s + 1) * rows, :]
        part = dot_nn(at_ref[:, mine], dq)
        dwq = part if dwq is None else dwq + part
        da_ref[mine, :] += dot_nt(dq, wq)
    for m, grad in enumerate((dwq, dot_nn(at_ref[...], dk_ref[...]), dot_nn(at_ref[...], dv_ref[...]))):
        part_blocks(grad, pairs, bit, keep_ref.at[:, m], send_ref.at[:, m])
    da_ref[...] += dot_nt(dk_ref[...], assemble(wk_own, wk_got, bit)) + dot_nt(
        dv_ref[...], assemble(wv_own, wv_got, bit)
    )

    @pl.when(step == pl.num_programs(0) - 1)
    def _():
        for s in range(slots):
            for n in range(len(near) // 2):
                keep = pl.multiple_of(s * keys + (2 * n + bit) * rows, 128)
                send = pl.multiple_of(s * keys + (2 * n + 1 - bit) * rows, 128)
                xkeep_ref[s * (len(near) // 2) + n] = da_ref[pl.ds(keep, rows), :].astype(BF)
                xsend_ref[s * (len(near) // 2) + n] = da_ref[pl.ds(send, rows), :].astype(BF)


def self_backward(lims, near, xs, gh1, own, got, gains, line, q, k, v, lse):
    slots, rows, width = xs[0].shape
    keys = rows * len(near)
    tokens = slots * rows
    blocks = width // WIDE
    pairs, count, unit, _ = own.shape
    heads = WIDE // DK
    half = jax.ShapeDtypeStruct((slots * len(near) // 2, rows, width), BF)
    grads = pl.BlockSpec((pairs, count - 1, unit, WIDE), lambda b, *_: (0, 0, 0, b))
    return pl.pallas_call(
        functools.partial(self_backward_body, near),
        grid_spec=pltpu.PrefetchScalarGridSpec(
            num_scalar_prefetch=1,
            grid=(blocks,),
            in_specs=[whole((slots, rows, width))] * len(near)
            + [whole((tokens, width))]
            + halves(3, own.shape, width)
            + [
                whole(gains.shape),
                pl.BlockSpec((1, heads, keys), lambda b, *_: (b, 0, 0)),
                wide((slots, rows, width)),
                wide((slots, keys, width)),
                wide((slots, keys, width)),
                pl.BlockSpec((slots, 2, rows, PAIR), lambda b, *_: (0, b, 0, 0)),
            ]
            + halves(0, own.shape)
            + halves(1, own.shape)
            + halves(2, own.shape),
            out_specs=[
                result(half.shape),
                result(half.shape),
                pl.BlockSpec((1, heads, keys), lambda b, *_: (b, 0, 0)),
                grads,
                grads,
            ],
            scratch_shapes=[
                pltpu.VMEM((blocks, slots, rows, WIDE), BF),
                pltpu.VMEM((width, slots * keys), BF),
                pltpu.VMEM((slots * keys, width), F32),
                pltpu.VMEM((tokens, WIDE), BF),
                pltpu.VMEM((slots * keys, WIDE), BF),
                pltpu.VMEM((slots * keys, WIDE), BF),
                pltpu.VMEM((heads, rows, keys), F32),
                pltpu.VMEM((heads, rows, keys), F32),
                pltpu.VMEM((2, rows, keys), F32),
                pltpu.VMEM((2, rows, keys), F32),
                pltpu.VMEM((2, rows, keys), BF),
                pltpu.VMEM((2, rows, keys), BF),
            ],
        ),
        out_shape=[
            half,
            half,
            jax.ShapeDtypeStruct((blocks, heads, keys), F32),
            jax.ShapeDtypeStruct((pairs, count - 1, unit, width), BF),
            jax.ShapeDtypeStruct((pairs, count - 1, unit, width), BF),
        ],
        compiler_params=params(),
        cost_estimate=COST,
        name="self_backward",
    )(lims, *xs, gh1, own, got, gains, line, q, k, v, lse, own, got, own, got, own, got)


TABLE_ROWS = 16


def unpack_body(*refs):
    terms, outs = refs[:-7], refs[-7:]
    x = [ref[...] for ref in terms]
    while len(x) > 1:
        x = [p + q for p, q in zip(x[::2], x[1::2], strict=True)]
    x = x[0]
    gains, table, self_cols, cross_cols, gate, down, proj = outs

    def rows(out, first, count, at):
        lanes = out.shape[1] // 128
        for i in range(count):
            for n in range(lanes):
                row = at + i * lanes + n
                out[first + i : first + i + 1, n * 128 : (n + 1) * 128] = x[row : row + 1]
        return at + count * lanes

    at = rows(gains, 0, 3, 0)
    table[...] = x[at : at + table.shape[0], : table.shape[1]]
    at += TABLE_ROWS
    at = rows(self_cols, 0, 3, at)
    at = rows(proj, 0, 1, at)
    at = rows(cross_cols, 0, 3, at)
    at = rows(proj, 1, 1, at)
    at = rows(gate, 0, 2, at)
    rows(down, 0, 1, at)


def unpack(terms, width, hidden, buckets):
    shapes = [(3, width), (H, buckets), (3, width), (3, width), (2, hidden), (1, width), (2, width)]
    return pl.pallas_call(
        unpack_body,
        out_shape=[jax.ShapeDtypeStruct(shape, F32) for shape in shapes],
        compiler_params=pltpu.CompilerParams(vmem_limit_bytes=SMALL),
        cost_estimate=COST,
        name="unpack_statistics",
    )(*terms)


def to_tiles(w):
    m, r, c = w.shape
    return w.reshape(m, r // 8, 8, c // 128, 128).transpose(0, 1, 3, 2, 4).reshape(-1, 8, 128)


def place_body(ways, scalar_ref, *refs):
    for r in range(ways):

        @pl.when(pl.program_id(0) == r)
        def _():
            refs[ways][...] = refs[r][...]


def place_blocks(place, parts):
    ways = len(parts)
    outer, inner, tail = parts[0].shape[0], parts[0].shape[1], parts[0].shape[2:]
    rest = (0,) * len(tail)
    spec = pl.BlockSpec((outer, inner) + tail, lambda r, s: (0, 0) + rest)
    return pl.pallas_call(
        functools.partial(place_body, ways),
        grid_spec=pltpu.PrefetchScalarGridSpec(
            num_scalar_prefetch=1,
            grid=(ways,),
            in_specs=[spec] * ways,
            out_specs=pl.BlockSpec((outer, None, inner) + tail, lambda r, s: (0, s[0] ^ r, 0) + rest),
        ),
        out_shape=jax.ShapeDtypeStruct((outer, ways, inner) + tail, BF),
        compiler_params=params(MIDDLE),
        cost_estimate=COST,
        name="place_blocks",
    )(place.reshape(1), *parts)


def fold_body(groups, ways, last, *refs):
    refs = refs[1:]
    inputs = ways * sum(1 + terms for _, terms in groups)
    outs = refs[inputs:]
    n = 0
    for j in range(ways):
        at = 0
        for size, terms in groups:
            x = refs[n][...].astype(F32)
            for t in range(terms):
                x = x + refs[n + 1 + t][...].astype(F32)
            n += 1 + terms
            outs[j][:, :, at : at + size] = x if last else x.astype(BF)
            at += size


def fold(place, ways, inner, groups, last):
    outer, width = groups[0][0].shape[0] // (ways * inner), groups[0][0].shape[-1]
    sizes = [g[0].shape[1] for g in groups]
    total = sum(sizes)
    step = outer
    moved = sum(size * (len(g) + 1) for size, g in zip(sizes, groups, strict=True))
    while step > 1 and step * inner * ways * moved * 8 * width * 2 > 6 * 1024 * 1024:
        step //= 2

    def spec(j, size):
        return pl.BlockSpec((step, None, inner, size, 8, width), lambda g, s: (g, s[0] ^ j, 0, 0, 0, 0))

    in_specs, ins = [], []
    for j in range(ways):
        for size, terms in zip(sizes, groups, strict=True):
            in_specs += [spec(j, size)] * len(terms)
            ins += [t.reshape((outer, ways, inner) + t.shape[1:]) for t in terms]
    made = pl.pallas_call(
        functools.partial(fold_body, [(size, len(g) - 1) for size, g in zip(sizes, groups, strict=True)], ways, last),
        grid_spec=pltpu.PrefetchScalarGridSpec(
            num_scalar_prefetch=1,
            grid=(outer // step,),
            in_specs=in_specs,
            out_specs=[pl.BlockSpec((step, inner, total, 8, width), lambda g, s: (g, 0, 0, 0, 0))] * ways,
        ),
        out_shape=[jax.ShapeDtypeStruct((outer, inner, total, 8, width), F32 if last else BF)] * ways,
        compiler_params=params(MIDDLE),
        cost_estimate=COST,
        name="fold_blocks",
    )(place.reshape(1), *ins)
    return [x.reshape((outer * inner,) + x.shape[2:]) for x in made]


def in_halves(w):
    x = w.reshape(w.shape[0], -1, 2, UNIT, w.shape[-1]).transpose(2, 1, 0, 3, 4)
    return x[0], x[1]


def from_halves(first, second):
    x = jnp.stack([first, second], axis=1)
    return x.transpose(2, 0, 1, 3, 4).reshape(x.shape[2], -1, x.shape[-1])


def in_rows(x):
    return x.reshape(x.shape[0], -1, 8, x.shape[-1])


class Cube:
    axes = ("dp", "seq")

    def __init__(self, mesh):
        self.near = mesh.shape["seq"].bit_length() - 1
        self.count = mesh.shape["dp"] * mesh.shape["seq"]
        bits = self.count.bit_length() - 1
        assert self.count == 1 << bits
        self.core, self.y, self.x, self.xy, self.z = (0, 2), (1, 2), (2, 2), (1, 4), (3, 4)
        self.z_near, self.z_far = (3, 2), (4, 2)
        self.fits = self.near == 2 and bits == 5
        self.bits = [(b, 2) for b in range(bits)]
        self.near_groups = [(b, 2) for b in range(self.near)]

    def place(self, group):
        low, ways = group
        return (lax.axis_index(self.axes).astype(jnp.int32) >> low) & (ways - 1)

    def partner(self, x, group, r):
        low, _ = group
        return lax.ppermute(x, self.axes, [(i, i ^ (r << low)) for i in range(self.count)])

    def total(self, x, groups):
        terms = [x]
        for group in groups:
            while len(terms) > 1:
                terms = [p + q for p, q in zip(terms[::2], terms[1::2], strict=True)]
            x = terms[0]
            terms = [x] + [self.partner(x, group, r) for r in range(1, group[1])]
        return terms


class Gather:
    def __init__(self, cube, x, groups):
        self.cube, self.x, self.groups, self.seen = cube, x[None], list(groups), []

    def send(self):
        group = self.groups[0]
        self.got = [self.cube.partner(self.x, group, r) for r in range(1, group[1])]

    def take(self):
        group = self.groups.pop(0)
        inner = 1
        for low, ways in self.seen:
            inner *= ways if low < group[0] else 1
        self.seen.append(group)
        parts = [x.reshape((-1, inner) + x.shape[1:]) for x in [self.x] + list(self.got)]
        x = place_blocks(self.cube.place(group), parts)
        self.x = x.reshape((-1,) + self.x.shape[1:])

    def left(self):
        return len(self.groups)


class Parts:
    def __init__(self, cube, x, groups):
        self.cube, self.parts, self.ids, self.groups = cube, [x], [0], list(groups)

    def send(self):
        self.got = [self.cube.partner(x, self.groups[0], 1) for x in self.parts]

    def take(self):
        low, _ = self.groups.pop(0)
        self.parts = self.parts + list(self.got)
        self.ids = self.ids + [i | 1 << low for i in self.ids]

    def left(self):
        return len(self.groups)


class Sum:
    def __init__(self, cube, keeps, sends, groups):
        self.cube, self.groups = cube, list(groups)
        self.keeps, self.sends = list(keeps), [list(sends)]

    def send(self):
        group = self.groups[0]
        self.got = [[self.cube.partner(x, group, r + 1) for x in xs] for r, xs in enumerate(self.sends)]

    def take(self):
        self.groups.pop(0)
        terms = [[keep] + [got[i] for got in self.got] for i, keep in enumerate(self.keeps)]
        if self.groups:
            low, ways = self.groups[0]
            inner = 1
            for other, count in self.groups[1:]:
                inner *= count if other < low else 1
            keep, *sends = fold(self.cube.place((low, ways)), ways, inner, terms, False)
            self.keeps, self.sends = [keep], [[x] for x in sends]
        else:
            (self.x,) = fold(jnp.zeros((), jnp.int32), 1, 1, terms, True)

    def left(self):
        return len(self.groups)


def after(first, then):
    return lax.optimization_barrier((first, then))[1]


def land(moves, values):
    held = lax.optimization_barrier(([m.got for m in moves], tuple(values)))
    for m, got in zip(moves, held[0], strict=True):
        m.got = got
    return held[1]


def arrive(moves, values=()):
    values = land(moves, values)
    for m in moves:
        m.take()
    return values


def per_device(
    mesh,
    dec_in,
    memory,
    cotangent,
    dec_lengths,
    mem_mask,
    bucket_map,
    self_weights,
    cross_weights,
    ffn_in,
    ffn_out,
    norm_gains,
    bias_table,
):
    cube = Cube(mesh)
    near_sums, near_gathers = cube.near_groups, cube.near_groups[::-1]
    slots, rows, width = dec_in.shape
    tokens = slots * rows
    buckets = bias_table.shape[0]
    hidden = ffn_in.shape[2]
    unit = self_weights.shape[1]
    exchange = unit == UNIT and cube.fits
    bit = lax.axis_index("seq").astype(jnp.int32) & 1

    assert memory.shape[1] <= 256
    count = jnp.sum(mem_mask, axis=1).astype(BF)
    memory = jnp.concatenate([memory, jnp.broadcast_to(count[:, None, None], (slots, TAIL, width))], axis=1)
    x_move = Parts(cube, dec_in, near_gathers)
    m_move = Parts(cube, memory, near_gathers)
    x_move.send()
    if exchange:
        w_move = Gather(cube, self_weights, [cube.z, cube.xy])
        c_move = Gather(cube, cross_weights, [cube.y, cube.z, cube.x])
        w_move.send()
        c_move.send()
        packed = jnp.concatenate([to_tiles(ffn_in), to_tiles(ffn_out[None])])
        w_move.got = after(packed, w_move.got)
        w_move.take()
        w_move.send()
        x_move.got, c_move.got, packed = after(w_move.x, (x_move.got, c_move.got, packed))
        x_move.take()
        x_move.send()
        (c_move.got,) = arrive([x_move], (c_move.got,))
        c_move.take()
        c_move.send()
        gathered = lax.all_gather(packed, ("dp", "seq"), axis=0, tiled=False)
        w_move.got = after(x_move.parts, w_move.got)
        w_move.take()
        w_move.x = after(c_move.got, w_move.x)
        w_got = cube.partner(w_move.x, cube.core, 1)
        c_move.got = after(w_move.x, c_move.got)
        c_move.take()
        c_move.send()
        m_move.parts[0] = after(c_move.x, m_move.parts[0])
        m_move.send()
        own1, got1 = after(c_move.x, (w_move.x, w_got))
        ffn_tiles = gathered.reshape(cube.count, 3 * UNIT // 8, hidden // 128, 8, 128)
    else:
        bit = bit * 0
        for move in (x_move, m_move):
            if move is m_move:
                move.send()
            arrive([move])
            while move.left():
                move.send()
                arrive([move])
        own1, got1 = in_halves(lax.all_gather(self_weights, ("dp", "seq"), axis=1, tiled=True))
        own2, got2 = in_halves(lax.all_gather(cross_weights, ("dp", "seq"), axis=1, tiled=True))
        w01 = lax.all_gather(ffn_in, ("dp", "seq"), axis=1, tiled=True)
        w2 = lax.all_gather(ffn_out, ("dp", "seq"), axis=0, tiled=True)
        w01 = w01.reshape(2, -1, UNIT // 8, 8, hidden // 128, 128).transpose(1, 0, 2, 4, 3, 5)
        w01 = w01.reshape(w01.shape[0], -1, hidden // 128, 8, 128)
        w2 = w2.reshape(w01.shape[0], -1, 8, width // 128, 128).transpose(0, 1, 3, 2, 4)
        w2 = w2.reshape(w01.shape[0], -1, hidden // 128, 8, 128)
        ffn_tiles = jnp.concatenate([w01, w2], axis=1)

    positions = bucket_map.shape[0]
    hot = (bucket_map[::-1][None, :] == jnp.arange(buckets, dtype=jnp.int32)[:, None]).astype(F32)
    line = jnp.einsum("bh,bm->hm", bias_table, hot, precision=lax.Precision.HIGHEST)
    line = line.reshape(H * DK // WIDE, WIDE // DK, positions)
    me = lax.axis_index("seq").astype(jnp.int32)
    lims = jnp.concatenate([(me * rows)[None], dec_lengths, me[None], bit[None]])

    near = tuple(x_move.ids)
    outs = self_forward(lims, near, x_move.parts, norm_gains, own1, got1, line)
    if exchange:
        outs = arrive([c_move, m_move], outs)
        own2, got2 = c_move.x, cube.partner(c_move.x, cube.core, 1)
        m_move.send()
        arrive([m_move])
    q1, k1, v1, o1, lse1 = outs
    h1, q2, k2, v2, o2, lse2 = cross_forward(
        lims, near, m_move.parts, dec_in, o1, own1, got1, norm_gains, own2, got2
    )
    flat = (tokens, width)
    h1 = h1.reshape(flat)
    o1 = o1.reshape(flat)
    o2 = o2.reshape(flat)
    layer_out, gh2, gain_third, dw = feed_forward(
        lims, h1, o2, own2, got2, norm_gains, cotangent.reshape(flat), ffn_tiles
    )
    if exchange:
        ffn_shard = lax.psum_scatter(dw, ("dp", "seq"), scatter_dimension=0, tiled=True)
    outs = cross_backward(lims, near, m_move.parts, gh2, h1, o1, o2, own2, got2, norm_gains, q2, k2, v2, lse2)
    gh1, gain_second, mkeep, msend, ckeep, csend, skeep, ssend = outs
    mem = Sum(cube, [in_rows(mkeep)], [in_rows(msend)], near_sums)
    mem.send()
    if exchange:
        others = Sum(
            cube,
            [in_rows(ckeep), in_rows(skeep)],
            [in_rows(csend), in_rows(ssend)],
            [cube.core, cube.xy, cube.z_near, cube.z_far],
        )
        others.send()
        (gh1,) = arrive([others], (gh1,))
        gh1 = after(others.sends, gh1)
        others.send()
    else:
        arrive([mem])
        mem.send()
    outs = self_backward(lims, near, x_move.parts, gh1, own1, got1, norm_gains, line, q1, k1, v1, lse1)
    xkeep, xsend, table, keep, send = outs
    if exchange:
        (xsend, send) = land([others, mem], (xsend, send))
    first = Sum(cube, [in_rows(xkeep)], [in_rows(xsend)], near_sums)
    if exchange:
        own = Sum(cube, [in_rows(keep)], [in_rows(send)], [cube.core, cube.xy, cube.z])
        own.send()
        first.send()
        others.take()
        others.send()
        mem.take()
        mem.send()
        own.got = after((others.sends, mem.sends), own.got)
        own.take()
        own.send()
        (first.got, others.got, mem.got) = after(own.sends, (first.got, others.got, mem.got))
        first.take()
        others.take()
        others.send()
        (own.got, first.sends) = after((first.sends, others.sends), (own.got, first.sends))
        (first.sends,) = land([own], (first.sends,))
        own.take()
        own.send()
        first.send()
        (others.got, mem.got) = after(own.sends, (others.got, mem.got))
        others.take()
        mem.take()
        own.take()
        first.take()
        tiles = unit // 8
        pieces = others.x[0]
        *cross_shard, out1 = [pieces[tiles * m : tiles * (m + 1)].reshape(unit, width) for m in range(5)]
        gate_shard, down_shard = ffn_shard[:, : 2 * hidden], down_back(ffn_shard[:, 2 * hidden :], width)
        self_shard = own.x[0].reshape(3, unit, width)
        self_shard = jnp.concatenate([self_shard, out1[None]])
        cross_shard = jnp.stack(cross_shard)
    else:
        first.send()
        arrive([mem, first])
        while first.left():
            first.send()
            arrive([first])
        self_grad = jnp.concatenate([from_halves(keep, send), from_halves(skeep[:, None], ssend[:, None])])
        self_shard = lax.psum_scatter(self_grad, ("dp", "seq"), scatter_dimension=1, tiled=True).astype(F32)
        cross_grad = from_halves(ckeep, csend)
        cross_shard = lax.psum_scatter(cross_grad, ("dp", "seq"), scatter_dimension=1, tiled=True).astype(F32)
        gate_shard = lax.psum_scatter(dw[:, : 2 * hidden], ("dp", "seq"), scatter_dimension=0, tiled=True)
        down_grad = down_back(dw[:, 2 * hidden :], width)
        down_shard = lax.psum_scatter(down_grad, ("dp", "seq"), scatter_dimension=0, tiled=True)
    while mem.left():
        mem.send()
        arrive([mem])
    mem_grad = mem.x.reshape(slots, -1, width)
    down_shard = down_shard.astype(F32)
    gate_shard = jnp.stack([gate_shard[:, :hidden], gate_shard[:, hidden:]]).astype(F32)
    dv_terms, gain_first = normed_back(dec_in.astype(F32).reshape(flat), norm_gains[0:1], first.x.reshape(flat))
    table_part = jnp.einsum("hm,bm->hb", table.reshape(H, positions), hot, precision=lax.Precision.HIGHEST)

    self_square = self_shard * self_shard
    cross_square = cross_shard * cross_shard
    gate_square = gate_shard * gate_shard
    down_square = down_shard * down_shard
    hidden = ffn_in.shape[2]
    table_part = jnp.pad(table_part, ((0, TABLE_ROWS - H), (0, 128 - buckets)))
    terms = [
        gain_first,
        gain_second,
        gain_third,
        table_part,
        jnp.sum(self_square, axis=1) / width,
        jnp.sum(cross_square, axis=1) / width,
        jnp.sum(gate_square, axis=1) / width,
        jnp.sum(down_square, axis=0) / hidden,
    ]
    packed = jnp.concatenate([t.reshape(-1, 128) for t in terms])
    dec_grad = (gh1 + dv_terms).reshape(dec_in.shape)
    packed = after(dec_grad, packed)
    parts = cube.total(packed, [cube.core, cube.xy, cube.z] if exchange else cube.bits)
    gains_grad, table_grad, self_cols, cross_cols, gate_cols, down_cols, proj_cols = unpack(
        parts, width, hidden, buckets
    )
    self_row_means = jnp.mean(self_square, axis=2)
    cross_row_means = jnp.mean(cross_square, axis=2)
    shard_rows = self_shard.shape[1]
    column_start = lax.axis_index(("dp", "seq")) * shard_rows
    column_pieces = lax.dynamic_slice_in_dim(proj_cols, column_start, shard_rows, 1)
    row_pieces = jnp.stack([self_row_means[3], cross_row_means[3]])
    out_proj_stats = jnp.stack([row_pieces, column_pieces], axis=1)
    return (
        layer_out.reshape(dec_in.shape),
        dec_grad,
        mem_grad,
        self_shard,
        cross_shard,
        gate_shard,
        down_shard,
        gains_grad,
        table_grad.T,
        self_row_means[:3],
        self_cols,
        cross_row_means[:3],
        cross_cols,
        jnp.mean(gate_square, axis=2),
        gate_cols,
        jnp.mean(down_square, axis=1),
        down_cols.reshape(-1),
        out_proj_stats,
    )


def solution(mesh):
    in_specs = (
        P("dp", "seq", None),
        P("dp", "seq", None),
        P("dp", "seq", None),
        P("dp"),
        P("dp", "seq"),
        P(),
        P(None, ("dp", "seq"), None),
        P(None, ("dp", "seq"), None),
        P(None, ("dp", "seq"), None),
        P(("dp", "seq"), None),
        P(),
        P(),
    )
    out_specs = (
        P("dp", "seq", None),
        P("dp", "seq", None),
        P("dp", "seq", None),
        P(None, ("dp", "seq"), None),
        P(None, ("dp", "seq"), None),
        P(None, ("dp", "seq"), None),
        P(("dp", "seq"), None),
        P(),
        P(),
        P(None, ("dp", "seq")),
        P(),
        P(None, ("dp", "seq")),
        P(),
        P(None, ("dp", "seq")),
        P(),
        P(("dp", "seq")),
        P(),
        P(None, None, ("dp", "seq")),
    )
    return jax.shard_map(
        functools.partial(per_device, mesh),
        mesh=mesh,
        in_specs=in_specs,
        out_specs=out_specs,
        check_vma=False,
    )
```
